32 devices in a mesh: dp: 8 (over z, x), expert: 4 (over y, core).
Axes of the slice: x: 2, y: 2, z: 4, core: 2. Of those that a mesh axis runs over, the one named last changes fastest.
Arguments:
- tokens: bfloat16 [8192, 768], P(('dp', 'expert')), may hold values from -6 to 6
- conditioning: bfloat16 [8, 4, 768], P('dp'), may hold values from -6 to 6
- routes: int32 [8192, 2], P(('dp', 'expert')), may hold values from 0 to 3, as said below
- gate_weights: float32 [8192, 2], P(('dp', 'expert')), may hold values from 0.25 to 0.75
- image_counts: int32 [8], P('dp'), may hold values from 1 to 4
- image_lengths: int32 [8, 4], P('dp'), may hold values from 0 to 1024, as said below
- cotangent: bfloat16 [8192, 768], P(('dp', 'expert')), may hold values from -6 to 6
- qkv_weight: bfloat16 [768, 2304], P('dp'), may hold values from -0.21875 to 0.21875
- qv_bias: bfloat16 [1536], P('dp'), may hold values from -1.5 to 1.5
- proj_weight: bfloat16 [768, 768], P('dp'), may hold values from -1.75 to 1.75
- proj_bias: bfloat16 [768], P('dp'), may hold values from -1.5 to 1.5
- ada_weight: bfloat16 [768, 4608], P('dp'), may hold values from -0.21875 to 0.21875
- ada_bias: bfloat16 [4608], P('dp'), may hold values from -1.5 to 1.5
- up_weight: bfloat16 [768, 3072], P('dp'), may hold values from -0.21875 to 0.21875
- up_bias: bfloat16 [3072], P('dp'), may hold values from -1.5 to 1.5
- down_weight: bfloat16 [3072, 768], P('dp'), may hold values from -0.109375 to 0.109375
- down_bias: bfloat16 [768], P('dp'), may hold values from -1.5 to 1.5
- routed_up: bfloat16 [4, 768, 3072], P('expert', 'dp'), may hold values from -0.21875 to 0.21875
- routed_upbias: bfloat16 [4, 3072], P('expert', 'dp'), may hold values from -1.5 to 1.5
- routed_down: bfloat16 [4, 3072, 768], P('expert', 'dp'), may hold values from -0.109375 to 0.109375
- routed_downbias: bfloat16 [4, 768], P('expert', 'dp'), may hold values from -1.5 to 1.5
Outputs:
- output: bfloat16 [8192, 768], P(('dp', 'expert'))
- tokens_grad: float32 [8192, 768], P(('dp', 'expert'))
- conditioning_grad: float32 [8, 4, 768], P('dp')
- qkv_grad: float32 [768, 2304], P('dp')
- qvbias_grad: float32 [1536], P('dp')
- proj_grad: float32 [768, 768], P('dp')
- projbias_grad: float32 [768], P('dp')
- ada_grad: float32 [768, 4608], P('dp')
- adabias_grad: float32 [4608], P('dp')
- up_grad: float32 [768, 3072], P('dp')
- upbias_grad: float32 [3072], P('dp')
- down_grad: float32 [3072, 768], P('dp')
- downbias_grad: float32 [768], P('dp')
- routedup_grad: float32 [4, 768, 3072], P('expert', 'dp')
- routedupbias_grad: float32 [4, 3072], P('expert', 'dp')
- routeddown_grad: float32 [4, 3072, 768], P('expert', 'dp')
- routeddownbias_grad: float32 [4, 768], P('expert', 'dp')
- expert_counts: int32 [4], replicated
The draws below stay inside these ranges and needn't reach their ends.
Inputs may be any that keep to these rules, and one draw needn't show every extreme that they name: `routes`: each row names two different experts. `image_lengths`: in each row the first image_counts entries are 256 or 1024 and add up to 1024; the other entries are 0.
All inputs are finite; a program needn't handle non-finite values.
Results may differ from the reference program's by a relative error of at most 0.014.
The reference program's roundings to bfloat16 on the way count: a program that leaves them out, or rounds other values in their place, can miss the bound.
Values may be sent and summed in bfloat16 or wider, within the bound.
No kernel may reach another device: no remote copies, remote signals or barrier semaphores. Data moves between devices by JAX's collectives and lax.ppermute only.
A program may use at most 256 MiB of HBM per device.

```python
import jax
import jax.numpy as jnp
from jax import lax

D = 768
HEADS = 12
HEAD_DIM = 64
FF = 3072
TOK_DEV = 256
SHORT = 256
LONG = 1024
EXPERTS = 4
GROUP = 1024
SLOTS = 4
CAP = 128
TOKENS = 8192
N_DP = 8
N_EXPERT = 4


def image_plan(key):
    picked = jax.random.fold_in(key, 4242)
    longs_most = GROUP // LONG
    drawn_long = jax.random.randint(picked, (N_DP,), 0, longs_most + 1, dtype=jnp.int32)
    group_index = jnp.arange(N_DP, dtype=jnp.int32)
    long_count = jnp.where(group_index == 0, longs_most, jnp.where(group_index == 1, 0, drawn_long)).astype(jnp.int32)
    short_count = (GROUP - long_count * LONG) // SHORT
    counts = long_count + short_count
    slot_ids = jnp.arange(SLOTS, dtype=jnp.int32)
    lengths = jnp.where(slot_ids[None, :] < long_count[:, None], LONG, jnp.where(slot_ids[None, :] < counts[:, None], SHORT, 0))
    return (counts.astype(jnp.int32), lengths.astype(jnp.int32))


def draw_image_counts(key, part):
    return image_plan(key)[0]


def draw_image_lengths(key, part):
    return image_plan(key)[1]


def draw_routes(key, part):
    first_key = jax.random.fold_in(key, 7101)
    second_key = jax.random.fold_in(key, 7102)
    third_key = jax.random.fold_in(key, 7103)
    fourth_key = jax.random.fold_in(key, 7104)
    fifth_key = jax.random.fold_in(key, 7105)
    blocks = TOKENS // TOK_DEV
    block_index = jnp.arange(TOKENS, dtype=jnp.int32) // TOK_DEV
    threshold = 800 - 800 * block_index // max(blocks - 1, 1)
    avoid = jax.random.randint(first_key, (TOKENS,), 0, 1000, dtype=jnp.int32) < threshold
    drawn_first = jax.random.randint(second_key, (TOKENS,), 0, EXPERTS, dtype=jnp.int32)
    drawn_step = jax.random.randint(third_key, (TOKENS,), 1, EXPERTS, dtype=jnp.int32)
    drawn_second = (drawn_first + drawn_step) % EXPERTS
    other_first = jax.random.randint(fourth_key, (TOKENS,), 0, EXPERTS - 1, dtype=jnp.int32)
    other_step = jax.random.randint(fifth_key, (TOKENS,), 1, EXPERTS - 1, dtype=jnp.int32)
    other_second = (other_first + other_step) % (EXPERTS - 1)
    first = jnp.where(avoid, other_first + 1, drawn_first)
    second = jnp.where(avoid, other_second + 1, drawn_second)
    return jnp.stack([first, second], axis=1).astype(jnp.int32)


def block_scale(key, shape, cuts, low, top_value):
    gain = 1.0
    for axis_at, blocks in cuts:
        steps = jax.random.uniform(jax.random.fold_in(jax.random.fold_in(key, 6), axis_at), (blocks,), jnp.float32, low / len(cuts), top_value / len(cuts))
        gain = gain * jnp.repeat(jnp.exp(steps), shape[axis_at] // blocks).reshape((-1,) + (1,) * (len(shape) - 1 - axis_at))
    return gain


def centred(rng, dims, spread, most, split=(), held_as=jnp.bfloat16):
    factor_of = block_scale(rng, dims, split, -0.22, 0.18) if split else 1.0
    drawn = jax.random.normal(rng, dims, jnp.float32) * spread * factor_of
    return jnp.minimum(jnp.maximum(drawn, -most), most).astype(held_as)


def setup_inputs(seed: int = 0) -> dict:
    streams_of = jax.random.split(jax.random.key(seed), 22)
    return {
        "tokens": centred(streams_of[0], (TOKENS, D), 1.0, 6.0, ((0, 32),)),
        "conditioning": centred(streams_of[1], (N_DP, SLOTS, D), 1.0, 6.0, ((0, 8),)),
        "routes": draw_routes(jax.random.fold_in(streams_of[21], 71), 0),
        "gate_weights": jnp.clip(0.25 + 0.5 * jax.random.uniform(streams_of[3], (TOKENS, 2), jnp.float32) ** block_scale(streams_of[3], (TOKENS, 2), ((0, 32),), -0.2, 0.2), 0.25, 0.75),
        "image_counts": draw_image_counts(jax.random.fold_in(streams_of[21], 71), 0),
        "image_lengths": draw_image_lengths(jax.random.fold_in(streams_of[21], 71), 0),
        "cotangent": centred(streams_of[6], (TOKENS, D), 1.0, 6.0, ((0, 32),)),
        "qkv_weight": centred(streams_of[7], (D, 3 * D), D ** -0.5, 0.21875, ((0, 8),)),
        "qv_bias": centred(streams_of[8], (2 * D,), 0.3, 1.5, ((0, 8),)),
        "proj_weight": centred(streams_of[9], (D, D), (D // 64) ** -0.5, 1.75, ((0, 8),)),
        "proj_bias": centred(streams_of[10], (D,), 0.3, 1.5, ((0, 8),)),
        "ada_weight": centred(streams_of[11], (D, 6 * D), D ** -0.5, 0.21875, ((0, 8),)),
        "ada_bias": centred(streams_of[12], (6 * D,), 0.3, 1.5, ((0, 8),)),
        "up_weight": centred(streams_of[13], (D, FF), D ** -0.5, 0.21875, ((0, 8),)),
        "up_bias": centred(streams_of[14], (FF,), 0.3, 1.5, ((0, 8),)),
        "down_weight": centred(streams_of[15], (FF, D), FF ** -0.5, 0.109375, ((0, 8),)),
        "down_bias": centred(streams_of[16], (D,), 0.3, 1.5, ((0, 8),)),
        "routed_up": centred(streams_of[17], (EXPERTS, D, FF), D ** -0.5, 0.21875, ((0, 4), (1, 8))),
        "routed_upbias": centred(streams_of[18], (EXPERTS, FF), 0.3, 1.5, ((0, 4), (1, 8))),
        "routed_down": centred(streams_of[19], (EXPERTS, FF, D), FF ** -0.5, 0.109375, ((0, 4), (1, 8))),
        "routed_downbias": centred(streams_of[20], (EXPERTS, D), 0.3, 1.5, ((0, 4), (1, 8))),
    }


@jax.custom_vjp
def low(v):
    return lax.optimization_barrier(v.astype(jnp.bfloat16)).astype(jnp.float32)

@jax.custom_vjp
def lowered_returned(v):
    return v

def low_keep(v):
    return (low(v), None)

def low_pass(kept, grad):
    return (grad,)

def back_keep(v):
    return (v, None)

def back_low(kept, grad):
    return (low(grad),)
low.defvjp(low_keep, low_pass)
lowered_returned.defvjp(back_keep, back_low)
highest_precision = lax.Precision.HIGHEST
epsilon = 1e-06

def layer_norm(values):
    centered = values - lax.optimization_barrier(jnp.mean(values, axis=-1, keepdims=True))
    variance = lax.optimization_barrier(jnp.mean(centered * centered, axis=-1, keepdims=True))
    return centered * lax.rsqrt(variance + epsilon)

def segment_ids(image_total, lengths):
    starts = jnp.cumsum(lengths, dtype=jnp.int32) - lengths
    slot_ids = jnp.arange(SLOTS, dtype=jnp.int32)
    live_slot = (slot_ids >= 1) & (slot_ids < image_total)
    positions = jnp.arange(GROUP, dtype=jnp.int32)
    covered = live_slot[None, :] & (starts[None, :] <= positions[:, None])
    return lax.optimization_barrier(jnp.sum(covered.astype(jnp.int32), axis=1, dtype=jnp.int32))

def group_forward(parameters, group_tokens, group_cond, group_routes, group_gates, image_total, lengths):
    query_key_value_weight, query_value_bias, projection_weight, projection_bias, modulation_weight, modulation_bias, shared_up_weight, shared_up_bias, shared_down_weight, shared_down_bias, expert_up_weight, expert_up_bias, expert_down_weight, expert_down_bias = parameters
    segment = segment_ids(image_total, lengths)
    cond_act = low(jax.nn.silu(group_cond))
    modulation = lowered_returned(jnp.dot(cond_act, modulation_weight, precision=highest_precision) + modulation_bias)
    per_token = modulation[segment]
    shift_a = per_token[:, 0:D]
    scale_a = per_token[:, D:2 * D]
    gate_a = per_token[:, 2 * D:3 * D]
    shift_b = per_token[:, 3 * D:4 * D]
    scale_b = per_token[:, 4 * D:5 * D]
    gate_b = per_token[:, 5 * D:6 * D]
    hidden_a = low(layer_norm(group_tokens) * (1.0 + scale_a) + shift_a)
    bias_three = jnp.concatenate([query_value_bias[:D], jnp.zeros((D,), query_value_bias.dtype), query_value_bias[D:]])
    projected = lowered_returned(low(jnp.dot(hidden_a, query_key_value_weight, precision=highest_precision) + bias_three))
    query = projected[:, 0:D].reshape(GROUP, HEADS, HEAD_DIM)
    keys = projected[:, D:2 * D].reshape(GROUP, HEADS, HEAD_DIM)
    values = projected[:, 2 * D:3 * D].reshape(GROUP, HEADS, HEAD_DIM)
    scores = jnp.einsum('qhd,khd->hqk', query, keys, precision=highest_precision) * HEAD_DIM ** (-0.5)
    scores = lowered_returned(scores)
    same_image = segment[:, None] == segment[None, :]
    masked = jnp.where(same_image[None, :, :], scores, -1e+30)
    probabilities = low(jax.nn.softmax(masked, axis=-1))
    attended = jnp.einsum('hqk,khd->qhd', probabilities, values, precision=highest_precision).reshape(GROUP, D)
    attended = lowered_returned(low(attended))
    attn_out = lowered_returned(jnp.dot(attended, projection_weight, precision=highest_precision) + projection_bias)
    residual_mid = group_tokens + gate_a * attn_out
    hidden_b = low(layer_norm(residual_mid) * (1.0 + scale_b) + shift_b)
    shared_pre = lowered_returned(jnp.dot(hidden_b, shared_up_weight, precision=highest_precision) + shared_up_bias)
    shared_hid = low(jax.nn.gelu(shared_pre, approximate=True))
    shared_out = lowered_returned(jnp.dot(shared_hid, shared_down_weight, precision=highest_precision) + shared_down_bias)
    expert_ids = jnp.arange(EXPERTS, dtype=jnp.int32)
    choose = (group_routes[:, :, None] == expert_ids[None, None, :]).astype(hidden_b.dtype)
    route_hot = lax.optimization_barrier(jnp.sum(choose, axis=1)).reshape(N_EXPERT, TOK_DEV, EXPERTS)
    gate_hot = lax.optimization_barrier(jnp.sum(choose * group_gates[:, :, None], axis=1)).reshape(N_EXPERT, TOK_DEV, EXPERTS)
    slot_rank = jnp.cumsum(route_hot, axis=1) - route_hot
    kept_pairs = route_hot * (slot_rank < CAP).astype(hidden_b.dtype)
    capacity_ids = jnp.arange(CAP, dtype=jnp.int32).astype(hidden_b.dtype)
    slot_table = kept_pairs[:, :, :, None] * (slot_rank[:, :, :, None] == capacity_ids).astype(hidden_b.dtype)
    slot_table = jnp.transpose(slot_table, (0, 2, 3, 1))
    block_hidden = hidden_b.reshape(N_EXPERT, TOK_DEV, D)
    exchange_buffer = lowered_returned(jnp.einsum('bect,btd->becd', slot_table, block_hidden, precision=highest_precision))
    expert_preactivation = lowered_returned(jnp.einsum('jzhn,znq->jzhq', exchange_buffer, expert_up_weight, precision=highest_precision) + expert_up_bias[None, :, None, :])
    expert_hid = low(jax.nn.gelu(expert_preactivation, approximate=True))
    expert_out = jnp.einsum('becf,efd->becd', expert_hid, expert_down_weight, precision=highest_precision) + expert_down_bias[None, :, None, :]
    expert_out = lowered_returned(low(expert_out))
    weighted = slot_table * jnp.transpose(gate_hot, (0, 2, 1))[:, :, None, :]
    routed = jnp.einsum('bect,becd->btd', weighted, expert_out, precision=highest_precision).reshape(GROUP, D)
    return residual_mid + gate_b * (shared_out + routed)

def reference(tokens, conditioning, routes, gate_weights, image_counts, image_lengths, cotangent, qkv_weight, qv_bias, proj_weight, proj_bias, ada_weight, ada_bias, up_weight, up_bias, down_weight, down_bias, routed_up, routed_upbias, routed_down, routed_downbias):
    parameters = tuple((item.astype(jnp.float32) for item in (qkv_weight, qv_bias, proj_weight, proj_bias, ada_weight, ada_bias, up_weight, up_bias, down_weight, down_bias, routed_up, routed_upbias, routed_down, routed_downbias)))
    route_groups = routes.reshape(N_DP, GROUP, 2)
    gate_groups = gate_weights.astype(jnp.float32).reshape(N_DP, GROUP, 2)
    step_group = jax.checkpoint(group_forward)

    def forward_all(weights_in, all_tokens, all_cond):
        token_groups = all_tokens.reshape(N_DP, GROUP, D)

        def scan_step(carry, items):
            return (carry, step_group(weights_in, items[0], items[1], items[2], items[3], items[4], items[5]))
        start_carry = jnp.zeros((), jnp.float32)
        unused, results = lax.scan(scan_step, start_carry, (token_groups, all_cond, route_groups, gate_groups, image_counts, image_lengths))
        return results.reshape(TOKENS, D)
    primal, pullback = jax.vjp(forward_all, parameters, tokens.astype(jnp.float32), conditioning.astype(jnp.float32))
    grad_params, grad_tokens, grad_cond = pullback(cotangent.astype(jnp.float32))
    expert_ids = jnp.arange(EXPERTS, dtype=jnp.int32)
    hot_pairs = lax.optimization_barrier(jnp.sum((routes[:, :, None] == expert_ids[None, None, :]).astype(jnp.int32), axis=1, dtype=jnp.int32))
    hot_pairs = hot_pairs.reshape(N_DP * N_EXPERT, TOK_DEV, EXPERTS)
    rank_int = jnp.cumsum(hot_pairs, axis=1, dtype=jnp.int32) - hot_pairs
    kept_int = hot_pairs * (rank_int < CAP).astype(jnp.int32)
    counts = lax.optimization_barrier(jnp.sum(kept_int, axis=(0, 1), dtype=jnp.int32))
    return (primal.astype(jnp.bfloat16), grad_tokens, grad_cond, grad_params[0], grad_params[1], grad_params[2], grad_params[3], grad_params[4], grad_params[5], grad_params[6], grad_params[7], grad_params[8], grad_params[9], grad_params[10], grad_params[11], grad_params[12], grad_params[13], counts)
```

```python
import jax
import jax.numpy as jnp
from jax import lax
from jax.sharding import PartitionSpec as P

HEADS = 12
HEAD_DIM = 64
CAP = 128

epsilon = 1e-06
gelu_root = 0.7978845608028654
gelu_cubic = 0.044715

bf16 = jnp.bfloat16
f32 = jnp.float32


def norm_parts(values):
    centered = values - jnp.mean(values, axis=-1, keepdims=True)
    inv_std = lax.rsqrt(jnp.mean(centered * centered, axis=-1, keepdims=True) + epsilon)
    return (centered * inv_std, inv_std)


def norm_back(grad_normed, normed, inv_std):
    mean_grad = jnp.mean(grad_normed, axis=-1, keepdims=True)
    mean_cross = jnp.mean(grad_normed * normed, axis=-1, keepdims=True)
    return inv_std * (grad_normed - mean_grad - normed * mean_cross)


def gelu_parts(values):
    inner_arg = gelu_root * (values + gelu_cubic * values * values * values)
    tangent = jnp.tanh(inner_arg)
    activation = 0.5 * values * (1.0 + tangent)
    slope = 0.5 * (1.0 + tangent) + 0.5 * values * (1.0 - tangent * tangent) * gelu_root * (
        1.0 + 3.0 * gelu_cubic * values * values
    )
    return (activation, slope)


def mm(spec, a, b):
    return jnp.einsum(spec, a, b, preferred_element_type=f32)


def swap(value, mask):
    size = lax.axis_size("expert")
    return lax.ppermute(value, "expert", [(i, i ^ mask) for i in range(size)])


def gather_group(value):
    across = swap(value, 2)
    beside = swap(jnp.stack([value, across]), 1)
    return jnp.stack([value, beside[0], across, beside[1]])


def reduce_group(parts):
    beside = swap(jnp.stack([parts[1], parts[3]]).astype(bf16), 1).astype(f32)
    own = parts[0] + beside[0]
    other = (parts[2] + beside[1]).astype(bf16)
    return own + swap(other, 2).astype(f32)


def in_order(relative, position):
    return jnp.stack(
        [
            lax.dynamic_index_in_dim(relative, position ^ a, 0, keepdims=False)
            for a in range(relative.shape[0])
        ]
    )


def body(
    tokens,
    conditioning,
    routes,
    gate_weights,
    image_counts,
    image_lengths,
    cotangent,
    qkv_weight,
    qv_bias,
    proj_weight,
    proj_bias,
    ada_weight,
    ada_bias,
    up_weight,
    up_bias,
    down_weight,
    down_bias,
    routed_up,
    routed_upbias,
    routed_down,
    routed_downbias,
):
    group = lax.axis_size("expert")
    copies = lax.axis_size("dp")
    position = lax.axis_index("expert")
    place = lax.axis_index("dp")
    rows, width = tokens.shape
    group_rows = group * rows
    score_scale = HEAD_DIM ** (-0.5)
    heads_own = HEADS // group
    cols_own = heads_own * HEAD_DIM
    d_rows = qkv_weight.shape[0]
    f_rows = down_weight.shape[0]
    f_own = f_rows // group
    hidden_units = f_rows * copies
    quarter = hidden_units // group
    chunks = hidden_units // width

    qkv_share = lax.dynamic_index_in_dim(
        qkv_weight.reshape(d_rows, 3, group, cols_own), position, 2, keepdims=False
    ).reshape(d_rows, 3 * cols_own)
    first_share = jnp.concatenate([proj_weight, qkv_share], axis=1)
    wide = first_share.shape[1]
    bias_list = [qv_bias, proj_bias, up_bias, down_bias, routed_upbias[0], routed_downbias[0]]
    bias_sizes = [b.shape[0] for b in bias_list]
    bias_flat = jnp.concatenate(bias_list)
    bias_rows = 16
    bias_flat = jnp.pad(bias_flat, (0, bias_rows * wide - bias_flat.shape[0])).reshape(
        bias_rows, wide
    )
    first_all = lax.all_gather(jnp.concatenate([first_share, bias_flat]), "dp", axis=0)
    proj_full = first_all[:, :d_rows, :width].reshape(width, width)
    qkv_own = first_all[:, :d_rows, width:].reshape(width, 3 * cols_own)
    bias_all = first_all[:, d_rows:, :].reshape(copies, bias_rows * wide)
    offsets = [sum(bias_sizes[:i]) for i in range(len(bias_sizes))]
    qvb, projb, upb, downb, rupb, rdownb = (
        bias_all[:, o : o + n].reshape(copies * n).astype(f32)
        for o, n in zip(offsets, bias_sizes)
    )

    up_share = lax.dynamic_index_in_dim(
        up_weight.reshape(d_rows, copies, group, f_own), position, 2, keepdims=False
    ).reshape(d_rows, quarter)
    down_share = lax.dynamic_slice_in_dim(down_weight, position * f_own, f_own, axis=0)
    rup_share = [routed_up[0, :, c * width : (c + 1) * width] for c in range(chunks)]
    second_share = jnp.concatenate([*rup_share, up_share, routed_down[0], down_share], axis=0)
    second_all = lax.all_gather(second_share, "dp", axis=0)

    def piece(at, count):
        return second_all[:, at : at + count, :].reshape(copies * count, width)

    rup = jnp.concatenate([piece(c * d_rows, d_rows) for c in range(chunks)], axis=1)
    up_own = piece(chunks * d_rows, d_rows)
    rdown = piece((chunks + 1) * d_rows, f_rows)
    down_own = piece((chunks + 1) * d_rows + f_rows, f_own)

    both = gather_group(jnp.concatenate([tokens, cotangent], axis=1))
    residual = both[:, :, :width].astype(f32)
    upstream = both[:, :, width:].astype(f32)
    pairs = gather_group(jnp.concatenate([routes.astype(f32).T, gate_weights.T], axis=0))

    lengths = image_lengths[0]
    image_total = image_counts[0]
    slots = lengths.shape[0]
    slot_ids = jnp.arange(slots, dtype=jnp.int32)
    starts = jnp.sum(
        jnp.where(slot_ids[None, :] < slot_ids[:, None], lengths[None, :], 0), axis=1
    )
    live = (slot_ids >= 1) & (slot_ids < image_total)
    block_ids = position ^ jnp.arange(group, dtype=jnp.int32)
    segment = jnp.sum(
        (live[None, :] & (starts[None, :] <= (block_ids * rows)[:, None])).astype(jnp.int32),
        axis=1,
    )
    block_hot = segment[:, None] == slot_ids[None, :]

    chosen = (pairs[:, 0:2, :] == position.astype(f32)).astype(f32)
    hot = chosen[:, 0] + chosen[:, 1]
    gate_own = chosen[:, 0] * pairs[:, 2] + chosen[:, 1] * pairs[:, 3]
    row_ids = jnp.arange(rows, dtype=jnp.int32)
    earlier = (row_ids[:, None] < row_ids[None, :]).astype(bf16)
    rank = mm("bu,ut->bt", hot.astype(bf16), earlier)
    kept = hot * (rank < CAP).astype(f32)
    cap_ids = jnp.arange(CAP, dtype=jnp.int32).astype(f32)
    table = (kept[:, None, :] * (rank[:, None, :] == cap_ids[None, :, None]).astype(f32)).astype(
        bf16
    )
    count_own = jnp.sum(kept)

    cond_value = conditioning[0].astype(f32)
    cond_act = jax.nn.silu(cond_value).astype(bf16)
    act_parts = lax.all_to_all(
        cond_act.reshape(slots, copies, d_rows).transpose(1, 0, 2),
        "dp",
        split_axis=0,
        concat_axis=0,
        tiled=True,
    ).reshape(copies * slots, d_rows)
    mod_width = ada_weight.shape[1]
    bias_line = lax.dynamic_update_slice(
        jnp.zeros((mod_width,), f32), ada_bias.astype(f32), (place * ada_bias.shape[0],)
    )
    mod_parts = mm("sd,dm->sm", act_parts, ada_weight) + bias_line[None, :]
    mod_parts = jnp.concatenate(
        [mod_parts, jnp.full((copies * slots, 128), count_own, f32)], axis=1
    ).reshape(copies, slots, mod_width + 128)
    mod_sum = jnp.sum(
        lax.all_to_all(mod_parts, "dp", split_axis=0, concat_axis=0, tiled=True), axis=0
    )
    modulation = mod_sum[:, :mod_width]
    expert_total = mod_sum[0, mod_width:]
    per_block = jnp.sum(
        jnp.where(block_hot[:, :, None], modulation[None, :, :], 0.0), axis=1
    )
    shift_a, scale_a, gate_a, shift_b, scale_b, gate_b = (
        per_block[:, None, i * width : (i + 1) * width] for i in range(6)
    )

    normed_a, inv_std_a = norm_parts(residual)
    hidden_a = (normed_a * (1.0 + scale_a) + shift_a).astype(bf16).reshape(group_rows, width)
    q_bias = lax.dynamic_slice_in_dim(qvb, position * cols_own, cols_own)
    v_bias = lax.dynamic_slice_in_dim(qvb, width + position * cols_own, cols_own)
    bias_three = jnp.concatenate([q_bias, jnp.zeros((cols_own,), f32), v_bias])
    projected = (mm("td,de->te", hidden_a, qkv_own) + bias_three).astype(bf16)
    query, key, value = (
        projected[:, i * cols_own : (i + 1) * cols_own].reshape(group_rows, heads_own, HEAD_DIM)
        for i in range(3)
    )
    segment_rows = jnp.repeat(segment, rows)
    same_image = segment_rows[:, None] == segment_rows[None, :]
    scores = mm("qhd,khd->hqk", query, key) * score_scale
    masked = jnp.where(same_image[None], scores, -1e30)
    row_top = jnp.max(masked, axis=-1, keepdims=True)
    exponent = jnp.exp(masked - row_top)
    row_total = jnp.sum(exponent, axis=-1, keepdims=True)
    logsum = row_top + jnp.log(row_total)
    attended_own = (
        mm("hqk,khd->qhd", (exponent / row_total).astype(bf16), value)
        .reshape(group, rows, cols_own)
        .astype(bf16)
    )
    heads_all = gather_group(attended_own)
    attended = jnp.concatenate(
        [
            jnp.concatenate([heads_all[k, m ^ k] for k in range(group)], axis=1)
            for m in range(group)
        ],
        axis=0,
    )
    proj_rel = in_order(proj_full.reshape(group, cols_own, width), position)
    attn_out = mm("td,de->te", attended, proj_rel.reshape(width, width)) + projb
    attn_out = attn_out.reshape(group, rows, width)
    residual_mid = residual + gate_a * attn_out
    normed_b, inv_std_b = norm_parts(residual_mid)
    hidden_b3 = (normed_b * (1.0 + scale_b) + shift_b).astype(bf16)
    hidden_b = hidden_b3.reshape(group_rows, width)

    upb_own = lax.dynamic_index_in_dim(
        upb.reshape(copies, group, f_own), position, 1, keepdims=False
    ).reshape(quarter)
    shared_pre = mm("td,df->tf", hidden_b, up_own) + upb_own
    shared_act, shared_slope = gelu_parts(shared_pre)
    shared_hid = shared_act.astype(bf16)
    buffer = mm("bct,btd->bcd", table, hidden_b3).astype(bf16).reshape(group * CAP, width)
    expert_pre = mm("sd,df->sf", buffer, rup) + rupb
    expert_act, expert_slope = gelu_parts(expert_pre)
    expert_hid = expert_act.astype(bf16)

    grad_comb = gate_b * upstream
    grad_comb_low = grad_comb.astype(bf16).reshape(group_rows, width)
    pair_grad = (gate_own[:, :, None] * grad_comb).astype(bf16)
    slot_grad = mm("bct,btd->bcd", table, pair_grad).astype(bf16).reshape(group * CAP, width)

    def scatter(value):
        return lax.psum_scatter(value, "dp", scatter_dimension=0, tiled=False)

    rdown_grad = mm("sf,sd->fd", expert_hid, slot_grad).astype(bf16)
    down_grad = mm("tf,td->fd", shared_hid, grad_comb_low).astype(bf16)
    sums_one = scatter(
        jnp.concatenate(
            [
                rdown_grad.reshape(copies, f_rows, width),
                down_grad.reshape(copies, f_own, width),
            ],
            axis=1,
        )
    )

    grad_shared_hid = mm("td,fd->tf", grad_comb_low, down_own)
    grad_shared_pre = (grad_shared_hid * shared_slope).astype(bf16)
    grad_expert_hid = mm("sd,fd->sf", slot_grad, rdown)
    grad_expert_pre = (grad_expert_hid * expert_slope).astype(bf16)
    rup_grad = mm("sd,sf->df", buffer, grad_expert_pre).astype(bf16)
    up_grad = mm("td,tf->df", hidden_b, grad_shared_pre).astype(bf16)
    bias_row = jnp.concatenate(
        [
            jnp.sum(grad_expert_pre.astype(f32), axis=0).reshape(copies, f_rows),
            jnp.sum(grad_shared_pre.astype(f32), axis=0).reshape(copies, f_own),
            jnp.sum(slot_grad.astype(f32), axis=0).reshape(copies, d_rows),
            jnp.sum(grad_comb_low.astype(f32), axis=0).reshape(copies, d_rows),
        ],
        axis=1,
    ).astype(bf16)
    bias_used = bias_row.shape[1]
    bias_row = jnp.pad(bias_row, ((0, 0), (0, width - bias_used)))[:, None, :]
    bias_row = jnp.pad(bias_row, ((0, 0), (0, 15), (0, 0)))
    sums_two = scatter(
        jnp.concatenate(
            [
                *(
                    rup_grad[:, c * width : (c + 1) * width].reshape(copies, d_rows, width)
                    for c in range(chunks)
                ),
                up_grad.reshape(copies, d_rows, quarter),
                bias_row,
            ],
            axis=1,
        )
    )

    grad_buffer = mm("sf,df->sd", grad_expert_pre, rup).astype(bf16).reshape(group, CAP, width)
    hidden_parts = mm("tf,df->td", grad_shared_pre, up_own).reshape(group, rows, width) + mm(
        "bct,bcd->btd", table, grad_buffer
    )
    grad_hidden_b = reduce_group(hidden_parts)

    expert_out = (mm("sf,fd->sd", expert_hid, rdown) + rdownb).astype(bf16)
    routed_parts = gate_own[:, :, None] * mm(
        "bct,bcd->btd", table, expert_out.reshape(group, CAP, width)
    )
    shared_parts = mm("tf,fd->td", shared_hid, down_own).reshape(group, rows, width)
    combined = reduce_group(shared_parts + routed_parts) + downb
    output = (residual_mid[0] + gate_b[0] * combined).astype(bf16)

    grad_gate_b = upstream[0] * combined
    grad_scale_b = grad_hidden_b * normed_b[0]
    grad_mid = upstream[0] + norm_back(
        grad_hidden_b * (1.0 + scale_b[0]), normed_b[0], inv_std_b[0]
    )
    grad_gate_a = grad_mid * attn_out[0]
    grad_attn_own = (gate_a[0] * grad_mid).astype(bf16)
    grad_attn = gather_group(grad_attn_own).reshape(group_rows, width)

    grad_attn_cols = lax.dynamic_slice_in_dim(grad_attn, position * cols_own, cols_own, axis=1)
    proj_grad = in_order(
        mm("td,te->de", attended, grad_attn_cols).reshape(group, cols_own, cols_own), position
    ).reshape(copies, d_rows, cols_own)
    grad_attended = (
        mm("te,de->td", grad_attn, proj_rel[0]).astype(bf16).reshape(group_rows, heads_own, HEAD_DIM)
    )
    again = jnp.where(same_image[None], mm("qhd,khd->hqk", query, key) * score_scale, -1e30)
    again_probs = jnp.exp(again - logsum)
    grad_value = mm("hqk,qhd->khd", again_probs.astype(bf16), grad_attended)
    grad_probs = mm("qhd,khd->hqk", grad_attended, value)
    inner_sum = jnp.sum(again_probs * grad_probs, axis=-1, keepdims=True)
    grad_scores = (again_probs * (grad_probs - inner_sum)).astype(bf16)
    grad_query = mm("hqk,khd->qhd", grad_scores, key) * score_scale
    grad_key = mm("hqk,qhd->khd", grad_scores, query) * score_scale
    grad_projected = jnp.concatenate(
        [g.reshape(group_rows, cols_own) for g in (grad_query, grad_key, grad_value)], axis=1
    ).astype(bf16)
    qkv_grad = mm("td,te->de", hidden_a, grad_projected)
    sums_qkv = jnp.sum(grad_projected.astype(f32), axis=0)
    qv_line = lax.dynamic_update_slice(
        jnp.zeros((2 * width,), f32), sums_qkv[:cols_own], (position * cols_own,)
    )
    qv_line = lax.dynamic_update_slice(
        qv_line, sums_qkv[2 * cols_own :], (width + position * cols_own,)
    ).reshape(copies, -1)
    pb_line = jnp.sum(grad_attn.astype(f32), axis=0).reshape(copies, d_rows)
    tail_width = 4 * cols_own
    small_row = jnp.concatenate([qv_line, pb_line], axis=1)
    small_row = jnp.pad(small_row, ((0, 0), (0, tail_width - small_row.shape[1])))[:, None, :]
    small_row = jnp.pad(small_row, ((0, 0), (0, 15), (0, 0)))
    sums_three = scatter(
        jnp.concatenate(
            [
                jnp.concatenate([qkv_grad.reshape(copies, d_rows, 3 * cols_own), proj_grad], axis=2),
                small_row,
            ],
            axis=1,
        ).astype(bf16)
    )

    grad_hidden_a = reduce_group(
        mm("te,de->td", grad_projected, qkv_own).reshape(group, rows, width)
    )
    grad_scale_a = grad_hidden_a * normed_a[0]
    tokens_grad = grad_mid + norm_back(
        grad_hidden_a * (1.0 + scale_a[0]), normed_a[0], inv_std_a[0]
    )

    block_sums = jnp.concatenate(
        [
            jnp.sum(g, axis=0)
            for g in (
                grad_hidden_a,
                grad_scale_a,
                grad_gate_a,
                grad_hidden_b,
                grad_scale_b,
                grad_gate_b,
            )
        ]
        + [expert_total]
    )
    group_sums = gather_group(block_sums[None])[:, 0]
    grad_modulation = jnp.sum(
        jnp.where(block_hot[:, :, None], group_sums[:, None, :mod_width], 0.0), axis=0
    ).astype(bf16)
    counts_rel = group_sums[:, mod_width]
    expert_counts = in_order(counts_rel, position).astype(jnp.int32)
    mod_all = lax.all_to_all(
        jnp.broadcast_to(grad_modulation[None], (copies, slots, mod_width)),
        "dp",
        split_axis=0,
        concat_axis=0,
        tiled=True,
    ).reshape(copies * slots, mod_width)
    ada_grad = mm("sd,sm->dm", act_parts, mod_all)
    adabias_grad = jnp.sum(
        lax.dynamic_slice_in_dim(
            mod_all, place * ada_bias.shape[0], ada_bias.shape[0], axis=1
        ).astype(f32),
        axis=0,
    )
    cond_parts = mm("sm,dm->sd", mod_all, ada_weight).reshape(copies, slots, d_rows)
    grad_cond_act = (
        lax.all_to_all(cond_parts, "dp", split_axis=0, concat_axis=0, tiled=True)
        .transpose(1, 0, 2)
        .reshape(slots, width)
    )
    sigmoid_cond = jax.nn.sigmoid(cond_value)
    conditioning_grad = (grad_cond_act * sigmoid_cond * (1.0 + cond_value * (1.0 - sigmoid_cond)))[
        None
    ]

    down_rows = in_order(gather_group(sums_one[f_rows:]), position).reshape(f_rows, width)
    up_and_bias = in_order(gather_group(sums_two[chunks * d_rows :]), position)
    up_rows = (
        up_and_bias[:, :d_rows]
        .reshape(group, d_rows, copies, f_own)
        .transpose(1, 2, 0, 3)
        .reshape(d_rows, hidden_units)
    )
    upbias_rows = up_and_bias[:, d_rows, f_rows : f_rows + f_own].reshape(f_rows)
    line = sums_two[(chunks + 1) * d_rows].astype(f32)
    rupbias_row = line[:f_rows]
    rdownbias_row = line[f_rows + f_own : f_rows + f_own + d_rows]
    downbias_row = line[f_rows + f_own + d_rows : f_rows + f_own + 2 * d_rows]
    rup_rows = jnp.concatenate(
        [sums_two[c * d_rows : (c + 1) * d_rows] for c in range(chunks)], axis=1
    )
    last = in_order(gather_group(sums_three), position)
    qkv_rows = (
        last[:, :d_rows, : 3 * cols_own]
        .reshape(group, d_rows, 3, cols_own)
        .transpose(1, 2, 0, 3)
        .reshape(d_rows, 3 * width)
    )
    proj_rows = last[:, :d_rows, 3 * cols_own :].transpose(1, 0, 2).reshape(d_rows, width)
    qv_count = 2 * width // copies
    qvbias_rows = jnp.sum(last[:, d_rows, :qv_count].astype(f32), axis=0)
    projbias_rows = last[0, d_rows, qv_count : qv_count + d_rows]

    return (
        output,
        tokens_grad,
        conditioning_grad,
        qkv_rows.astype(f32),
        qvbias_rows,
        proj_rows.astype(f32),
        projbias_rows.astype(f32),
        ada_grad,
        adabias_grad,
        up_rows.astype(f32),
        upbias_rows.astype(f32),
        down_rows.astype(f32),
        downbias_row,
        rup_rows.astype(f32)[None],
        rupbias_row[None],
        sums_one[:f_rows].astype(f32)[None],
        rdownbias_row[None],
        expert_counts,
    )


def solution(mesh):
    in_specs = (
        P(("dp", "expert"), None),
        P("dp", None, None),
        P(("dp", "expert"), None),
        P(("dp", "expert"), None),
        P("dp"),
        P("dp", None),
        P(("dp", "expert"), None),
        P("dp", None),
        P("dp"),
        P("dp", None),
        P("dp"),
        P("dp", None),
        P("dp"),
        P("dp", None),
        P("dp"),
        P("dp", None),
        P("dp"),
        P("expert", "dp", None),
        P("expert", "dp"),
        P("expert", "dp", None),
        P("expert", "dp"),
    )
    out_specs = (
        P(("dp", "expert"), None),
        P(("dp", "expert"), None),
        P("dp", None, None),
        P("dp", None),
        P("dp"),
        P("dp", None),
        P("dp"),
        P("dp", None),
        P("dp"),
        P("dp", None),
        P("dp"),
        P("dp", None),
        P("dp"),
        P("expert", "dp", None),
        P("expert", "dp"),
        P("expert", "dp", None),
        P("expert", "dp"),
        P(),
    )
    return jax.shard_map(body, mesh=mesh, in_specs=in_specs, out_specs=out_specs, check_vma=False)
```

```python
import jax
import jax.numpy as jnp
from jax import lax
from jax.experimental import pallas as pl
from jax.experimental.pallas import tpu as pltpu
from jax.sharding import PartitionSpec as P

HEADS = 12
HEAD_DIM = 64
CAP = 128

epsilon = 1e-06
gelu_root = 0.7978845608028654
gelu_cubic = 0.044715

bf16 = jnp.bfloat16
f32 = jnp.float32


def norm_parts(values):
    centered = values - jnp.mean(values, axis=-1, keepdims=True)
    inv_std = lax.rsqrt(jnp.mean(centered * centered, axis=-1, keepdims=True) + epsilon)
    return (centered * inv_std, inv_std)


def norm_back(grad_normed, normed, inv_std):
    mean_grad = jnp.mean(grad_normed, axis=-1, keepdims=True)
    mean_cross = jnp.mean(grad_normed * normed, axis=-1, keepdims=True)
    return inv_std * (grad_normed - mean_grad - normed * mean_cross)


def gelu_parts(values):
    square = values * values
    half = 0.5 + 0.5 * jnp.tanh(values * (gelu_root + gelu_root * gelu_cubic * square))
    activation = values * half
    slope = half + activation * (1.0 - half) * (
        2.0 * gelu_root + 6.0 * gelu_root * gelu_cubic * square
    )
    return (activation, slope)


def mm(spec, a, b):
    return jnp.einsum(spec, a, b, preferred_element_type=f32)


def swap(value, mask):
    size = lax.axis_size("expert")
    return lax.ppermute(value, "expert", [(i, i ^ mask) for i in range(size)])


def gather_group(value):
    across = swap(value, 2)
    beside = swap(jnp.stack([value, across]), 1)
    return jnp.stack([value, beside[0], across, beside[1]])


def reduce_group(send, keep):
    beside = swap(send, 1).astype(f32)
    own = keep[0] + beside[0]
    other = (keep[1] + beside[1]).astype(bf16)
    return own, swap(other, 2)


def dp_swap(value, mask):
    copies = lax.axis_size("dp")
    return lax.ppermute(value, "dp", [(i, i ^ mask) for i in range(copies)])


def pair_swap(value):
    return dp_swap(value, 2)


def side_groups(copies):
    return [[i for i in range(copies) if (i >> 1) % 2 == side] for side in range(2)]


def pair_places(p):
    first = ((p >> 1) << 2) | (p & 1)
    return first, first + 2


def spread(value):
    far = dp_swap(value, 4)
    return [value, dp_swap(value, 1), far, dp_swap(far, 1)]


def collect(send, keep, start, middle, end):
    got = dp_swap(tied(send, *start), 1)
    wide = tied(got, *middle).astype(f32)
    far = dp_swap((keep[1] + wide[1]).astype(bf16), 4)
    return keep[0] + wide[0] + tied(far, *end).astype(f32), got


def tied(value, *others):
    return lax.optimization_barrier((value, *others))[0]


def ring_place(at, copies):
    at = lax.rem(at + copies, copies)
    return jnp.where(at < copies // 2, 2 * at, 2 * (copies - 1 - at) + 1)


def ring_gather(share):
    copies = lax.axis_size("dp")
    if copies > 8:
        whole = lax.all_gather(share, "dp", axis=0)
        whole = whole.reshape((8, copies // 8 * share.shape[0]) + share.shape[1:])
        return [whole[k] for k in range(8)], jnp.arange(8, dtype=jnp.int32)
    half = copies // 2
    ring = [2 * i for i in range(half)] + [2 * i + 1 for i in reversed(range(half))]
    place = lax.axis_index("dp")
    position = jnp.where(lax.rem(place, 2) == 0, place // 2, copies - 1 - place // 2)

    def hop(value, way):
        return lax.ppermute(
            value, "dp", [(ring[i], ring[(i + way) % copies]) for i in range(copies)]
        )

    pieces, offsets = [share], [0]
    right = left = share
    for step in range(1, half + 1):
        right = hop(right, 1)
        pieces.append(right)
        offsets.append(-step)
        if step < half:
            left = hop(left, -1)
            pieces.append(left)
            offsets.append(step)
    return pieces, ring_place(position + jnp.array(offsets, jnp.int32), copies)


def dot(a, b, left=1, right=0):
    return lax.dot_general(
        a, b, (((left,), (right,)), ((), ())), preferred_element_type=f32
    )


def full(shape):
    return pl.BlockSpec(shape, lambda i: (0,) * len(shape), pipeline_mode=pl.Buffered(1))


SCALARS = pl.BlockSpec(memory_space=pltpu.SMEM)


def kernel_call(body, grid, in_specs, out_specs, out_shape, scratch, flops, operands):
    out_bytes = sum(int(o.size) * o.dtype.itemsize for o in out_shape)
    in_bytes = sum(int(o.size) * o.dtype.itemsize for o in operands)
    return pl.pallas_call(
        body,
        grid=(grid,),
        in_specs=in_specs,
        out_specs=out_specs,
        out_shape=out_shape,
        scratch_shapes=scratch,
        compiler_params=pltpu.CompilerParams(vmem_limit_bytes=56 * 2**20),
        cost_estimate=pl.CostEstimate(
            flops=int(flops), bytes_accessed=out_bytes + in_bytes, transcendentals=0
        ),
    )(*operands)


def shape(dims, dtype):
    return jax.ShapeDtypeStruct(dims, dtype)


def prepare(info, proj, qkv, biases, up, down, rup, rdown, keep, group):
    d_rows, width = proj.shape
    cols = width // group
    f_rows = down.shape[0]
    f_own = f_rows // group
    count = up.shape[1] // f_rows
    wide = 3 * cols

    def body(info, proj, qkv, *refs):
        biases, (up, down, rup, rdown, first, third, mine, theirs, d_mine, d_theirs) = (
            refs[: len(biases_in)],
            refs[len(biases_in) :],
        )
        third[d_rows + f_own :, :] = proj[...]
        lines = [
            jnp.concatenate([b[...].astype(f32), jnp.zeros((1, wide - b.shape[1]), f32)], axis=1)
            for b in biases[1:]
        ]
        for p in range(group):

            @pl.when(info[8] == p)
            def _():
                own = slice(p * f_own, (p + 1) * f_own)
                first[:d_rows, :] = jnp.concatenate(
                    [qkv[:, i * width + p * cols : i * width + (p + 1) * cols] for i in range(3)],
                    axis=1,
                )
                line = jnp.concatenate(
                    [biases[0][:, own].astype(f32), jnp.zeros((1, wide - f_own), f32)], axis=1
                )
                first[d_rows:, :] = jnp.concatenate(
                    [line] + lines + [jnp.zeros((15 - len(lines), wide), f32)], axis=0
                ).astype(bf16)
                third[:d_rows, :] = jnp.concatenate(
                    [
                        up[:, d * f_rows + p * f_own : d * f_rows + (p + 1) * f_own]
                        for d in range(count)
                    ],
                    axis=1,
                )
                third[d_rows : d_rows + f_own, :] = down[own, :]

        one, two = [], []
        for p in range(count // 2):
            at, to = (d * f_rows for d in pair_places(p))
            one += [(at, at + keep), (to, to + f_rows - keep)]
            two += [(to + f_rows - keep, to + f_rows), (at + keep, at + f_rows)]
        for side in range(2):

            @pl.when(info[9] == side)
            def _():
                own, other = (one, two) if side == 0 else (two, one)
                for ref, parts in ((mine, own), (theirs, other)):
                    at = 0
                    for low, high in parts:
                        ref[:, at : at + high - low] = rup[:, low:high]
                        at += high - low
                start = side * (f_rows - keep)
                d_mine[...] = rdown[start : start + keep, :]
                start = (1 - side) * keep
                d_theirs[...] = rdown[start : start + f_rows - keep, :]

    biases_in = biases
    operands = [proj, qkv, *biases, up, down, rup, rdown]
    outs = [
        shape((d_rows + 16, wide), bf16),
        shape((2 * d_rows + f_own, width), bf16),
        shape((d_rows, rup.shape[1] // 2), bf16),
        shape((d_rows, rup.shape[1] // 2), bf16),
        shape((keep, width), bf16),
        shape((f_rows - keep, width), bf16),
    ]
    return kernel_call(
        body,
        1,
        [SCALARS] + [full(o.shape) for o in operands],
        [full(o.shape) for o in outs],
        outs,
        [],
        0,
        [info, *operands],
    )


def middle_back(own, got, middle_rows, attn_out, cotangent, mods):
    rows, width = own.shape

    def body(own, got, mid, out, cot, mod, grad_mid, grad_attn, sums):
        grad = own[...] + got[...].astype(f32)
        normed, inv_std = norm_parts(mid[...])
        value = cot[...].astype(f32) + norm_back(
            grad * (1.0 + mod[0, 4:5, :]), normed, inv_std
        )
        grad_mid[...] = value
        grad_attn[...] = (mod[0, 2:3, :] * value).astype(bf16)
        sums[0:1, :] = jnp.sum(value * out[...], axis=0, keepdims=True)
        sums[1:2, :] = jnp.sum(grad, axis=0, keepdims=True)
        sums[2:3, :] = jnp.sum(grad * normed, axis=0, keepdims=True)
        sums[3:, :] = jnp.zeros((5, width), f32)

    operands = [own, got, middle_rows, attn_out, cotangent]
    outs = [shape((rows, width), f32), shape((rows, width), bf16), shape((8, width), f32)]
    return kernel_call(
        body,
        1,
        [full(o.shape) for o in operands] + [pl.BlockSpec((1, 8, width), lambda i: (0, 0, 0))],
        [full(o.shape) for o in outs],
        outs,
        [],
        0,
        [*operands, mods],
    )


def routed_rows(info, up_own, up_got, down_own, down_got, keep):
    d_rows, half = up_got.shape
    f_rows = down_own.shape[0]
    width = down_own.shape[1]
    pairs = half // f_rows

    def body(info, uo, ug, do, dg, up, down):
        for side in range(2):

            @pl.when(info[9] == side)
            def _():
                first, second = (0, 1) if side == 0 else (1, 0)
                values = (uo[:d_rows, :], ug[...].astype(f32))
                for p in range(pairs):
                    at, to = (d * f_rows for d in pair_places(p))
                    for whose, low, high, frm in (
                        (first, at, at + keep, 0),
                        (first, to, to + f_rows - keep, keep),
                        (second, to + f_rows - keep, to + f_rows, 0),
                        (second, at + keep, at + f_rows, keep),
                    ):
                        base = p * f_rows + frm
                        up[:, low:high] = values[whose][:, base : base + high - low]
                start = side * (f_rows - keep)
                down[start : start + keep, :] = do[:keep, :]
                start = (1 - side) * keep
                down[start : start + f_rows - keep, :] = dg[...].astype(f32)

    operands = [up_own, up_got, down_own, down_got]
    outs = [shape((d_rows, 2 * half), f32), shape((f_rows, width), f32)]
    return kernel_call(
        body,
        1,
        [SCALARS] + [full(o.shape) for o in operands],
        [full(o.shape) for o in outs],
        outs,
        [],
        0,
        [info, *operands],
    )


def group_rows_out(info, shared, last, d_rows, f_rows):
    group, _, width = shared.shape
    f_own = f_rows // group
    cols = width // group
    count = width // f_own

    def body(info, shared, last, up, down, qkv, proj):
        for a in range(group):
            part = shared[info[8] ^ a].astype(f32)
            for d in range(count):
                at = d * f_rows + a * f_own
                up[:, at : at + f_own] = part[:d_rows, d * f_own : (d + 1) * f_own]
            down[a * f_own : (a + 1) * f_own, :] = part[d_rows:, :]
            part = last[info[8] ^ a].astype(f32)
            for i in range(3):
                at = i * width + a * cols
                qkv[:, at : at + cols] = part[:, i * cols : (i + 1) * cols]
            proj[:, a * cols : (a + 1) * cols] = part[:, 3 * cols :]

    outs = [
        shape((d_rows, count * f_rows), f32),
        shape((f_rows, width), f32),
        shape((d_rows, 3 * width), f32),
        shape((d_rows, width), f32),
    ]
    return kernel_call(
        body,
        1,
        [SCALARS, full(shared.shape), full(last.shape)],
        [full(o.shape) for o in outs],
        outs,
        [],
        0,
        [info, shared, last],
    )


def front(info, tokens, mods, bias, pairs, pieces, rows_piece, cols_own, cut):
    blocks, rows, _ = tokens.shape
    width = 8 * rows_piece
    wide = 3 * cols_own

    def body(info, tok, mod, bias, pairs, *refs):
        parts = refs[:8]
        (hid, prj, qkv, table, gates, low_grad, slot, sums, lines, units, three, lists) = refs[8:]
        step = pl.program_id(0)

        @pl.when(step == 0)
        def _():
            for k in range(8):
                at = pl.multiple_of(info[k] * rows_piece, rows_piece)
                qkv[pl.ds(at, rows_piece), :] = parts[k][:rows_piece, :]
                if cut:
                    lists[info[k]] = parts[k][rows_piece:, :].astype(f32)
            three[...] = bias[...]
            if cut:
                three[:, :cols_own] = lists[info[8]][2:3, :cols_own]
                three[:, 2 * cols_own :] = lists[info[8] + 4][2:3, :cols_own]
                lines[...] = jnp.zeros_like(lines)
                for d in range(8):
                    at = slice(d * rows_piece, (d + 1) * rows_piece)
                    for i, row in enumerate((0, 3, 4, 5)):
                        lines[i : i + 1, at] = lists[d, row : row + 1, :rows_piece]
                size = units.shape[2]
                for side in range(2):

                    @pl.when(info[9] == side)
                    def _():
                        for p in range(units.shape[0]):
                            one, two = pair_places(p)
                            if side == 0:
                                units[p, :, :cut] = lists[one, 1:2, :cut]
                                units[p, :, cut:] = lists[two, 1:2, : size - cut]
                            else:
                                units[p, :, :cut] = lists[two, 1:2, size - cut : size]
                                units[p, :, cut:] = lists[one, 1:2, cut:size]

            sums[...] = jnp.zeros_like(sums)

        normed, _ = norm_parts(tok[0, :, :width].astype(f32))
        low = (normed * (1.0 + mod[0, 1:2, :]) + mod[0, 0:1, :]).astype(bf16)
        hid[...] = low
        prj[...] = (dot(low, qkv[...]) + three[...]).astype(bf16)

        me = info[8].astype(f32)
        one = (pairs[0, 0:1, :] == me).astype(f32)
        two = (pairs[0, 1:2, :] == me).astype(f32)
        hot = one + two
        gate = one * pairs[0, 2:3, :] + two * pairs[0, 3:4, :]
        across = lax.broadcasted_iota(jnp.int32, (rows, rows), 1)
        down = lax.broadcasted_iota(jnp.int32, (rows, rows), 0)
        earlier = (down < across).astype(f32).astype(bf16)
        rank = dot(jnp.broadcast_to(hot, (8, rows)).astype(bf16), earlier)[0:1, :]
        kept = hot * (rank < CAP).astype(f32)
        places = lax.broadcasted_iota(jnp.int32, (CAP, rows), 0).astype(f32)
        placed = jnp.where(rank == places, kept, 0.0)
        table[0] = placed.astype(bf16)
        gates[0] = jnp.sum(jnp.where(down == across, gate, 0.0), axis=1, keepdims=True)
        cot = tok[0, :, width:]
        grad = (mod[0, 5:6, :] * cot.astype(f32)).astype(bf16)
        low_grad[...] = grad
        gate_slot = jnp.sum(placed * gate, axis=1, keepdims=True)
        slot_grad = (gate_slot * (mod[0, 5:6, :] * dot(table[0], cot))).astype(bf16)
        slot[...] = slot_grad
        sums[0:1, :] += jnp.sum(slot_grad.astype(f32), axis=0, keepdims=True)
        sums[1:2, :] += jnp.sum(grad.astype(f32), axis=0, keepdims=True)
        sums[2:3, :] += jnp.broadcast_to(jnp.sum(kept, axis=1, keepdims=True), (1, width))

    return kernel_call(
        body,
        blocks,
        [
            SCALARS,
            pl.BlockSpec((1, rows, 2 * width), lambda i: (i, 0, 0)),
            pl.BlockSpec((1, 8, width), lambda i: (i, 0, 0)),
            full((1, wide)),
            pl.BlockSpec((1, 4, rows), lambda i: (i, 0, 0)),
        ]
        + [full(p.shape) for p in pieces],
        [
            pl.BlockSpec((rows, width), lambda i: (i, 0)),
            pl.BlockSpec((rows, wide), lambda i: (i, 0)),
            full((width, wide)),
            pl.BlockSpec((1, CAP, rows), lambda i: (i, 0, 0)),
            pl.BlockSpec((1, rows, 1), lambda i: (i, 0, 0)),
            pl.BlockSpec((rows, width), lambda i: (i, 0)),
            pl.BlockSpec((CAP, width), lambda i: (i, 0)),
            full((8, width)),
            full((8, width)),
            full((4, 1, width // 2)),
        ],
        [
            shape((blocks * rows, width), bf16),
            shape((blocks * rows, wide), bf16),
            shape((width, wide), bf16),
            shape((blocks, CAP, rows), bf16),
            shape((blocks, rows, 1), f32),
            shape((blocks * rows, width), bf16),
            shape((blocks * CAP, width), bf16),
            shape((8, width), f32),
            shape((8, width), f32),
            shape((4, 1, width // 2), f32),
        ],
        [pltpu.VMEM((1, wide), f32), pltpu.VMEM((8, 16, wide), f32)],
        2 * blocks * rows * width * wide,
        [info, tokens, mods, bias, pairs, *pieces],
    )


def to_rows(own, got, bias, table, gates, addend, tokens, line):
    blocks, cap, rows = table.shape
    width = own.shape[1]

    def body(own, got, bias, tab, gate, add, tok, line, send, keep, sums):
        slots = (own[...] + got[...].astype(f32) + bias[...]).astype(bf16)
        value = add[...] + gate[0] * dot(tab[0], slots, 0, 0)
        first = (pl.program_id(0) == 0).astype(f32)
        sums[0] = jnp.sum(
            tok[0].astype(f32) * (value + first * line[...]), axis=0, keepdims=True
        )
        for k in range(blocks):

            @pl.when(pl.program_id(0) == k)
            def _():
                if k % 2 == 1:
                    send[k // 2] = value.astype(bf16)
                else:
                    keep[k // 2] = value

    operands = [own, got, bias, table, gates, addend, tokens, line]
    return kernel_call(
        body,
        blocks,
        [
            pl.BlockSpec((cap, width), lambda i: (i, 0)),
            pl.BlockSpec((cap, width), lambda i: (i, 0)),
            full((1, width)),
            pl.BlockSpec((1, cap, rows), lambda i: (i, 0, 0)),
            pl.BlockSpec((1, rows, 1), lambda i: (i, 0, 0)),
            pl.BlockSpec((rows, width), lambda i: (i, 0)),
            pl.BlockSpec((1, rows, width), lambda i: (i, 0, 1)),
            full((1, width)),
        ],
        [
            full((2, rows, width)),
            full((2, rows, width)),
            pl.BlockSpec((1, 1, width), lambda i: (i, 0, 0)),
        ],
        [
            shape((2, rows, width), bf16),
            shape((2, rows, width), f32),
            shape((blocks, 1, width), f32),
        ],
        [],
        2 * blocks * rows * width * cap,
        operands,
    )


def score_parts(info, query, key, blocks, rows):
    own = info[10 + pl.program_id(0)]
    lanes = lax.broadcasted_iota(jnp.int32, (1, blocks * rows), 1) // rows
    seen = jnp.zeros((1, blocks * rows), jnp.int32)
    for j in range(blocks):
        seen = jnp.where((lanes == j) & (info[10 + j] == own), 1, seen)
    scores = dot(query, key, 1, 1) * (HEAD_DIM ** (-0.5))
    masked = jnp.where(seen == 1, scores, -1e30)
    exponent = jnp.exp(masked - jnp.max(masked, axis=-1, keepdims=True))
    return exponent / jnp.sum(exponent, axis=-1, keepdims=True)


def attention(info, projected, blocks, cols_own):
    total, wide = projected.shape
    rows = total // blocks

    def body(info, own, every, out):
        for h in range(cols_own // HEAD_DIM):
            q = slice(h * HEAD_DIM, (h + 1) * HEAD_DIM)
            k = slice(cols_own + h * HEAD_DIM, cols_own + (h + 1) * HEAD_DIM)
            v = slice(2 * cols_own + h * HEAD_DIM, 2 * cols_own + (h + 1) * HEAD_DIM)
            probs = score_parts(info, own[:, q], every[:, k], blocks, rows)
            out[:, q] = dot(probs.astype(bf16), every[:, v]).astype(bf16)

    return kernel_call(
        body,
        blocks,
        [SCALARS, pl.BlockSpec((rows, wide), lambda i: (i, 0)), full((total, wide))],
        [pl.BlockSpec((rows, cols_own), lambda i: (i, 0))],
        [shape((total, cols_own), bf16)],
        [],
        4 * total * total * cols_own,
        [info, projected, projected],
    )[0]


def attention_back(info, projected, grad_attn, proj_rel, blocks, cols_own):
    total, wide = projected.shape
    rows = total // blocks
    width = grad_attn.shape[1]
    scale = HEAD_DIM ** (-0.5)

    def body(info, own, every, grad, rel, out, sums_k, sums_v, sums_q):
        step = pl.program_id(0)

        @pl.when(step == 0)
        def _():
            sums_k[...] = jnp.zeros_like(sums_k)
            sums_v[...] = jnp.zeros_like(sums_v)

        back = dot(grad[...], rel[...], 1, 1).astype(bf16)
        for h in range(cols_own // HEAD_DIM):
            q = slice(h * HEAD_DIM, (h + 1) * HEAD_DIM)
            k = slice(cols_own + h * HEAD_DIM, cols_own + (h + 1) * HEAD_DIM)
            v = slice(2 * cols_own + h * HEAD_DIM, 2 * cols_own + (h + 1) * HEAD_DIM)
            probs = score_parts(info, own[:, q], every[:, k], blocks, rows)
            grad_probs = dot(back[:, q], every[:, v], 1, 1)
            inner = jnp.sum(probs * grad_probs, axis=-1, keepdims=True)
            scores = (probs * (grad_probs - inner)).astype(bf16)
            at = pl.multiple_of(step * rows, rows)
            sums_q[pl.ds(at, rows), q] = dot(scores, every[:, k]) * scale
            sums_k[:, q] += dot(scores, own[:, q], 0, 0)
            sums_v[:, q] += dot(probs.astype(bf16), back[:, q], 0, 0)

        @pl.when(step == blocks - 1)
        def _():
            out[:, :cols_own] = sums_q[...].astype(bf16)
            out[:, cols_own : 2 * cols_own] = (sums_k[...] * scale).astype(bf16)
            out[:, 2 * cols_own :] = sums_v[...].astype(bf16)

    return kernel_call(
        body,
        blocks,
        [
            SCALARS,
            pl.BlockSpec((rows, wide), lambda i: (i, 0)),
            full((total, wide)),
            pl.BlockSpec((rows, width), lambda i: (i, 0)),
            full((cols_own, width)),
        ],
        [full((total, wide))],
        [shape((total, wide), bf16)],
        [pltpu.VMEM((total, cols_own), f32)] * 3,
        10 * total * total * cols_own + 2 * total * width * cols_own,
        [info, projected, projected, grad_attn, proj_rel],
    )[0]


def middle(info, tokens, mods, heads, pieces, proj_bias, table, rows_piece):
    blocks, rows, _ = tokens.shape
    width = 8 * rows_piece
    cols = width // blocks
    cap = table.shape[1]

    def body(info, tok, mod, h0, h1, h2, h3, bias, tab, *refs):
        parts, (hid, att, buf, out0, mid0, own, rel) = refs[:4], refs[4:]

        @pl.when(pl.program_id(0) == 0)
        def _():
            for k in range(8):
                place = info[18 + k]
                at = ((place >> 1) ^ info[8]) * cols + (place & 1) * rows_piece
                at = pl.multiple_of(at, rows_piece)
                rel[pl.ds(at, rows_piece), :] = parts[k // 2][k % 2, -rows_piece:, :]
            own[...] = rel[:cols, :]

        attended = jnp.concatenate([h0[...], h1[...], h2[...], h3[...]], axis=1)
        att[...] = attended
        out = dot(attended, rel[...]) + bias[...]
        mid = tok[0].astype(f32) + mod[0, 2:3, :] * out
        normed, _ = norm_parts(mid)
        low = (normed * (1.0 + mod[0, 4:5, :]) + mod[0, 3:4, :]).astype(bf16)
        hid[...] = low
        buf[...] = dot(tab[0], low).astype(bf16)

        @pl.when(pl.program_id(0) == 0)
        def _():
            out0[...] = out
            mid0[...] = mid

    return kernel_call(
        body,
        blocks,
        [
            SCALARS,
            pl.BlockSpec((1, rows, width), lambda i: (i, 0, 0)),
            pl.BlockSpec((1, 8, width), lambda i: (i, 0, 0)),
            pl.BlockSpec((rows, cols), lambda i: (i, 0)),
            pl.BlockSpec((rows, cols), lambda i: (i ^ 1, 0)),
            pl.BlockSpec((rows, cols), lambda i: (i ^ 2, 0)),
            pl.BlockSpec((rows, cols), lambda i: (i ^ 3, 0)),
            full((1, width)),
            pl.BlockSpec((1, cap, rows), lambda i: (i, 0, 0)),
        ]
        + [full(p.shape) for p in pieces],
        [
            pl.BlockSpec((rows, width), lambda i: (i, 0)),
            pl.BlockSpec((rows, width), lambda i: (i, 0)),
            pl.BlockSpec((cap, width), lambda i: (i, 0)),
            full((rows, width)),
            full((rows, width)),
            full((cols, width)),
        ],
        [
            shape((blocks * rows, width), bf16),
            shape((blocks * rows, width), bf16),
            shape((blocks * cap, width), bf16),
            shape((rows, width), f32),
            shape((rows, width), f32),
            shape((cols, width), bf16),
        ],
        [pltpu.VMEM((width, width), bf16)],
        2 * blocks * rows * width * (width + cap),
        [info, tokens, mods, *heads, proj_bias, table, *pieces],
    )


def shared_expert(info, hidden, grad, bias, pieces, rows_piece, blocks, paired):
    total, width = hidden.shape
    rows = total // blocks
    pairs = 4
    sums_mine = (pairs, 2 * rows_piece, width) if paired else (2, width, width)
    sums_theirs = (pairs, 2 * rows_piece, width) if paired else (1, 8, width)

    def body(info, hid, gcl, bias, *refs):
        parts, (out, back, mine, theirs, line, up, down, up_sum, down_sum, wide) = refs[:4], refs[4:]
        step = pl.program_id(0)

        @pl.when(step == 0)
        def _():
            for k in range(8):
                at = pl.multiple_of(info[18 + k] * rows_piece, rows_piece)
                up[pl.ds(at, rows_piece), :] = parts[k // 2][k % 2, :rows_piece, :]
                down[pl.ds(at, rows_piece), :] = parts[k // 2][k % 2, rows_piece : 2 * rows_piece, :]
            up_sum[...] = jnp.zeros_like(up_sum)
            down_sum[...] = jnp.zeros_like(down_sum)
            wide[...] = jnp.zeros_like(wide)

        act, slope = gelu_parts(dot(hid[...], up[...]) + bias[...])
        low = act.astype(bf16)
        out[...] = dot(low, down[...])
        down_sum[...] += dot(low, gcl[...], 0, 0)
        grad_pre = dot(gcl[...], down[...], 1, 1) * slope
        grad_low = grad_pre.astype(bf16)
        wide[...] += jnp.sum(grad_low.astype(f32), axis=0, keepdims=True)
        up_sum[...] += dot(hid[...], grad_low, 0, 0)
        back[...] = dot(grad_low, up[...], 1, 1)

        @pl.when(step == blocks - 1)
        def _():
            line[...] = wide[...]
            if not paired:
                mine[0], mine[1] = up_sum[...], down_sum[...]
            for p in range(pairs if paired else 0):
                at = pl.multiple_of(info[18 + 2 * p] * rows_piece, rows_piece)
                far = pl.multiple_of(info[19 + 2 * p] * rows_piece, rows_piece)
                mine[p, :rows_piece, :] = up_sum[pl.ds(at, rows_piece), :]
                mine[p, rows_piece:, :] = down_sum[pl.ds(at, rows_piece), :]
                theirs[p, :rows_piece, :] = up_sum[pl.ds(far, rows_piece), :].astype(bf16)
                theirs[p, rows_piece:, :] = down_sum[pl.ds(far, rows_piece), :].astype(bf16)

    return kernel_call(
        body,
        blocks,
        [
            SCALARS,
            pl.BlockSpec((rows, width), lambda i: (i, 0)),
            pl.BlockSpec((rows, width), lambda i: (i, 0)),
            full((1, width)),
        ]
        + [full(p.shape) for p in pieces],
        [
            pl.BlockSpec((rows, width), lambda i: (i, 0)),
            pl.BlockSpec((rows, width), lambda i: (i, 0)),
            full(sums_mine),
            full(sums_theirs),
            full((1, width)),
        ],
        [
            shape((total, width), f32),
            shape((total, width), f32),
            shape(sums_mine, f32),
            shape(sums_theirs, bf16),
            shape((1, width), f32),
        ],
        [
            pltpu.VMEM((width, width), bf16),
            pltpu.VMEM((width, width), bf16),
            pltpu.VMEM((width, width), f32),
            pltpu.VMEM((width, width), f32),
            pltpu.VMEM((1, width), f32),
        ],
        12 * total * width * width,
        [info, hidden, grad, bias, *pieces],
    )


def routed_expert(info, buffers, slots, ups, downs, bias):
    pairs, _, units = bias.shape
    count, width = buffers[0].shape
    piece = width // (2 * pairs)
    every = pairs * units

    def body(info, b0, b1, s0, s1, *refs):
        ups, downs, bias = refs[:4], refs[4:8], refs[8]
        (ds, dk, us, uk, g0, g1, e0, e1, line, up, down, grad, gsum, esum, bs, ss) = refs[9:]
        step = pl.program_id(0)

        @pl.when(step == 0)
        def _():
            for r in range(pairs):
                for j in range(2):
                    at = pl.multiple_of(info[18 + 2 * r + j] * piece, piece)
                    up[pl.ds(at, piece), :] = ups[r][j]
                at = pl.multiple_of(info[14 + r] * units, units)
                down[pl.ds(at, units), :] = downs[r][...]
            bs[:count, :], bs[count:, :] = b0[...], b1[...]
            ss[:count, :], ss[count:, :] = s0[...], s1[...]
            gsum[...] = jnp.zeros_like(gsum)
            esum[...] = jnp.zeros_like(esum)

        block = info[14 + step]
        at = pl.multiple_of(block * units, 128)
        w_up = up[:, pl.ds(at, units)]
        w_down = down[pl.ds(at, units), :]
        bias_now = bias[pl.ds(block, 1)][0]
        act, slope = gelu_parts(dot(bs[...], w_up) + bias_now)
        low = act.astype(bf16)
        esum[...] += dot(low, w_down)
        rdown = dot(low, ss[...], 0, 0)
        grad_low = (dot(ss[...], w_down, 1, 1) * slope).astype(bf16)
        total = jnp.sum(grad_low.astype(f32), axis=0, keepdims=True)
        grad[...] = dot(bs[...], grad_low, 0, 0)
        gsum[...] += dot(grad_low, w_up, 1, 1)
        line[pl.ds(block, 1)] = total[None]
        for r in range(pairs):
            for j in range(2):
                row = pl.multiple_of(info[18 + 2 * r + j] * piece, piece)
                value = grad[pl.ds(row, piece), :]
                if r % 2 == 1:
                    us[r // 2, j * piece : (j + 1) * piece, pl.ds(at, units)] = value.astype(bf16)
                else:
                    uk[r // 2, j * piece : (j + 1) * piece, pl.ds(at, units)] = value

            @pl.when(step == r)
            def _():
                if r % 2 == 1:
                    ds[r // 2] = rdown.astype(bf16)
                else:
                    dk[r // 2] = rdown

        @pl.when(step == pairs - 1)
        def _():
            g0[...] = gsum[:count, :]
            g1[...] = gsum[count:, :].astype(bf16)
            e0[...] = esum[:count, :]
            e1[...] = esum[count:, :].astype(bf16)

    outs = [
        shape((2, units, width), bf16),
        shape((2, units, width), f32),
        shape((2, 2 * piece, every), bf16),
        shape((2, 2 * piece, every), f32),
        shape((count, width), f32),
        shape((count, width), bf16),
        shape((count, width), f32),
        shape((count, width), bf16),
        shape((pairs, 1, units), f32),
    ]
    operands = [*buffers, *slots, *ups, *downs, bias]
    return kernel_call(
        body,
        pairs,
        [SCALARS] + [full(o.shape) for o in operands],
        [full(o.shape) for o in outs],
        outs,
        [
            pltpu.VMEM((width, every), bf16),
            pltpu.VMEM((every, width), bf16),
            pltpu.VMEM((width, units), f32),
            pltpu.VMEM((2 * count, width), f32),
            pltpu.VMEM((2 * count, width), f32),
            pltpu.VMEM((2 * count, width), bf16),
            pltpu.VMEM((2 * count, width), bf16),
        ],
        24 * count * width * every,
        [info, *operands],
    )


def tail_grads(info, tokens, hidden, grads, attended, grad_attn, qkv):
    total, width = hidden.shape
    wide = grads.shape[1]
    blocks, rows, _ = tokens.shape
    cols = width // blocks
    piece = width // 8

    def body(info, tok, hid, gr, att, ga, qkv, out, send, keep, sums, lines, proj):
        out_qkv = dot(hid[...], gr[...], 0, 0).astype(bf16)
        for m in range(blocks):
            these = slice(m * rows, (m + 1) * rows)
            grad = dot(gr[these, :], qkv[...], 1, 1)
            if m % 2 == 1:
                send[m // 2] = grad.astype(bf16)
            else:
                keep[m // 2] = grad
            normed, _ = norm_parts(tok[m].astype(f32))
            sums[m : m + 1, :] = jnp.sum(grad, axis=0, keepdims=True)
            sums[blocks + m : blocks + m + 1, :] = jnp.sum(grad * normed, axis=0, keepdims=True)
        lines[:, :wide] = jnp.sum(gr[...].astype(f32), axis=0, keepdims=True)
        lines[:, wide:] = jnp.sum(ga[...].astype(f32), axis=0, keepdims=True)
        own = ga[:, :cols]
        for k in range(1, blocks):
            own = jnp.where(info[8] == k, ga[:, k * cols : (k + 1) * cols], own)
        proj[...] = dot(att[...], own, 0, 0)
        for d in range(8):
            out[d, :, :wide] = out_qkv[d * piece : (d + 1) * piece, :]
            at = ((d // 2) ^ info[8]) * cols + (d % 2) * piece
            at = pl.multiple_of(at, piece)
            out[d, :, wide:] = proj[pl.ds(at, piece), :].astype(bf16)

    return kernel_call(
        body,
        1,
        [SCALARS, pl.BlockSpec((blocks, rows, width), lambda i: (0, 0, 0))]
        + [full((total, width)), full((total, wide)), full((total, width))]
        + [full((total, width)), full((width, wide))],
        [
            full((8, piece, width)),
            full((2, rows, width)),
            full((2, rows, width)),
            full((2 * blocks, width)),
            full((1, wide + width)),
        ],
        [
            shape((8, piece, width), bf16),
            shape((2, rows, width), bf16),
            shape((2, rows, width), f32),
            shape((2 * blocks, width), f32),
            shape((1, wide + width), f32),
        ],
        [pltpu.VMEM((width, cols), f32)],
        2 * total * width * (2 * wide + cols),
        [info, tokens, hidden, grads, attended, grad_attn, qkv],
    )


def in_order(relative, position):
    return jnp.stack(
        [
            lax.dynamic_index_in_dim(relative, position ^ a, 0, keepdims=False)
            for a in range(relative.shape[0])
        ]
    )


def body(
    tokens,
    conditioning,
    routes,
    gate_weights,
    image_counts,
    image_lengths,
    cotangent,
    qkv_weight,
    qv_bias,
    proj_weight,
    proj_bias,
    ada_weight,
    ada_bias,
    up_weight,
    up_bias,
    down_weight,
    down_bias,
    routed_up,
    routed_upbias,
    routed_down,
    routed_downbias,
):
    group = lax.axis_size("expert")
    copies = lax.axis_size("dp")
    position = lax.axis_index("expert")
    place = lax.axis_index("dp")
    rows, width = tokens.shape
    group_rows = group * rows
    heads_own = HEADS // group
    cols_own = heads_own * HEAD_DIM
    d_rows = qkv_weight.shape[0]
    f_rows = down_weight.shape[0]
    f_own = f_rows // group
    hidden_units = f_rows * copies
    quarter = hidden_units // group
    side = lax.rem(place // 2, 2)
    first_side = side == 0
    pairs_count = copies // 2
    keep = f_rows * 2 // 3
    send = f_rows - keep
    half_units = hidden_units // 2

    def my_units(value):
        one, two = [], []
        for p in range(pairs_count):
            at, to = (d * f_rows for d in pair_places(p))
            one += [value[..., at : at + keep], value[..., to : to + send]]
            two += [value[..., to + send : to + f_rows], value[..., at + keep : at + f_rows]]
        one, two = jnp.concatenate(one, axis=-1), jnp.concatenate(two, axis=-1)
        return jnp.where(first_side, one, two), jnp.where(first_side, two, one)

    def from_units(mine, theirs):
        one = jnp.where(first_side, mine, theirs)
        two = jnp.where(first_side, theirs, mine)
        out = [None] * copies
        for p in range(pairs_count):
            at = f_rows * p
            first, second = pair_places(p)
            out[first] = [one[..., at : at + keep], two[..., at + keep : at + f_rows]]
            out[second] = [one[..., at + keep : at + f_rows], two[..., at : at + keep]]
        out = sum(out, [])
        return jnp.concatenate(out, axis=-1)

    bias_list = [up_bias, routed_upbias[0], qv_bias, proj_bias, down_bias, routed_downbias[0]]
    if copies == 8:
        first_share, third_share, rup_mine, rup_theirs, rdown_mine, rdown_theirs = prepare(
            jnp.stack([position] * 9 + [side]).astype(jnp.int32),
            proj_weight,
            qkv_weight,
            [b[None] for b in bias_list],
            up_weight,
            down_weight,
            routed_up[0],
            routed_down[0],
            keep,
            group,
        )
    else:
        qkv_share = lax.dynamic_index_in_dim(
            qkv_weight.reshape(d_rows, 3, group, cols_own), position, 2, keepdims=False
        ).reshape(d_rows, 3 * cols_own)
        first_share = qkv_share
        up_share = lax.dynamic_index_in_dim(
            up_weight.reshape(d_rows, copies, group, f_own), position, 2, keepdims=False
        ).reshape(d_rows, quarter)
        down_share = lax.dynamic_slice_in_dim(down_weight, position * f_own, f_own, axis=0)
        third_share = jnp.concatenate([up_share, down_share, proj_weight], axis=0)
        rup_mine, rup_theirs = my_units(routed_up[0])
        rdown_mine = lax.dynamic_slice_in_dim(routed_down[0], side * send, keep, axis=0)
        rdown_theirs = lax.dynamic_slice_in_dim(routed_down[0], (1 - side) * keep, send, axis=0)
    rup_got = pair_swap(rup_theirs)
    rdown_got = pair_swap(rdown_theirs)
    first, order = ring_gather(first_share)
    bias_three = jnp.zeros((1, 3 * cols_own), f32)
    if copies > 8:
        upb, rupb, qvb, projb, downb, rdownb = (
            lax.all_gather(b, "dp", axis=0, tiled=True).astype(f32) for b in bias_list
        )
        upb_own = lax.dynamic_index_in_dim(
            upb.reshape(copies, group, f_own), position, 1, keepdims=False
        ).reshape(quarter)
        bias_lines = jnp.stack([upb_own, projb, downb, rdownb])
        rupb_own = my_units(rupb)[0].reshape(4, 1, half_units // 4)
        bias_three = jnp.concatenate(
            [
                lax.dynamic_slice_in_dim(qvb, position * cols_own, cols_own),
                jnp.zeros((cols_own,), f32),
                lax.dynamic_slice_in_dim(qvb, width + position * cols_own, cols_own),
            ]
        )[None]

    pair_steps = jnp.arange(4, dtype=jnp.int32)
    if copies == 8:
        third = spread(tied(jnp.stack([third_share, pair_swap(third_share)]), *first[3:5]))
        downs = spread(tied(jnp.concatenate([rdown_mine, rdown_got]), third[2]))
        ups = spread(tied(jnp.stack([rup_mine, rup_got]), downs[2]))
        pair_now = (place >> 2) * 2 + (place & 1)
        unit_blocks = pair_now ^ pair_steps
        masks = jnp.array([0, 2, 1, 3, 4, 6, 5, 7], jnp.int32)
        row_blocks = place ^ masks
    else:
        groups = side_groups(copies)
        whole = lax.all_gather(third_share, "dp", axis=0)
        third = jnp.concatenate(
            [
                whole[:, :d_rows].reshape(8, -1, width),
                whole[:, d_rows : d_rows + f_own].reshape(8, -1, width),
                whole[:, d_rows + f_own :].reshape(8, -1, width),
            ],
            axis=1,
        ).reshape(4, 2, -1, width)
        sided = jnp.where(
            first_side, jnp.stack([rup_mine, rup_got]), jnp.stack([rup_got, rup_mine])
        )
        ups = lax.all_gather(sided, "dp", axis=0, axis_index_groups=groups)
        ups = ups.reshape(pairs_count // 2, 2, 2, d_rows, half_units).transpose(0, 2, 1, 3, 4)
        ups = ups.reshape(4, 2, width // 8, half_units)
        downs = lax.all_gather(
            jnp.concatenate([rdown_mine, rdown_got]), "dp", axis=0, axis_index_groups=groups
        ).reshape(4, half_units // 4, width)
        third, ups, downs = ([v[r] for r in range(4)] for v in (third, ups, downs))
        unit_blocks = pair_steps
        row_blocks = jnp.arange(8, dtype=jnp.int32)

    def by_side(whole):
        out = whole.reshape(pairs_count // 2, 2, 2, d_rows, -1).transpose(1, 0, 2, 3, 4)
        return out.reshape(2, 4, width // 8, -1)

    both = gather_group(jnp.concatenate([tokens, cotangent], axis=1))
    pairs = gather_group(jnp.concatenate([routes.astype(f32).T, gate_weights.T], axis=0))

    lengths = image_lengths[0]
    image_total = image_counts[0]
    slots = lengths.shape[0]
    slot_ids = jnp.arange(slots, dtype=jnp.int32)
    starts = jnp.sum(
        jnp.where(slot_ids[None, :] < slot_ids[:, None], lengths[None, :], 0), axis=1
    )
    live = (slot_ids >= 1) & (slot_ids < image_total)
    block_ids = position ^ jnp.arange(group, dtype=jnp.int32)
    segment = jnp.sum(
        (live[None, :] & (starts[None, :] <= (block_ids * rows)[:, None])).astype(jnp.int32),
        axis=1,
    )
    block_hot = segment[:, None] == slot_ids[None, :]

    info = jnp.concatenate(
        [
            order,
            jnp.stack([position, side]),
            segment,
            unit_blocks,
            row_blocks,
            jnp.zeros((6,), jnp.int32),
        ]
    ).astype(jnp.int32)

    cond_value = conditioning[0].astype(f32)
    cond_act = jax.nn.silu(cond_value).astype(bf16)
    act_parts = lax.all_to_all(
        cond_act.reshape(slots, copies, d_rows).transpose(1, 0, 2),
        "dp",
        split_axis=0,
        concat_axis=0,
        tiled=True,
    ).reshape(copies * slots, d_rows)
    mod_width = ada_weight.shape[1]
    mod_own = mod_width // group
    bias_line = lax.dynamic_update_slice(
        jnp.zeros((mod_width,), f32), ada_bias.astype(f32), (place * ada_bias.shape[0],)
    )
    ada_own = lax.dynamic_slice_in_dim(ada_weight, position * mod_own, mod_own, axis=1)
    bias_own = lax.dynamic_slice_in_dim(bias_line, position * mod_own, mod_own)
    mod_parts = (mm("sd,dm->sm", tied(act_parts, *first[1:3]), ada_own) + bias_own[None]).reshape(
        copies, slots, mod_own
    )
    mod_got = lax.all_to_all(mod_parts, "dp", split_axis=0, concat_axis=0, tiled=True)
    mod_sum = jnp.sum(tied(mod_got, *first[3:5]), axis=0)
    mod_across = tied(swap(mod_sum, 2), *first[5:7])
    mod_beside = swap(jnp.stack([mod_sum, mod_across]), 1)
    mod_group = jnp.stack([mod_sum, mod_beside[0], mod_across, mod_beside[1]])
    modulation = in_order(mod_group, position).transpose(1, 0, 2).reshape(slots, mod_width)
    per_block = jnp.sum(
        jnp.where(block_hot[:, :, None], modulation[None, :, :], 0.0), axis=1
    )
    mods = jnp.pad(per_block.reshape(group, 6, width), ((0, 0), (0, 2), (0, 0)))
    shift_a, scale_a, gate_a, shift_b, scale_b, gate_b = (mods[0, i : i + 1] for i in range(6))

    (
        hidden_a,
        projected,
        qkv_own,
        table,
        gates,
        grad_comb_low,
        slot_own,
        sums_f,
        lines_got,
        units_got,
    ) = front(
        info,
        both,
        mods,
        bias_three,
        pairs,
        first,
        width // 8,
        cols_own,
        keep if copies == 8 else 0,
    )
    if copies == 8:
        bias_lines, rupb_own = lines_got, units_got
    upb_line, projb_line, downb_line, rdownb_line = (bias_lines[i : i + 1] for i in range(4))
    slot_got = pair_swap(slot_own)
    heads_0 = attention(info, tied(projected, third[1], third[2]), group, cols_own)
    heads_2 = swap(heads_0, 2)
    heads_1 = swap(heads_0, 1)
    heads_3 = swap(heads_2, 1)
    hidden_b, attended, buffer_own, attn_out, residual_mid, proj_own = middle(
        info,
        both,
        mods,
        (heads_0, heads_1, heads_2, heads_3),
        third,
        projb_line,
        tied(table, downs[1], downs[2]),
        width // 8,
    )
    buffer_got = pair_swap(buffer_own)

    shared_parts, shared_back, shared_mine, shared_theirs, upbias_line = shared_expert(
        info, tied(hidden_b, ups[1]), grad_comb_low, upb_line, third, width // 8, group, copies == 8
    )
    if copies != 8:
        sided = jnp.concatenate([by_side(shared_mine[0]), by_side(shared_mine[1])], axis=2)
        shared_mine, shared_theirs = (
            lax.dynamic_index_in_dim(sided, which, 0, keepdims=False) for which in (side, 1 - side)
        )
        shared_theirs = shared_theirs.astype(bf16)
    shared_sums = shared_mine + pair_swap(shared_theirs).astype(f32)
    (
        down_send,
        down_keep,
        up_send,
        up_keep,
        back_own,
        back_theirs,
        out_own,
        out_theirs,
        units_sum,
    ) = routed_expert(
        info,
        (tied(buffer_own, shared_theirs), buffer_got),
        (slot_own, slot_got),
        ups,
        downs,
        rupb_own,
    )
    units_sum = units_sum.reshape(pairs_count, f_rows)
    blank = jnp.zeros((pairs_count, f_rows), f32)
    units_one = jnp.where(first_side, units_sum, blank)
    units_two = jnp.where(first_side, blank, units_sum)
    units_by_place = jnp.stack(
        [
            jnp.concatenate([units_one[:, :keep], units_two[:, keep:]], axis=1),
            jnp.concatenate([units_one[:, keep:], units_two[:, :keep]], axis=1),
        ]
    )
    units_by_place = units_by_place.reshape(2, pairs_count // 2, 2, f_rows).transpose(1, 0, 2, 3)
    expert_line = jnp.concatenate(
        [
            units_by_place.reshape(copies, f_rows),
            upbias_line.reshape(copies, f_own),
            sums_f[0].reshape(copies, d_rows),
            sums_f[1].reshape(copies, d_rows),
        ],
        axis=1,
    )
    zero_line = jnp.zeros((1, width), f32)
    rows_send, rows_keep, _ = to_rows(
        back_own,
        pair_swap(back_theirs),
        zero_line,
        table,
        jnp.ones((group, rows, 1), f32),
        shared_back,
        both,
        zero_line,
    )
    back_near, back_got = reduce_group(rows_send, rows_keep)
    grad_mid, grad_attn_own, sums_b = middle_back(
        back_near, back_got, residual_mid, attn_out, cotangent, mods
    )
    attn_2 = swap(grad_attn_own, 2)
    grad_attn = jnp.concatenate(
        [grad_attn_own, swap(grad_attn_own, 1), attn_2, swap(attn_2, 1)]
    )

    grad_projected = attention_back(info, projected, grad_attn, proj_own, group, cols_own)
    last_parts, back_send, back_keep, sums_a, lines = tail_grads(
        info, both, hidden_a, grad_projected, attended, grad_attn, qkv_own
    )
    last_sums = jnp.sum(
        lax.all_to_all(
            last_parts.reshape(copies, d_rows, width), "dp", split_axis=0, concat_axis=0, tiled=True
        ).astype(f32),
        axis=0,
    )
    if copies == 8:
        end = (last_parts,)
        rdown_sums, down_got = collect(down_send, down_keep, (), (grad_attn_own,), end)
        rup_sums, up_got = collect(up_send, up_keep, (down_got,), (grad_projected,), end)
        shared_rows, _ = collect(
            jnp.stack([shared_sums[1], shared_sums[3]]).astype(bf16),
            (shared_sums[0], shared_sums[2]),
            (up_got,),
            (grad_projected,),
            end,
        )
    else:

        def scatter(value, each):
            return lax.psum_scatter(
                value.reshape(pairs_count, each, -1).astype(bf16),
                "dp",
                scatter_dimension=0,
                axis_index_groups=side_groups(copies),
                tiled=False,
            )

        def whole_of(send, keep):
            send = send.astype(f32)
            return jnp.stack([keep[0], send[0], keep[1], send[1]])

        shared_rows = jnp.concatenate(
            [scatter(shared_sums[:, : width // 8], d_rows), scatter(shared_sums[:, width // 8 :], f_own)]
        )
        rdown_sums = scatter(whole_of(down_send, down_keep), f_rows)
        sided = by_side(whole_of(up_send, up_keep))
        rup_sums = jnp.concatenate(
            [
                scatter(lax.dynamic_index_in_dim(sided, which, 0, keepdims=False), d_rows)
                for which in (side, 1 - side)
            ]
        )

    lines = lines[0]
    qv_line = lax.dynamic_update_slice(
        jnp.zeros((2 * width,), f32), lines[:cols_own], (position * cols_own,)
    )
    qv_line = lax.dynamic_update_slice(
        qv_line, lines[2 * cols_own : 3 * cols_own], (width + position * cols_own,)
    ).reshape(copies, -1)
    pb_line = lines[3 * cols_own :].reshape(copies, d_rows)
    count_own = sums_f[2, 0]
    count_high = jnp.floor(count_own / 128.0)
    count_line = jnp.broadcast_to(
        jnp.stack([count_high, count_own - 128.0 * count_high])[None], (copies, 2)
    )
    line = jnp.concatenate([expert_line, qv_line, pb_line, count_line], axis=1)
    line_width = -(-line.shape[1] // (slots * 128)) * 128
    line = jnp.pad(line, ((0, 0), (0, slots * line_width - line.shape[1]))).reshape(
        copies, slots, line_width
    )

    rows_send, rows_keep, sums_out = to_rows(
        tied(out_own, last_parts),
        pair_swap(tied(out_theirs, grad_attn_own)),
        rdownb_line,
        table,
        gates,
        shared_parts,
        both,
        downb_line,
    )
    combined_near, combined_got = reduce_group(rows_send, rows_keep)
    combined = combined_near + combined_got.astype(f32) + downb_line
    output = (residual_mid + gate_b * combined).astype(bf16)

    block_of = block_hot.astype(f32)
    sums_all = jnp.concatenate(
        [
            sums_a[:group],
            sums_a[group:],
            jnp.pad(sums_b[:3].reshape(1, 3 * width), ((0, group - 1), (0, 0))),
            sums_out.reshape(group, width),
        ],
        axis=1,
    )
    slot_sums = jnp.sum(block_of[:, :, None] * sums_all[:, None, :], axis=0)
    slot_sums = slot_sums + swap(slot_sums, 1)
    slot_sums = slot_sums + swap(slot_sums, 2)
    grad_modulation = slot_sums.astype(bf16)
    mod_got = lax.all_to_all(
        jnp.concatenate(
            [
                jnp.broadcast_to(grad_modulation[None], (copies, slots, mod_width)),
                line.astype(bf16),
            ],
            axis=2,
        ),
        "dp",
        split_axis=0,
        concat_axis=0,
        tiled=True,
    )
    mod_all = mod_got[:, :, :mod_width].reshape(copies * slots, mod_width)
    line_sums = jnp.sum(mod_got[:, :, mod_width:].astype(f32), axis=0).reshape(-1)
    ada_grad = mm("sd,sm->dm", act_parts, mod_all)
    adabias_grad = jnp.sum(
        lax.dynamic_slice_in_dim(
            mod_all, place * ada_bias.shape[0], ada_bias.shape[0], axis=1
        ).astype(f32),
        axis=0,
    )
    cond_parts = mm("sm,dm->sd", mod_all, ada_weight).reshape(copies, slots, d_rows)
    grad_cond_act = (
        lax.all_to_all(cond_parts, "dp", split_axis=0, concat_axis=0, tiled=True)
        .transpose(1, 0, 2)
        .reshape(slots, width)
    )
    sigmoid_cond = jax.nn.sigmoid(cond_value)
    conditioning_grad = (grad_cond_act * sigmoid_cond * (1.0 + cond_value * (1.0 - sigmoid_cond)))[
        None
    ]

    near_a, got_a = reduce_group(back_send, back_keep)
    grad_hidden_a = near_a + got_a.astype(f32)
    normed_a, inv_std_a = norm_parts(tokens.astype(f32))
    tokens_grad = grad_mid + norm_back(grad_hidden_a * (1.0 + scale_a), normed_a, inv_std_a)

    rup_got = pair_swap(rup_sums[d_rows:].astype(bf16))
    rdown_got = pair_swap(rdown_sums[keep:].astype(bf16))
    shared_all = gather_group(shared_rows.astype(bf16))
    last_all = gather_group(last_sums.astype(bf16))
    if copies == 8:
        rup_rows, rdown_rows = routed_rows(info, rup_sums, rup_got, rdown_sums, rdown_got, keep)
        up_rows, down_rows, qkv_rows, proj_rows = group_rows_out(
            info, shared_all, last_all, d_rows, f_rows
        )
    else:
        rup_rows = from_units(rup_sums[:d_rows].astype(f32), rup_got.astype(f32))
        kept, back = rdown_sums[:keep].astype(f32), rdown_got.astype(f32)
        rdown_rows = jnp.where(
            first_side, jnp.concatenate([kept, back]), jnp.concatenate([back, kept])
        )
        shared_all, last_all = (
            in_order(v, position).astype(f32) for v in (shared_all, last_all)
        )
        up_rows = (
            shared_all[:, :d_rows]
            .reshape(group, d_rows, copies, f_own)
            .transpose(1, 2, 0, 3)
            .reshape(d_rows, hidden_units)
        )
        down_rows = shared_all[:, d_rows:].reshape(f_rows, width)
        qkv_rows = (
            last_all[:, :, : 3 * cols_own]
            .reshape(group, d_rows, 3, cols_own)
            .transpose(1, 2, 0, 3)
            .reshape(d_rows, 3 * width)
        )
        proj_rows = last_all[:, :, 3 * cols_own :].transpose(1, 0, 2).reshape(d_rows, width)
    cuts = [f_rows, f_own, d_rows, d_rows, 2 * width // copies, d_rows, 2]
    at = [sum(cuts[:i]) for i in range(len(cuts))]
    rupbias_row, upbias_sum, rdownbias_row, downbias_row, qvbias_sum, projbias_row, counts = (
        line_sums[o : o + n] for o, n in zip(at, cuts)
    )
    small = in_order(
        gather_group(jnp.concatenate([upbias_sum, qvbias_sum, counts])[None]), position
    )[:, 0]
    upbias_rows = small[:, :f_own].reshape(f_rows)
    qvbias_rows = jnp.sum(small[:, f_own:-2], axis=0)
    expert_counts = (128.0 * small[:, -2] + small[:, -1]).astype(jnp.int32)

    return (
        output,
        tokens_grad,
        conditioning_grad,
        qkv_rows,
        qvbias_rows,
        proj_rows,
        projbias_row,
        ada_grad,
        adabias_grad,
        up_rows,
        upbias_rows,
        down_rows,
        downbias_row,
        rup_rows[None],
        rupbias_row[None],
        rdown_rows[None],
        rdownbias_row[None],
        expert_counts,
    )


def solution(mesh):
    in_specs = (
        P(("dp", "expert"), None),
        P("dp", None, None),
        P(("dp", "expert"), None),
        P(("dp", "expert"), None),
        P("dp"),
        P("dp", None),
        P(("dp", "expert"), None),
        P("dp", None),
        P("dp"),
        P("dp", None),
        P("dp"),
        P("dp", None),
        P("dp"),
        P("dp", None),
        P("dp"),
        P("dp", None),
        P("dp"),
        P("expert", "dp", None),
        P("expert", "dp"),
        P("expert", "dp", None),
        P("expert", "dp"),
    )
    out_specs = (
        P(("dp", "expert"), None),
        P(("dp", "expert"), None),
        P("dp", None, None),
        P("dp", None),
        P("dp"),
        P("dp", None),
        P("dp"),
        P("dp", None),
        P("dp"),
        P("dp", None),
        P("dp"),
        P("dp", None),
        P("dp"),
        P("expert", "dp", None),
        P("expert", "dp"),
        P("expert", "dp", None),
        P("expert", "dp"),
        P(),
    )
    return jax.shard_map(body, mesh=mesh, in_specs=in_specs, out_specs=out_specs, check_vma=False)
```

```python
import jax
import jax.numpy as jnp
from jax import lax
from jax.experimental import pallas as pl
from jax.experimental.pallas import tpu as pltpu
from jax.sharding import PartitionSpec as P

HEADS = 12
HEAD_DIM = 64
CAP = 128

epsilon = 1e-06
gelu_root = 0.7978845608028654
gelu_cubic = 0.044715

bf16 = jnp.bfloat16
f32 = jnp.float32


def norm_parts(values):
    centered = values - jnp.mean(values, axis=-1, keepdims=True)
    inv_std = lax.rsqrt(jnp.mean(centered * centered, axis=-1, keepdims=True) + epsilon)
    return (centered * inv_std, inv_std)


def norm_back(grad_normed, normed, inv_std):
    mean_grad = jnp.mean(grad_normed, axis=-1, keepdims=True)
    mean_cross = jnp.mean(grad_normed * normed, axis=-1, keepdims=True)
    return inv_std * (grad_normed - mean_grad - normed * mean_cross)


def gelu_parts(values):
    square = values * values
    half = 0.5 + 0.5 * jnp.tanh(values * (gelu_root + gelu_root * gelu_cubic * square))
    activation = values * half
    slope = half + activation * (1.0 - half) * (
        2.0 * gelu_root + 6.0 * gelu_root * gelu_cubic * square
    )
    return (activation, slope)


def mm(spec, a, b):
    return jnp.einsum(spec, a, b, preferred_element_type=f32)


def swap(value, mask):
    size = lax.axis_size("expert")
    return lax.ppermute(value, "expert", [(i, i ^ mask) for i in range(size)])


def gather_group(value):
    across = swap(value, 2)
    beside = swap(jnp.stack([value, across]), 1)
    return jnp.stack([value, beside[0], across, beside[1]])


def reduce_group(send, keep):
    beside = swap(send, 1).astype(f32)
    own = keep[0] + beside[0]
    other = (keep[1] + beside[1]).astype(bf16)
    return own, swap(other, 2)


def dp_swap(value, mask):
    copies = lax.axis_size("dp")
    return lax.ppermute(value, "dp", [(i, i ^ mask) for i in range(copies)])


def pair_swap(value):
    return dp_swap(value, 2)


def side_groups(copies):
    return [[i for i in range(copies) if (i >> 1) % 2 == side] for side in range(2)]


def pair_places(p):
    first = ((p >> 1) << 2) | (p & 1)
    return first, first + 2


def spread(value, *before):
    far = dp_swap(value, 4)
    return [value, dp_swap(tied(value, *before), 1), far, dp_swap(far, 1)]


def collect(send, keep, start, middle, end):
    got = dp_swap(tied(send, *start), 1)
    wide = tied(got, *middle).astype(f32)
    far = dp_swap((keep[1] + wide[1]).astype(bf16), 4)
    return keep[0] + wide[0] + tied(far, *end).astype(f32), got


def tied(value, *others):
    return lax.optimization_barrier((value, *others))[0]


def ring_place(at, copies):
    at = lax.rem(at + copies, copies)
    return jnp.where(at < copies // 2, 2 * at, 2 * (copies - 1 - at) + 1)


def ring_gather(share):
    copies = lax.axis_size("dp")
    if copies > 8:
        whole = lax.all_gather(share, "dp", axis=0)
        whole = whole.reshape((8, copies // 8 * share.shape[0]) + share.shape[1:])
        return [whole[k] for k in range(8)], jnp.arange(8, dtype=jnp.int32)
    half = copies // 2
    ring = [2 * i for i in range(half)] + [2 * i + 1 for i in reversed(range(half))]
    place = lax.axis_index("dp")
    position = jnp.where(lax.rem(place, 2) == 0, place // 2, copies - 1 - place // 2)

    def hop(value, way):
        return lax.ppermute(
            value, "dp", [(ring[i], ring[(i + way) % copies]) for i in range(copies)]
        )

    pieces, offsets = [share], [0]
    right = left = share
    for step in range(1, half + 1):
        right = hop(right, 1)
        pieces.append(right)
        offsets.append(-step)
        if step < half:
            left = hop(left, -1)
            pieces.append(left)
            offsets.append(step)
    return pieces, ring_place(position + jnp.array(offsets, jnp.int32), copies)


def dot(a, b, left=1, right=0):
    return lax.dot_general(
        a, b, (((left,), (right,)), ((), ())), preferred_element_type=f32
    )


def full(shape):
    return pl.BlockSpec(shape, lambda i: (0,) * len(shape), pipeline_mode=pl.Buffered(1))


SCALARS = pl.BlockSpec(memory_space=pltpu.SMEM)


def kernel_call(body, grid, in_specs, out_specs, out_shape, scratch, flops, operands):
    out_bytes = sum(int(o.size) * o.dtype.itemsize for o in out_shape)
    in_bytes = sum(int(o.size) * o.dtype.itemsize for o in operands)
    return pl.pallas_call(
        body,
        grid=(grid,),
        in_specs=in_specs,
        out_specs=out_specs,
        out_shape=out_shape,
        scratch_shapes=scratch,
        compiler_params=pltpu.CompilerParams(vmem_limit_bytes=56 * 2**20),
        cost_estimate=pl.CostEstimate(
            flops=int(flops), bytes_accessed=out_bytes + in_bytes, transcendentals=0
        ),
    )(*operands)


def shape(dims, dtype):
    return jax.ShapeDtypeStruct(dims, dtype)


def prepare(info, proj, qkv, biases, up, down, rup, rdown, keep, group):
    d_rows, width = proj.shape
    cols = width // group
    f_rows = down.shape[0]
    f_own = f_rows // group
    count = up.shape[1] // f_rows
    wide = 3 * cols
    chunks = rup.shape[1] // 2 // width

    def body(info, proj, qkv, *refs):
        biases, (up, down, rup, rdown, first, third, mine, theirs) = (
            refs[: len(biases_in)],
            refs[len(biases_in) :],
        )
        third[d_rows + f_own :, :] = proj[...]
        lines = [
            jnp.concatenate([b[...].astype(f32), jnp.zeros((1, wide - b.shape[1]), f32)], axis=1)
            for b in biases[1:]
        ]
        for p in range(group):

            @pl.when(info[8] == p)
            def _():
                own = slice(p * f_own, (p + 1) * f_own)
                first[:d_rows, :] = jnp.concatenate(
                    [qkv[:, i * width + p * cols : i * width + (p + 1) * cols] for i in range(3)],
                    axis=1,
                )
                line = jnp.concatenate(
                    [biases[0][:, own].astype(f32), jnp.zeros((1, wide - f_own), f32)], axis=1
                )
                first[d_rows:, :] = jnp.concatenate(
                    [line] + lines + [jnp.zeros((15 - len(lines), wide), f32)], axis=0
                ).astype(bf16)
                third[:d_rows, :] = jnp.concatenate(
                    [
                        up[:, d * f_rows + p * f_own : d * f_rows + (p + 1) * f_own]
                        for d in range(count)
                    ],
                    axis=1,
                )
                third[d_rows : d_rows + f_own, :] = down[own, :]

        one, two = [], []
        for p in range(count // 2):
            at, to = (d * f_rows for d in pair_places(p))
            one += [(at, at + keep), (to, to + f_rows - keep)]
            two += [(to + f_rows - keep, to + f_rows), (at + keep, at + f_rows)]
        for side in range(2):

            @pl.when(info[9] == side)
            def _():
                own, other = (one, two) if side == 0 else (two, one)
                for ref, parts in ((mine, own), (theirs, other)):
                    line = jnp.concatenate([rup[:, low:high] for low, high in parts], axis=1)
                    for c in range(line.shape[1] // width):
                        ref[c * d_rows : (c + 1) * d_rows, :] = line[:, c * width : (c + 1) * width]
                start = side * (f_rows - keep)
                mine[chunks * d_rows :, :] = rdown[start : start + keep, :]
                start = (1 - side) * keep
                theirs[chunks * d_rows :, :] = rdown[start : start + f_rows - keep, :]

    biases_in = biases
    operands = [proj, qkv, *biases, up, down, rup, rdown]
    outs = [
        shape((d_rows + 16, wide), bf16),
        shape((2 * d_rows + f_own, width), bf16),
        shape((chunks * d_rows + keep, width), bf16),
        shape((chunks * d_rows + f_rows - keep, width), bf16),
    ]
    return kernel_call(
        body,
        1,
        [SCALARS] + [full(o.shape) for o in operands],
        [full(o.shape) for o in outs],
        outs,
        [],
        0,
        [info, *operands],
    )


def middle_back(own, got, middle_rows, attn_out, cotangent, mods):
    rows, width = own.shape

    def body(own, got, mid, out, cot, mod, grad_mid, grad_attn, sums):
        grad = own[...] + got[...].astype(f32)
        normed, inv_std = norm_parts(mid[...])
        value = cot[...].astype(f32) + norm_back(
            grad * (1.0 + mod[0, 4:5, :]), normed, inv_std
        )
        grad_mid[...] = value
        grad_attn[...] = (mod[0, 2:3, :] * value).astype(bf16)
        sums[0:1, :] = jnp.sum(value * out[...], axis=0, keepdims=True)
        sums[1:2, :] = jnp.sum(grad, axis=0, keepdims=True)
        sums[2:3, :] = jnp.sum(grad * normed, axis=0, keepdims=True)
        sums[3:, :] = jnp.zeros((5, width), f32)

    operands = [own, got, middle_rows, attn_out, cotangent]
    outs = [shape((rows, width), f32), shape((rows, width), bf16), shape((8, width), f32)]
    return kernel_call(
        body,
        1,
        [full(o.shape) for o in operands] + [pl.BlockSpec((1, 8, width), lambda i: (0, 0, 0))],
        [full(o.shape) for o in outs],
        outs,
        [],
        0,
        [*operands, mods],
    )


def routed_rows(info, up_own, up_got, down_own, down_got, keep):
    d_rows, half = up_got.shape
    f_rows = down_own.shape[0]
    width = down_own.shape[1]
    pairs = half // f_rows

    def body(info, uo, ug, do, dg, up, down):
        for side in range(2):

            @pl.when(info[9] == side)
            def _():
                first, second = (0, 1) if side == 0 else (1, 0)
                values = (uo[:d_rows, :], ug[...].astype(f32))
                for p in range(pairs):
                    at, to = (d * f_rows for d in pair_places(p))
                    for whose, low, high, frm in (
                        (first, at, at + keep, 0),
                        (first, to, to + f_rows - keep, keep),
                        (second, to + f_rows - keep, to + f_rows, 0),
                        (second, at + keep, at + f_rows, keep),
                    ):
                        base = p * f_rows + frm
                        up[:, low:high] = values[whose][:, base : base + high - low]
                start = side * (f_rows - keep)
                down[start : start + keep, :] = do[:keep, :]
                start = (1 - side) * keep
                down[start : start + f_rows - keep, :] = dg[...].astype(f32)

    operands = [up_own, up_got, down_own, down_got]
    outs = [shape((d_rows, 2 * half), f32), shape((f_rows, width), f32)]
    return kernel_call(
        body,
        1,
        [SCALARS] + [full(o.shape) for o in operands],
        [full(o.shape) for o in outs],
        outs,
        [],
        0,
        [info, *operands],
    )


def group_rows_out(info, shared, last, d_rows, f_rows):
    group, _, width = shared.shape
    f_own = f_rows // group
    cols = width // group
    count = width // f_own

    def body(info, shared, last, up, down, qkv, proj):
        for a in range(group):
            part = shared[info[8] ^ a].astype(f32)
            for d in range(count):
                at = d * f_rows + a * f_own
                up[:, at : at + f_own] = part[:d_rows, d * f_own : (d + 1) * f_own]
            down[a * f_own : (a + 1) * f_own, :] = part[d_rows:, :]
            part = last[info[8] ^ a].astype(f32)
            for i in range(3):
                at = i * width + a * cols
                qkv[:, at : at + cols] = part[:, i * cols : (i + 1) * cols]
            proj[:, a * cols : (a + 1) * cols] = part[:, 3 * cols :]

    outs = [
        shape((d_rows, count * f_rows), f32),
        shape((f_rows, width), f32),
        shape((d_rows, 3 * width), f32),
        shape((d_rows, width), f32),
    ]
    return kernel_call(
        body,
        1,
        [SCALARS, full(shared.shape), full(last.shape)],
        [full(o.shape) for o in outs],
        outs,
        [],
        0,
        [info, shared, last],
    )


def front(info, tokens, mods, bias, pieces, rows_piece, cols_own, cut):
    blocks, rows = tokens.shape[0], tokens.shape[1] - 16
    width = 8 * rows_piece
    wide = 3 * cols_own

    def body(info, tok, more, mod, bias, *refs):
        parts = refs[:8]
        (hid, prj, qkv, table, gates, low_grad, slot, sums, lines, units, three, lists) = refs[8:]
        step = pl.program_id(0)

        @pl.when(step == 0)
        def _():
            for k in range(8):
                at = pl.multiple_of(info[k] * rows_piece, rows_piece)
                qkv[pl.ds(at, rows_piece), :] = parts[k][:rows_piece, :]
                if cut:
                    lists[info[k]] = parts[k][rows_piece:, :].astype(f32)
            three[...] = bias[...]
            if cut:
                three[:, :cols_own] = lists[info[8]][2:3, :cols_own]
                three[:, 2 * cols_own :] = lists[info[8] + 4][2:3, :cols_own]
                lines[...] = jnp.zeros_like(lines)
                for d in range(8):
                    at = slice(d * rows_piece, (d + 1) * rows_piece)
                    for i, row in enumerate((0, 3, 4, 5)):
                        lines[i : i + 1, at] = lists[d, row : row + 1, :rows_piece]
                size = units.shape[2]
                for side in range(2):

                    @pl.when(info[9] == side)
                    def _():
                        for p in range(units.shape[0]):
                            one, two = pair_places(p)
                            if side == 0:
                                units[p, :, :cut] = lists[one, 1:2, :cut]
                                units[p, :, cut:] = lists[two, 1:2, : size - cut]
                            else:
                                units[p, :, :cut] = lists[two, 1:2, size - cut : size]
                                units[p, :, cut:] = lists[one, 1:2, cut:size]

            sums[...] = jnp.zeros_like(sums)

        normed, _ = norm_parts(tok[0, :, :width].astype(f32))
        low = (normed * (1.0 + mod[0, 1:2, :]) + mod[0, 0:1, :]).astype(bf16)
        hid[...] = low
        prj[...] = (dot(low, qkv[...]) + three[...]).astype(bf16)

        me = info[8].astype(f32)
        pairs = more[0].astype(f32)
        one = (pairs[0:1, :] == me).astype(f32)
        two = (pairs[1:2, :] == me).astype(f32)
        hot = one + two
        gate = one * (pairs[2:3, :] + pairs[4:5, :] + pairs[6:7, :]) + two * (
            pairs[3:4, :] + pairs[5:6, :] + pairs[7:8, :]
        )
        across = lax.broadcasted_iota(jnp.int32, (rows, rows), 1)
        down = lax.broadcasted_iota(jnp.int32, (rows, rows), 0)
        earlier = (down < across).astype(f32).astype(bf16)
        rank = dot(jnp.broadcast_to(hot, (8, rows)).astype(bf16), earlier)[0:1, :]
        kept = hot * (rank < CAP).astype(f32)
        places = lax.broadcasted_iota(jnp.int32, (CAP, rows), 0).astype(f32)
        placed = jnp.where(rank == places, kept, 0.0)
        table[0] = placed.astype(bf16)
        gates[0] = jnp.sum(jnp.where(down == across, gate, 0.0), axis=1, keepdims=True)
        cot = tok[0, :, width:]
        grad = (mod[0, 5:6, :] * cot.astype(f32)).astype(bf16)
        low_grad[...] = grad
        gate_slot = jnp.sum(placed * gate, axis=1, keepdims=True)
        slot_grad = (gate_slot * (mod[0, 5:6, :] * dot(table[0], cot))).astype(bf16)
        slot[...] = slot_grad
        sums[0:1, :] += jnp.sum(slot_grad.astype(f32), axis=0, keepdims=True)
        sums[1:2, :] += jnp.sum(grad.astype(f32), axis=0, keepdims=True)
        sums[2:3, :] += jnp.broadcast_to(jnp.sum(kept, axis=1, keepdims=True), (1, width))

    return kernel_call(
        body,
        blocks,
        [
            SCALARS,
            pl.BlockSpec((1, rows, 2 * width), lambda i: (i, 0, 0)),
            pl.BlockSpec((1, 16, rows), lambda i: (i, rows // 16, 0)),
            pl.BlockSpec((1, 8, width), lambda i: (i, 0, 0)),
            full((1, wide)),
        ]
        + [full(p.shape) for p in pieces],
        [
            pl.BlockSpec((rows, width), lambda i: (i, 0)),
            pl.BlockSpec((rows, wide), lambda i: (i, 0)),
            full((width, wide)),
            pl.BlockSpec((1, CAP, rows), lambda i: (i, 0, 0)),
            pl.BlockSpec((1, rows, 1), lambda i: (i, 0, 0)),
            pl.BlockSpec((rows, width), lambda i: (i, 0)),
            pl.BlockSpec((CAP, width), lambda i: (i, 0)),
            full((8, width)),
            full((8, width)),
            full((4, 1, width // 2)),
        ],
        [
            shape((blocks * rows, width), bf16),
            shape((blocks * rows, wide), bf16),
            shape((width, wide), bf16),
            shape((blocks, CAP, rows), bf16),
            shape((blocks, rows, 1), f32),
            shape((blocks * rows, width), bf16),
            shape((blocks * CAP, width), bf16),
            shape((8, width), f32),
            shape((8, width), f32),
            shape((4, 1, width // 2), f32),
        ],
        [pltpu.VMEM((1, wide), f32), pltpu.VMEM((8, 16, wide), f32)],
        2 * blocks * rows * width * wide,
        [info, tokens, tokens, mods, bias, *pieces],
    )


def to_rows(own, got, bias, table, gates, addend, tokens, line):
    blocks, cap, rows = table.shape
    width = own.shape[1]

    def body(own, got, bias, tab, gate, add, tok, line, send, keep, sums):
        slots = (own[...] + got[...].astype(f32) + bias[...]).astype(bf16)
        value = add[...] + gate[0] * dot(tab[0], slots, 0, 0)
        first = (pl.program_id(0) == 0).astype(f32)
        sums[0] = jnp.sum(
            tok[0].astype(f32) * (value + first * line[...]), axis=0, keepdims=True
        )
        for k in range(blocks):

            @pl.when(pl.program_id(0) == k)
            def _():
                if k % 2 == 1:
                    send[k // 2] = value.astype(bf16)
                else:
                    keep[k // 2] = value

    operands = [own, got, bias, table, gates, addend, tokens, line]
    return kernel_call(
        body,
        blocks,
        [
            pl.BlockSpec((cap, width), lambda i: (i, 0)),
            pl.BlockSpec((cap, width), lambda i: (i, 0)),
            full((1, width)),
            pl.BlockSpec((1, cap, rows), lambda i: (i, 0, 0)),
            pl.BlockSpec((1, rows, 1), lambda i: (i, 0, 0)),
            pl.BlockSpec((rows, width), lambda i: (i, 0)),
            pl.BlockSpec((1, rows, width), lambda i: (i, 0, 1)),
            full((1, width)),
        ],
        [
            full((2, rows, width)),
            full((2, rows, width)),
            pl.BlockSpec((1, 1, width), lambda i: (i, 0, 0)),
        ],
        [
            shape((2, rows, width), bf16),
            shape((2, rows, width), f32),
            shape((blocks, 1, width), f32),
        ],
        [],
        2 * blocks * rows * width * cap,
        operands,
    )


def score_parts(info, query, key, blocks, rows):
    own = info[10 + pl.program_id(0)]
    lanes = lax.broadcasted_iota(jnp.int32, (1, blocks * rows), 1) // rows
    seen = jnp.zeros((1, blocks * rows), jnp.int32)
    for j in range(blocks):
        seen = jnp.where((lanes == j) & (info[10 + j] == own), 1, seen)
    scores = dot(query, key, 1, 1) * (HEAD_DIM ** (-0.5))
    masked = jnp.where(seen == 1, scores, -1e30)
    exponent = jnp.exp(masked - jnp.max(masked, axis=-1, keepdims=True))
    return exponent / jnp.sum(exponent, axis=-1, keepdims=True)


def attention(info, projected, blocks, cols_own):
    total, wide = projected.shape
    rows = total // blocks

    def body(info, own, every, out):
        for h in range(cols_own // HEAD_DIM):
            q = slice(h * HEAD_DIM, (h + 1) * HEAD_DIM)
            k = slice(cols_own + h * HEAD_DIM, cols_own + (h + 1) * HEAD_DIM)
            v = slice(2 * cols_own + h * HEAD_DIM, 2 * cols_own + (h + 1) * HEAD_DIM)
            probs = score_parts(info, own[:, q], every[:, k], blocks, rows)
            out[:, q] = dot(probs.astype(bf16), every[:, v]).astype(bf16)

    return kernel_call(
        body,
        blocks,
        [SCALARS, pl.BlockSpec((rows, wide), lambda i: (i, 0)), full((total, wide))],
        [pl.BlockSpec((rows, cols_own), lambda i: (i, 0))],
        [shape((total, cols_own), bf16)],
        [],
        4 * total * total * cols_own,
        [info, projected, projected],
    )[0]


def attention_back(info, projected, grad_attn, proj_rel, blocks, cols_own):
    total, wide = projected.shape
    rows = total // blocks
    width = grad_attn.shape[1]
    scale = HEAD_DIM ** (-0.5)

    def body(info, own, every, grad, rel, out, sums_k, sums_v, sums_q):
        step = pl.program_id(0)

        @pl.when(step == 0)
        def _():
            sums_k[...] = jnp.zeros_like(sums_k)
            sums_v[...] = jnp.zeros_like(sums_v)

        back = dot(grad[...], rel[...], 1, 1).astype(bf16)
        for h in range(cols_own // HEAD_DIM):
            q = slice(h * HEAD_DIM, (h + 1) * HEAD_DIM)
            k = slice(cols_own + h * HEAD_DIM, cols_own + (h + 1) * HEAD_DIM)
            v = slice(2 * cols_own + h * HEAD_DIM, 2 * cols_own + (h + 1) * HEAD_DIM)
            probs = score_parts(info, own[:, q], every[:, k], blocks, rows)
            grad_probs = dot(back[:, q], every[:, v], 1, 1)
            inner = jnp.sum(probs * grad_probs, axis=-1, keepdims=True)
            scores = (probs * (grad_probs - inner)).astype(bf16)
            at = pl.multiple_of(step * rows, rows)
            sums_q[pl.ds(at, rows), q] = dot(scores, every[:, k]) * scale
            sums_k[:, q] += dot(scores, own[:, q], 0, 0)
            sums_v[:, q] += dot(probs.astype(bf16), back[:, q], 0, 0)

        @pl.when(step == blocks - 1)
        def _():
            out[:, :cols_own] = sums_q[...].astype(bf16)
            out[:, cols_own : 2 * cols_own] = (sums_k[...] * scale).astype(bf16)
            out[:, 2 * cols_own :] = sums_v[...].astype(bf16)

    return kernel_call(
        body,
        blocks,
        [
            SCALARS,
            pl.BlockSpec((rows, wide), lambda i: (i, 0)),
            full((total, wide)),
            pl.BlockSpec((rows, width), lambda i: (i, 0)),
            full((cols_own, width)),
        ],
        [full((total, wide))],
        [shape((total, wide), bf16)],
        [pltpu.VMEM((total, cols_own), f32)] * 3,
        10 * total * total * cols_own + 2 * total * width * cols_own,
        [info, projected, projected, grad_attn, proj_rel],
    )[0]


def middle(info, tokens, mods, heads, pieces, proj_bias, table, rows_piece):
    blocks, rows = tokens.shape[0], tokens.shape[1] - 16
    width = 8 * rows_piece
    cols = width // blocks
    cap = table.shape[1]

    def body(info, tok, mod, h0, h1, h2, h3, bias, tab, *refs):
        parts, (hid, att, buf, out0, mid0, own, rel) = refs[:8], refs[8:]

        @pl.when(pl.program_id(0) == 0)
        def _():
            for k in range(8):
                place = info[18 + k]
                at = ((place >> 1) ^ info[8]) * cols + (place & 1) * rows_piece
                at = pl.multiple_of(at, rows_piece)
                rel[pl.ds(at, rows_piece), :] = parts[k][2 * rows_piece :, :]
            own[...] = rel[:cols, :]

        attended = jnp.concatenate([h0[...], h1[...], h2[...], h3[...]], axis=1)
        att[...] = attended
        out = dot(attended, rel[...]) + bias[...]
        mid = tok[0].astype(f32) + mod[0, 2:3, :] * out
        normed, _ = norm_parts(mid)
        low = (normed * (1.0 + mod[0, 4:5, :]) + mod[0, 3:4, :]).astype(bf16)
        hid[...] = low
        buf[...] = dot(tab[0], low).astype(bf16)

        @pl.when(pl.program_id(0) == 0)
        def _():
            out0[...] = out
            mid0[...] = mid

    return kernel_call(
        body,
        blocks,
        [
            SCALARS,
            pl.BlockSpec((1, rows, width), lambda i: (i, 0, 0)),
            pl.BlockSpec((1, 8, width), lambda i: (i, 0, 0)),
            pl.BlockSpec((rows, cols), lambda i: (i, 0)),
            pl.BlockSpec((rows, cols), lambda i: (i ^ 1, 0)),
            pl.BlockSpec((rows, cols), lambda i: (i ^ 2, 0)),
            pl.BlockSpec((rows, cols), lambda i: (i ^ 3, 0)),
            full((1, width)),
            pl.BlockSpec((1, cap, rows), lambda i: (i, 0, 0)),
        ]
        + [full(p.shape) for p in pieces],
        [
            pl.BlockSpec((rows, width), lambda i: (i, 0)),
            pl.BlockSpec((rows, width), lambda i: (i, 0)),
            pl.BlockSpec((cap, width), lambda i: (i, 0)),
            full((rows, width)),
            full((rows, width)),
            full((cols, width)),
        ],
        [
            shape((blocks * rows, width), bf16),
            shape((blocks * rows, width), bf16),
            shape((blocks * cap, width), bf16),
            shape((rows, width), f32),
            shape((rows, width), f32),
            shape((cols, width), bf16),
        ],
        [pltpu.VMEM((width, width), bf16)],
        2 * blocks * rows * width * (width + cap),
        [info, tokens, mods, *heads, proj_bias, table, *pieces],
    )


def shared_expert(info, hidden, grad, bias, pieces, rows_piece, blocks, paired):
    total, width = hidden.shape
    rows = total // blocks
    pairs = 4
    sums_mine = (pairs, 2 * rows_piece, width) if paired else (2, width, width)
    sums_theirs = (pairs, 2 * rows_piece, width) if paired else (1, 8, width)

    def body(info, hid, gcl, bias, *refs):
        parts, (out, back, mine, theirs, line, up, down, up_sum, down_sum, wide) = refs[:8], refs[8:]
        step = pl.program_id(0)

        @pl.when(step == 0)
        def _():
            for k in range(8):
                at = pl.multiple_of(info[18 + k] * rows_piece, rows_piece)
                up[pl.ds(at, rows_piece), :] = parts[k][:rows_piece, :]
                down[pl.ds(at, rows_piece), :] = parts[k][rows_piece : 2 * rows_piece, :]
            up_sum[...] = jnp.zeros_like(up_sum)
            down_sum[...] = jnp.zeros_like(down_sum)
            wide[...] = jnp.zeros_like(wide)

        act, slope = gelu_parts(dot(hid[...], up[...]) + bias[...])
        low = act.astype(bf16)
        out[...] = dot(low, down[...])
        down_sum[...] += dot(low, gcl[...], 0, 0)
        grad_pre = dot(gcl[...], down[...], 1, 1) * slope
        grad_low = grad_pre.astype(bf16)
        wide[...] += jnp.sum(grad_low.astype(f32), axis=0, keepdims=True)
        up_sum[...] += dot(hid[...], grad_low, 0, 0)
        back[...] = dot(grad_low, up[...], 1, 1)

        @pl.when(step == blocks - 1)
        def _():
            line[...] = wide[...]
            if not paired:
                mine[0], mine[1] = up_sum[...], down_sum[...]
            for p in range(pairs if paired else 0):
                at = pl.multiple_of(info[18 + 2 * p] * rows_piece, rows_piece)
                far = pl.multiple_of(info[19 + 2 * p] * rows_piece, rows_piece)
                mine[p, :rows_piece, :] = up_sum[pl.ds(at, rows_piece), :]
                mine[p, rows_piece:, :] = down_sum[pl.ds(at, rows_piece), :]
                theirs[p, :rows_piece, :] = up_sum[pl.ds(far, rows_piece), :].astype(bf16)
                theirs[p, rows_piece:, :] = down_sum[pl.ds(far, rows_piece), :].astype(bf16)

    return kernel_call(
        body,
        blocks,
        [
            SCALARS,
            pl.BlockSpec((rows, width), lambda i: (i, 0)),
            pl.BlockSpec((rows, width), lambda i: (i, 0)),
            full((1, width)),
        ]
        + [full(p.shape) for p in pieces],
        [
            pl.BlockSpec((rows, width), lambda i: (i, 0)),
            pl.BlockSpec((rows, width), lambda i: (i, 0)),
            full(sums_mine),
            full(sums_theirs),
            full((1, width)),
        ],
        [
            shape((total, width), f32),
            shape((total, width), f32),
            shape(sums_mine, f32),
            shape(sums_theirs, bf16),
            shape((1, width), f32),
        ],
        [
            pltpu.VMEM((width, width), bf16),
            pltpu.VMEM((width, width), bf16),
            pltpu.VMEM((width, width), f32),
            pltpu.VMEM((width, width), f32),
            pltpu.VMEM((1, width), f32),
        ],
        12 * total * width * width,
        [info, hidden, grad, bias, *pieces],
    )


def routed_rows_grads(info, buffers, slots, own, other, bias):
    pairs, _, units = bias.shape
    count, width = buffers[0].shape
    piece = width // (2 * pairs)
    every = pairs * units
    chunks = every // width
    cut = own[0].shape[0] - chunks * piece

    def body(info, b0, b1, s0, s1, *refs):
        packs, bias = (refs[:4], refs[4:8]), refs[8]
        (g0, g1, e0, e1, line, act_low, grad_low, bs, ss, up, down, gsum, esum) = refs[9:]
        step = pl.program_id(0)

        @pl.when(step == 0)
        def _():
            for r in range(pairs):
                for j in range(2):
                    at = pl.multiple_of(info[18 + 2 * r + j] * piece, piece)
                    for c in range(chunks):
                        up[pl.ds(at, piece), c * width : (c + 1) * width] = packs[j][r][
                            c * piece : (c + 1) * piece, :
                        ]
                    at = info[14 + r] * units + j * cut
                    at = pl.multiple_of(at, 128)
                    size = units - cut if j else cut
                    down[pl.ds(at, size), :] = packs[j][r][chunks * piece :, :]
            bs[:count, :], bs[count:, :] = b0[...], b1[...]
            ss[:count, :], ss[count:, :] = s0[...], s1[...]
            gsum[...] = jnp.zeros_like(gsum)
            esum[...] = jnp.zeros_like(esum)

        at = pl.multiple_of(step * units, 128)
        w_up = up[:, pl.ds(at, units)]
        w_down = down[pl.ds(at, units), :]
        act, slope = gelu_parts(dot(bs[...], w_up) + bias[step])
        low = act.astype(bf16)
        act_low[...] = low
        esum[...] += dot(low, w_down)
        grad = (dot(ss[...], w_down, 1, 1) * slope).astype(bf16)
        grad_low[...] = grad
        line[0] = jnp.sum(grad.astype(f32), axis=0, keepdims=True)
        gsum[...] += dot(grad, w_up, 1, 1)

        @pl.when(step == pairs - 1)
        def _():
            g0[...] = gsum[:count, :]
            g1[...] = gsum[count:, :].astype(bf16)
            e0[...] = esum[:count, :]
            e1[...] = esum[count:, :].astype(bf16)

    outs = [
        shape((count, width), f32),
        shape((count, width), bf16),
        shape((count, width), f32),
        shape((count, width), bf16),
        shape((pairs, 1, units), f32),
        shape((2 * count, every), bf16),
        shape((2 * count, every), bf16),
        shape((2 * count, width), bf16),
        shape((2 * count, width), bf16),
    ]
    operands = [*buffers, *slots, *own, *other, bias]
    by_step = pl.BlockSpec((2 * count, units), lambda i: (0, i))
    return kernel_call(
        body,
        pairs,
        [SCALARS] + [full(o.shape) for o in operands],
        [full(o.shape) for o in outs[:4]]
        + [pl.BlockSpec((1, 1, units), lambda i: (i, 0, 0)), by_step, by_step]
        + [full(o.shape) for o in outs[7:]],
        outs,
        [
            pltpu.VMEM((width, every), bf16),
            pltpu.VMEM((every, width), bf16),
            pltpu.VMEM((2 * count, width), f32),
            pltpu.VMEM((2 * count, width), f32),
        ],
        16 * count * width * every,
        [info, *operands],
    )


def routed_weight_grads(info, act_low, grad_low, rows, slots, pairs):
    total, width = rows.shape
    every = act_low.shape[1]
    units = every // pairs
    piece = width // (2 * pairs)

    def body(info, act, grad, bs, ss, ds, dk, us, uk, values):
        step = pl.program_id(0)
        block = info[14 + step]
        at = pl.multiple_of(block * units, 128)
        rdown = dot(act[:, pl.ds(at, units)], ss[...], 0, 0)
        values[...] = dot(bs[...], grad[:, pl.ds(at, units)], 0, 0)
        for r in range(pairs):
            for j in range(2):
                row = pl.multiple_of(info[18 + 2 * r + j] * piece, piece)
                value = values[pl.ds(row, piece), :]
                if r % 2 == 1:
                    us[r // 2, j * piece : (j + 1) * piece, pl.ds(at, units)] = value.astype(bf16)
                else:
                    uk[r // 2, j * piece : (j + 1) * piece, pl.ds(at, units)] = value

            @pl.when(step == r)
            def _():
                if r % 2 == 1:
                    ds[r // 2] = rdown.astype(bf16)
                else:
                    dk[r // 2] = rdown

    outs = [
        shape((2, units, width), bf16),
        shape((2, units, width), f32),
        shape((2, 2 * piece, every), bf16),
        shape((2, 2 * piece, every), f32),
    ]
    operands = [act_low, grad_low, rows, slots]
    return kernel_call(
        body,
        pairs,
        [SCALARS] + [full(o.shape) for o in operands],
        [full(o.shape) for o in outs],
        outs,
        [pltpu.VMEM((width, units), f32)],
        4 * total * width * every,
        [info, *operands],
    )


def tail_grads(info, tokens, hidden, grads, attended, grad_attn, qkv):
    total, width = hidden.shape
    wide = grads.shape[1]
    blocks, rows = tokens.shape[0], tokens.shape[1] - 16
    cols = width // blocks
    piece = width // 8

    def body(info, tok, hid, gr, att, ga, qkv, away, stay, send, keep, sums, lines, proj, wq):
        wq[...] = dot(hid[...], gr[...], 0, 0)
        for m in range(blocks):
            these = slice(m * rows, (m + 1) * rows)
            grad = dot(gr[these, :], qkv[...], 1, 1)
            if m % 2 == 1:
                send[m // 2] = grad.astype(bf16)
            else:
                keep[m // 2] = grad
            normed, _ = norm_parts(tok[m].astype(f32))
            sums[m : m + 1, :] = jnp.sum(grad, axis=0, keepdims=True)
            sums[blocks + m : blocks + m + 1, :] = jnp.sum(grad * normed, axis=0, keepdims=True)
        lines[:, :wide] = jnp.sum(gr[...].astype(f32), axis=0, keepdims=True)
        lines[:, wide:] = jnp.sum(ga[...].astype(f32), axis=0, keepdims=True)
        own = ga[:, :cols]
        for k in range(1, blocks):
            own = jnp.where(info[8] == k, ga[:, k * cols : (k + 1) * cols], own)
        proj[...] = dot(att[...], own, 0, 0)
        for k in range(8):
            place = info[18 + k]
            at = pl.multiple_of(place * piece, piece)
            value = wq[pl.ds(at, piece), :]
            at = pl.multiple_of(((place >> 1) ^ info[8]) * cols + (place & 1) * piece, piece)
            other = proj[pl.ds(at, piece), :]
            i = k % 2 + 2 * (k // 4)
            if k // 2 % 2 == 1:
                away[i, :, :wide] = value.astype(bf16)
                away[i, :, wide:] = other.astype(bf16)
            else:
                stay[i, :, :wide] = value
                stay[i, :, wide:] = other

    return kernel_call(
        body,
        1,
        [SCALARS, pl.BlockSpec((blocks, rows, width), lambda i: (0, 0, 0))]
        + [full((total, width)), full((total, wide)), full((total, width))]
        + [full((total, width)), full((width, wide))],
        [
            full((4, piece, width)),
            full((4, piece, width)),
            full((2, rows, width)),
            full((2, rows, width)),
            full((2 * blocks, width)),
            full((1, wide + width)),
        ],
        [
            shape((4, piece, width), bf16),
            shape((4, piece, width), f32),
            shape((2, rows, width), bf16),
            shape((2, rows, width), f32),
            shape((2 * blocks, width), f32),
            shape((1, wide + width), f32),
        ],
        [pltpu.VMEM((width, cols), f32), pltpu.VMEM((width, wide), f32)],
        2 * total * width * (2 * wide + cols),
        [info, tokens, hidden, grads, attended, grad_attn, qkv],
    )


def in_order(relative, position):
    return jnp.stack(
        [
            lax.dynamic_index_in_dim(relative, position ^ a, 0, keepdims=False)
            for a in range(relative.shape[0])
        ]
    )


def body(
    tokens,
    conditioning,
    routes,
    gate_weights,
    image_counts,
    image_lengths,
    cotangent,
    qkv_weight,
    qv_bias,
    proj_weight,
    proj_bias,
    ada_weight,
    ada_bias,
    up_weight,
    up_bias,
    down_weight,
    down_bias,
    routed_up,
    routed_upbias,
    routed_down,
    routed_downbias,
):
    group = lax.axis_size("expert")
    copies = lax.axis_size("dp")
    position = lax.axis_index("expert")
    place = lax.axis_index("dp")
    rows, width = tokens.shape
    group_rows = group * rows
    heads_own = HEADS // group
    cols_own = heads_own * HEAD_DIM
    d_rows = qkv_weight.shape[0]
    f_rows = down_weight.shape[0]
    f_own = f_rows // group
    hidden_units = f_rows * copies
    quarter = hidden_units // group
    side = lax.rem(place // 2, 2)
    first_side = side == 0
    pairs_count = copies // 2
    keep = f_rows * 2 // 3
    send = f_rows - keep
    half_units = hidden_units // 2

    def my_units(value):
        one, two = [], []
        for p in range(pairs_count):
            at, to = (d * f_rows for d in pair_places(p))
            one += [value[..., at : at + keep], value[..., to : to + send]]
            two += [value[..., to + send : to + f_rows], value[..., at + keep : at + f_rows]]
        one, two = jnp.concatenate(one, axis=-1), jnp.concatenate(two, axis=-1)
        return jnp.where(first_side, one, two), jnp.where(first_side, two, one)

    def from_units(mine, theirs):
        one = jnp.where(first_side, mine, theirs)
        two = jnp.where(first_side, theirs, mine)
        out = [None] * copies
        for p in range(pairs_count):
            at = f_rows * p
            first, second = pair_places(p)
            out[first] = [one[..., at : at + keep], two[..., at + keep : at + f_rows]]
            out[second] = [one[..., at + keep : at + f_rows], two[..., at : at + keep]]
        out = sum(out, [])
        return jnp.concatenate(out, axis=-1)

    bias_list = [up_bias, routed_upbias[0], qv_bias, proj_bias, down_bias, routed_downbias[0]]
    if copies == 8:
        first_share, third_share, routed_mine, routed_theirs = prepare(
            jnp.stack([position] * 9 + [side]).astype(jnp.int32),
            proj_weight,
            qkv_weight,
            [b[None] for b in bias_list],
            up_weight,
            down_weight,
            routed_up[0],
            routed_down[0],
            keep,
            group,
        )
    else:
        qkv_share = lax.dynamic_index_in_dim(
            qkv_weight.reshape(d_rows, 3, group, cols_own), position, 2, keepdims=False
        ).reshape(d_rows, 3 * cols_own)
        first_share = qkv_share
        up_share = lax.dynamic_index_in_dim(
            up_weight.reshape(d_rows, copies, group, f_own), position, 2, keepdims=False
        ).reshape(d_rows, quarter)
        down_share = lax.dynamic_slice_in_dim(down_weight, position * f_own, f_own, axis=0)
        third_share = jnp.concatenate([up_share, down_share, proj_weight], axis=0)
        rup_mine, rup_theirs = my_units(routed_up[0])
        rdown_mine = lax.dynamic_slice_in_dim(routed_down[0], side * send, keep, axis=0)
        rdown_theirs = lax.dynamic_slice_in_dim(routed_down[0], (1 - side) * keep, send, axis=0)
        rup_got = pair_swap(rup_theirs)
        rdown_got = pair_swap(rdown_theirs)
    first, order = ring_gather(first_share)
    bias_three = jnp.zeros((1, 3 * cols_own), f32)
    if copies > 8:
        upb, rupb, qvb, projb, downb, rdownb = (
            lax.all_gather(b, "dp", axis=0, tiled=True).astype(f32) for b in bias_list
        )
        upb_own = lax.dynamic_index_in_dim(
            upb.reshape(copies, group, f_own), position, 1, keepdims=False
        ).reshape(quarter)
        bias_lines = jnp.stack([upb_own, projb, downb, rdownb])
        rupb_own = my_units(rupb)[0].reshape(4, 1, half_units // 4)
        bias_three = jnp.concatenate(
            [
                lax.dynamic_slice_in_dim(qvb, position * cols_own, cols_own),
                jnp.zeros((cols_own,), f32),
                lax.dynamic_slice_in_dim(qvb, width + position * cols_own, cols_own),
            ]
        )[None]

    pair_steps = jnp.arange(4, dtype=jnp.int32)
    if copies == 8:
        third_swap, routed_swap = pair_swap(third_share), pair_swap(routed_theirs)
        third_own = spread(third_share, *first[5:7])
        third_got = spread(third_swap, *first[5:7])
        routed_own = spread(tied(routed_mine, third_got[2]), *first[5:7])
        routed_got = spread(tied(routed_swap, third_got[2]), *first[5:7])
        third = [v for pair in zip(third_own, third_got) for v in pair]
        dues = [(*first[1:3], third_swap), (*first[3:5], third_own[2]), (*first[5:7], routed_swap), (third_got[2],), (third_own[3],), (), (routed_own[2],), (routed_own[3], routed_got[1])]
        pair_now = (place >> 2) * 2 + (place & 1)
        unit_blocks = pair_now ^ pair_steps
        masks = jnp.array([0, 2, 1, 3, 4, 6, 5, 7], jnp.int32)
        row_blocks = place ^ masks
    else:
        groups = side_groups(copies)
        whole = lax.all_gather(third_share, "dp", axis=0)
        third = jnp.concatenate(
            [
                whole[:, :d_rows].reshape(8, -1, width),
                whole[:, d_rows : d_rows + f_own].reshape(8, -1, width),
                whole[:, d_rows + f_own :].reshape(8, -1, width),
            ],
            axis=1,
        ).reshape(4, 2, -1, width)
        sided = jnp.where(
            first_side, jnp.stack([rup_mine, rup_got]), jnp.stack([rup_got, rup_mine])
        )
        ups = lax.all_gather(sided, "dp", axis=0, axis_index_groups=groups)
        ups = ups.reshape(pairs_count // 2, 2, 2, d_rows, half_units).transpose(0, 2, 1, 3, 4)
        ups = ups.reshape(4, 2, width // 8, half_units)
        downs = lax.all_gather(
            jnp.concatenate([rdown_mine, rdown_got]), "dp", axis=0, axis_index_groups=groups
        ).reshape(4, half_units // 4, width)
        third = [third[r, j] for r in range(4) for j in range(2)]
        cut = keep * half_units // (4 * f_rows)

        def packs(j, low, high):
            return [
                jnp.concatenate(
                    [ups[r, j, :, c : c + width] for c in range(0, half_units, width)]
                    + [downs[r, low:high]]
                )
                for r in range(4)
            ]

        routed_own, routed_got = packs(0, 0, cut), packs(1, cut, half_units // 4)
        dues = [()] * 8
        unit_blocks = pair_steps
        row_blocks = jnp.arange(8, dtype=jnp.int32)

    def by_side(whole):
        out = whole.reshape(pairs_count // 2, 2, 2, d_rows, -1).transpose(1, 0, 2, 3, 4)
        return out.reshape(2, 4, width // 8, -1)

    gates_left, gate_parts = gate_weights.T, []
    for _ in range(3):
        part = lax.reduce_precision(gates_left, 8, 7)
        gate_parts.append(part.astype(bf16))
        gates_left = gates_left - part
    under = jnp.concatenate([routes.T.astype(bf16), *gate_parts], axis=0)
    under = jnp.pad(under, ((0, 8), (0, 2 * width - rows)))
    both = gather_group(
        jnp.concatenate([jnp.concatenate([tokens, cotangent], axis=1), under], axis=0)
    )

    lengths = image_lengths[0]
    image_total = image_counts[0]
    slots = lengths.shape[0]
    slot_ids = jnp.arange(slots, dtype=jnp.int32)
    starts = jnp.sum(
        jnp.where(slot_ids[None, :] < slot_ids[:, None], lengths[None, :], 0), axis=1
    )
    live = (slot_ids >= 1) & (slot_ids < image_total)
    block_ids = position ^ jnp.arange(group, dtype=jnp.int32)
    segment = jnp.sum(
        (live[None, :] & (starts[None, :] <= (block_ids * rows)[:, None])).astype(jnp.int32),
        axis=1,
    )
    block_hot = segment[:, None] == slot_ids[None, :]

    info = jnp.concatenate(
        [
            order,
            jnp.stack([position, side]),
            segment,
            unit_blocks,
            row_blocks,
            jnp.zeros((6,), jnp.int32),
        ]
    ).astype(jnp.int32)

    cond_value = conditioning[0].astype(f32)
    cond_act = jax.nn.silu(cond_value).astype(bf16)
    act_parts = lax.all_to_all(
        cond_act.reshape(slots, copies, d_rows).transpose(1, 0, 2),
        "dp",
        split_axis=0,
        concat_axis=0,
        tiled=True,
    ).reshape(copies * slots, d_rows)
    mod_width = ada_weight.shape[1]
    mod_own = mod_width // group
    bias_line = lax.dynamic_update_slice(
        jnp.zeros((mod_width,), f32), ada_bias.astype(f32), (place * ada_bias.shape[0],)
    )
    ada_own = lax.dynamic_slice_in_dim(ada_weight, position * mod_own, mod_own, axis=1)
    bias_own = lax.dynamic_slice_in_dim(bias_line, position * mod_own, mod_own)
    mod_parts = (mm("sd,dm->sm", tied(act_parts, *dues[0]), ada_own) + bias_own[None]).reshape(
        copies, slots, mod_own
    )
    mod_got = lax.all_to_all(mod_parts, "dp", split_axis=0, concat_axis=0, tiled=True)
    mod_sum = jnp.sum(tied(mod_got, *dues[1]), axis=0)
    mod_across = tied(swap(mod_sum, 2), *dues[2])
    mod_beside = swap(jnp.stack([mod_sum, mod_across]), 1)
    mod_group = jnp.stack([mod_sum, mod_beside[0], mod_across, mod_beside[1]])
    modulation = in_order(mod_group, position).transpose(1, 0, 2).reshape(slots, mod_width)
    per_block = jnp.sum(
        jnp.where(block_hot[:, :, None], modulation[None, :, :], 0.0), axis=1
    )
    mods = jnp.pad(per_block.reshape(group, 6, width), ((0, 0), (0, 2), (0, 0)))
    shift_a, scale_a, gate_a, shift_b, scale_b, gate_b = (mods[0, i : i + 1] for i in range(6))

    (
        hidden_a,
        projected,
        qkv_own,
        table,
        gates,
        grad_comb_low,
        slot_own,
        sums_f,
        lines_got,
        units_got,
    ) = front(
        info,
        both,
        tied(mods, *dues[3]),
        bias_three,
        first,
        width // 8,
        cols_own,
        keep if copies == 8 else 0,
    )
    if copies == 8:
        bias_lines, rupb_own = lines_got, units_got
    upb_line, projb_line, downb_line, rdownb_line = (bias_lines[i : i + 1] for i in range(4))
    slot_got = pair_swap(slot_own)
    heads_0 = attention(info, tied(projected, *dues[4]), group, cols_own)
    heads_0 = tied(heads_0, *dues[5])
    heads_2 = swap(heads_0, 2)
    heads_1 = swap(heads_0, 1)
    heads_3 = swap(heads_2, 1)
    hidden_b, attended, buffer_own, attn_out, residual_mid, proj_own = middle(
        info,
        both,
        mods,
        (heads_0, heads_1, heads_2, heads_3),
        third,
        projb_line,
        tied(table, slot_got, *dues[6]),
        width // 8,
    )
    buffer_got = pair_swap(buffer_own)

    shared_parts, shared_back, shared_mine, shared_theirs, upbias_line = shared_expert(
        info, tied(hidden_b, *dues[7]), grad_comb_low, upb_line, third, width // 8, group, copies == 8
    )
    if copies != 8:
        sided = jnp.concatenate([by_side(shared_mine[0]), by_side(shared_mine[1])], axis=2)
        shared_mine, shared_theirs = (
            lax.dynamic_index_in_dim(sided, which, 0, keepdims=False) for which in (side, 1 - side)
        )
        shared_theirs = shared_theirs.astype(bf16)
    shared_back_got = pair_swap(shared_theirs)
    (
        back_own,
        back_theirs,
        out_own,
        out_theirs,
        units_sum,
        act_low,
        grad_low,
        both_rows,
        both_slots,
    ) = routed_rows_grads(
        info,
        (tied(buffer_own, shared_theirs), buffer_got),
        (slot_own, slot_got),
        routed_own,
        routed_got,
        rupb_own,
    )
    shared_sums = shared_mine + shared_back_got.astype(f32)
    shared_send = jnp.stack([shared_sums[1], shared_sums[3]]).astype(bf16)
    down_send, down_keep, up_send, up_keep = routed_weight_grads(
        info, tied(act_low, shared_send), grad_low, both_rows, both_slots, 4
    )
    if copies == 8:
        shared_first = dp_swap(shared_send, 1)
        shared_near = shared_sums[0] + shared_first[0].astype(f32)
        shared_far = dp_swap((shared_sums[2] + shared_first[1].astype(f32)).astype(bf16), 4)
        down_first = dp_swap(down_send, 1)
        due_rows = (down_send, shared_first)
        due_back = (down_first, shared_far)
    else:
        due_rows, due_back = (down_send,), ()
    units_sum = units_sum.reshape(pairs_count, f_rows)
    blank = jnp.zeros((pairs_count, f_rows), f32)
    units_one = jnp.where(first_side, units_sum, blank)
    units_two = jnp.where(first_side, blank, units_sum)
    units_by_place = jnp.stack(
        [
            jnp.concatenate([units_one[:, :keep], units_two[:, keep:]], axis=1),
            jnp.concatenate([units_one[:, keep:], units_two[:, :keep]], axis=1),
        ]
    )
    units_by_place = units_by_place.reshape(2, pairs_count // 2, 2, f_rows).transpose(1, 0, 2, 3)
    expert_line = jnp.concatenate(
        [
            units_by_place.reshape(copies, f_rows),
            upbias_line.reshape(copies, f_own),
            sums_f[0].reshape(copies, d_rows),
            sums_f[1].reshape(copies, d_rows),
        ],
        axis=1,
    )
    zero_line = jnp.zeros((1, width), f32)
    rows_send, rows_keep, _ = to_rows(
        tied(back_own, *due_rows),
        pair_swap(back_theirs),
        zero_line,
        table,
        jnp.ones((group, rows, 1), f32),
        shared_back,
        both,
        zero_line,
    )
    back_near, back_got = reduce_group(rows_send, rows_keep)
    grad_mid, grad_attn_own, sums_b = middle_back(
        tied(back_near, *due_back), back_got, residual_mid, attn_out, cotangent, mods
    )
    attn_2 = swap(grad_attn_own, 2)
    grad_attn = jnp.concatenate(
        [grad_attn_own, swap(grad_attn_own, 1), attn_2, swap(attn_2, 1)]
    )

    grad_projected = attention_back(info, projected, grad_attn, proj_own, group, cols_own)
    out_got = pair_swap(out_theirs)
    due_tail = (out_got,)
    if copies == 8:
        down_far = dp_swap((down_keep[1] + down_first[1].astype(f32)).astype(bf16), 4)
        up_first = dp_swap(tied(up_send, down_first), 1)
        due_tail = (out_got, down_far, up_first)
    away, stay, back_send, back_keep, sums_a, lines = tail_grads(
        info, both, tied(hidden_a, *due_tail), grad_projected, attended, grad_attn, qkv_own
    )

    if copies == 8:
        up_far = dp_swap((up_keep[1] + up_first[1].astype(f32)).astype(bf16), 4)
        shared_rows = shared_near + shared_far.astype(f32)
        rdown_sums = down_keep[0] + down_first[0].astype(f32) + down_far.astype(f32)
        rup_sums = up_keep[0] + up_first[0].astype(f32) + up_far.astype(f32)
        last_first = stay + dp_swap(away, 1).astype(f32)
        last_second = last_first[:2] + dp_swap(last_first[2:].astype(bf16), 4).astype(f32)
    else:

        def scatter(value, each):
            return lax.psum_scatter(
                value.reshape(pairs_count, each, -1).astype(bf16),
                "dp",
                scatter_dimension=0,
                axis_index_groups=side_groups(copies),
                tiled=False,
            )

        def whole_of(send, keep):
            send = send.astype(f32)
            return jnp.stack([keep[0], send[0], keep[1], send[1]])

        shared_rows = jnp.concatenate(
            [scatter(shared_sums[:, : width // 8], d_rows), scatter(shared_sums[:, width // 8 :], f_own)]
        )
        rdown_sums = scatter(whole_of(down_send, down_keep), f_rows)
        sided = by_side(whole_of(up_send, up_keep))
        rup_sums = jnp.concatenate(
            [
                scatter(lax.dynamic_index_in_dim(sided, which, 0, keepdims=False), d_rows)
                for which in (side, 1 - side)
            ]
        )
        last_parts = jnp.stack(
            [(away if k // 2 % 2 else stay)[k % 2 + 2 * (k // 4)].astype(bf16) for k in range(8)]
        )
        last_sums = jnp.sum(
            lax.all_to_all(
                last_parts.reshape(copies, d_rows, width),
                "dp",
                split_axis=0,
                concat_axis=0,
                tiled=True,
            ).astype(f32),
            axis=0,
        )

    lines = lines[0]
    qv_line = lax.dynamic_update_slice(
        jnp.zeros((2 * width,), f32), lines[:cols_own], (position * cols_own,)
    )
    qv_line = lax.dynamic_update_slice(
        qv_line, lines[2 * cols_own : 3 * cols_own], (width + position * cols_own,)
    ).reshape(copies, -1)
    pb_line = lines[3 * cols_own :].reshape(copies, d_rows)
    count_own = sums_f[2, 0]
    count_high = jnp.floor(count_own / 128.0)
    count_line = jnp.broadcast_to(
        jnp.stack([count_high, count_own - 128.0 * count_high])[None], (copies, 2)
    )
    line = jnp.concatenate([expert_line, qv_line, pb_line, count_line], axis=1)
    line_width = -(-line.shape[1] // (slots * 128)) * 128
    line = jnp.pad(line, ((0, 0), (0, slots * line_width - line.shape[1]))).reshape(
        copies, slots, line_width
    )

    rows_send, rows_keep, sums_out = to_rows(
        tied(out_own, away),
        out_got,
        rdownb_line,
        table,
        gates,
        shared_parts,
        both,
        downb_line,
    )
    combined_near, combined_got = reduce_group(rows_send, rows_keep)
    near_a, got_a = reduce_group(back_send, back_keep)

    block_of = block_hot.astype(f32)
    sums_all = jnp.concatenate(
        [
            sums_a[:group],
            sums_a[group:],
            jnp.pad(sums_b[:3].reshape(1, 3 * width), ((0, group - 1), (0, 0))),
            sums_out.reshape(group, width),
        ],
        axis=1,
    )
    slot_sums = jnp.sum(block_of[:, :, None] * sums_all[:, None, :], axis=0)
    slot_sums = slot_sums + swap(slot_sums, 1)
    slot_sums = slot_sums + swap(slot_sums, 2)
    grad_modulation = slot_sums.astype(bf16)
    mod_got = lax.all_to_all(
        jnp.concatenate(
            [
                jnp.broadcast_to(grad_modulation[None], (copies, slots, mod_width)),
                line.astype(bf16),
            ],
            axis=2,
        ),
        "dp",
        split_axis=0,
        concat_axis=0,
        tiled=True,
    )
    mod_all = mod_got[:, :, :mod_width].reshape(copies * slots, mod_width)
    line_sums = jnp.sum(mod_got[:, :, mod_width:].astype(f32), axis=0).reshape(-1)
    ada_grad = mm("sd,sm->dm", act_parts, mod_all)
    adabias_grad = jnp.sum(
        lax.dynamic_slice_in_dim(
            mod_all, place * ada_bias.shape[0], ada_bias.shape[0], axis=1
        ).astype(f32),
        axis=0,
    )
    cond_parts = mm("sm,dm->sd", mod_all, ada_weight).reshape(copies, slots, d_rows)
    after = cond_parts
    got_a, combined_got = tied(got_a, after), tied(combined_got, after)
    combined = combined_near + combined_got.astype(f32) + downb_line
    output = (residual_mid + gate_b * combined).astype(bf16)
    grad_hidden_a = near_a + got_a.astype(f32)
    normed_a, inv_std_a = norm_parts(tokens.astype(f32))
    tokens_grad = grad_mid + norm_back(grad_hidden_a * (1.0 + scale_a), normed_a, inv_std_a)
    if copies == 8:
        last_second = tied(last_second, after)
        last_third = dp_swap(last_second[1].astype(bf16), 2)
        last_sums = last_second[0] + last_third.astype(f32)
        rup_sums = tied(rup_sums, after)
    grad_cond_act = (
        lax.all_to_all(cond_parts, "dp", split_axis=0, concat_axis=0, tiled=True)
        .transpose(1, 0, 2)
        .reshape(slots, width)
    )
    sigmoid_cond = jax.nn.sigmoid(cond_value)
    conditioning_grad = (grad_cond_act * sigmoid_cond * (1.0 + cond_value * (1.0 - sigmoid_cond)))[
        None
    ]

    rup_got = pair_swap(rup_sums[d_rows:].astype(bf16))
    rdown_got = pair_swap(rdown_sums[keep:].astype(bf16))
    shared_all = gather_group(shared_rows.astype(bf16))
    last_all = gather_group(last_sums.astype(bf16))
    if copies == 8:
        rup_rows, rdown_rows = routed_rows(info, rup_sums, rup_got, rdown_sums, rdown_got, keep)
        up_rows, down_rows, qkv_rows, proj_rows = group_rows_out(
            info, shared_all, last_all, d_rows, f_rows
        )
    else:
        rup_rows = from_units(rup_sums[:d_rows].astype(f32), rup_got.astype(f32))
        kept, back = rdown_sums[:keep].astype(f32), rdown_got.astype(f32)
        rdown_rows = jnp.where(
            first_side, jnp.concatenate([kept, back]), jnp.concatenate([back, kept])
        )
        shared_all, last_all = (
            in_order(v, position).astype(f32) for v in (shared_all, last_all)
        )
        up_rows = (
            shared_all[:, :d_rows]
            .reshape(group, d_rows, copies, f_own)
            .transpose(1, 2, 0, 3)
            .reshape(d_rows, hidden_units)
        )
        down_rows = shared_all[:, d_rows:].reshape(f_rows, width)
        qkv_rows = (
            last_all[:, :, : 3 * cols_own]
            .reshape(group, d_rows, 3, cols_own)
            .transpose(1, 2, 0, 3)
            .reshape(d_rows, 3 * width)
        )
        proj_rows = last_all[:, :, 3 * cols_own :].transpose(1, 0, 2).reshape(d_rows, width)
    cuts = [f_rows, f_own, d_rows, d_rows, 2 * width // copies, d_rows, 2]
    at = [sum(cuts[:i]) for i in range(len(cuts))]
    rupbias_row, upbias_sum, rdownbias_row, downbias_row, qvbias_sum, projbias_row, counts = (
        line_sums[o : o + n] for o, n in zip(at, cuts)
    )
    small = in_order(
        gather_group(jnp.concatenate([upbias_sum, qvbias_sum, counts])[None]), position
    )[:, 0]
    upbias_rows = small[:, :f_own].reshape(f_rows)
    qvbias_rows = jnp.sum(small[:, f_own:-2], axis=0)
    expert_counts = (128.0 * small[:, -2] + small[:, -1]).astype(jnp.int32)

    return (
        output,
        tokens_grad,
        conditioning_grad,
        qkv_rows,
        qvbias_rows,
        proj_rows,
        projbias_row,
        ada_grad,
        adabias_grad,
        up_rows,
        upbias_rows,
        down_rows,
        downbias_row,
        rup_rows[None],
        rupbias_row[None],
        rdown_rows[None],
        rdownbias_row[None],
        expert_counts,
    )


def solution(mesh):
    in_specs = (
        P(("dp", "expert"), None),
        P("dp", None, None),
        P(("dp", "expert"), None),
        P(("dp", "expert"), None),
        P("dp"),
        P("dp", None),
        P(("dp", "expert"), None),
        P("dp", None),
        P("dp"),
        P("dp", None),
        P("dp"),
        P("dp", None),
        P("dp"),
        P("dp", None),
        P("dp"),
        P("dp", None),
        P("dp"),
        P("expert", "dp", None),
        P("expert", "dp"),
        P("expert", "dp", None),
        P("expert", "dp"),
    )
    out_specs = (
        P(("dp", "expert"), None),
        P(("dp", "expert"), None),
        P("dp", None, None),
        P("dp", None),
        P("dp"),
        P("dp", None),
        P("dp"),
        P("dp", None),
        P("dp"),
        P("dp", None),
        P("dp"),
        P("dp", None),
        P("dp"),
        P("expert", "dp", None),
        P("expert", "dp"),
        P("expert", "dp", None),
        P("expert", "dp"),
        P(),
    )
    return jax.shard_map(body, mesh=mesh, in_specs=in_specs, out_specs=out_specs, check_vma=False)
```

```python
import jax
import jax.numpy as jnp
from jax import lax
from jax.experimental import pallas as pl
from jax.experimental.pallas import tpu as pltpu
from jax.sharding import PartitionSpec as P

HEADS = 12
HEAD_DIM = 64
CAP = 128

epsilon = 1e-06
gelu_root = 0.7978845608028654
gelu_cubic = 0.044715

bf16 = jnp.bfloat16
f32 = jnp.float32


def norm_parts(values):
    centered = values - jnp.mean(values, axis=-1, keepdims=True)
    inv_std = lax.rsqrt(jnp.mean(centered * centered, axis=-1, keepdims=True) + epsilon)
    return (centered * inv_std, inv_std)


def norm_back(grad_normed, normed, inv_std):
    mean_grad = jnp.mean(grad_normed, axis=-1, keepdims=True)
    mean_cross = jnp.mean(grad_normed * normed, axis=-1, keepdims=True)
    return inv_std * (grad_normed - mean_grad - normed * mean_cross)


def gelu_parts(values):
    square = values * values
    half = 0.5 + 0.5 * jnp.tanh(values * (gelu_root + gelu_root * gelu_cubic * square))
    activation = values * half
    slope = half + activation * (1.0 - half) * (
        2.0 * gelu_root + 6.0 * gelu_root * gelu_cubic * square
    )
    return (activation, slope)


def mm(spec, a, b):
    return jnp.einsum(spec, a, b, preferred_element_type=f32)


def swap(value, mask):
    size = lax.axis_size("expert")
    return lax.ppermute(value, "expert", [(i, i ^ mask) for i in range(size)])


def exchange_group(value):
    across = swap(value, 2)
    return value, across, swap(jnp.stack([value, across]), 1)


def gather_group(value):
    value, across, beside = exchange_group(value)
    return jnp.stack([value, beside[0], across, beside[1]])


def reduce_group(send, keep):
    beside = swap(send, 1)
    own = keep[0] + beside[0].astype(f32)
    other = (keep[1] + beside[1].astype(f32)).astype(bf16)
    return own, swap(other, 2)


def dp_swap(value, mask):
    copies = lax.axis_size("dp")
    return lax.ppermute(value, "dp", [(i, i ^ mask) for i in range(copies)])


def pair_swap(value):
    return dp_swap(value, 2)


def side_groups(copies):
    return [[i for i in range(copies) if (i >> 1) % 2 == side] for side in range(2)]


def pair_places(p):
    first = ((p >> 1) << 2) | (p & 1)
    return first, first + 2


def spread(value, *before):
    far = dp_swap(value, 4)
    return [value, dp_swap(tied(value, *before), 1), far, dp_swap(far, 1)]


def collect(send, keep, start, middle, end):
    got = dp_swap(tied(send, *start), 1)
    wide = tied(got, *middle).astype(f32)
    far = dp_swap((keep[1] + wide[1]).astype(bf16), 4)
    return keep[0] + wide[0] + tied(far, *end).astype(f32), got


def tied(value, *others):
    return lax.optimization_barrier((value, *others))[0]


def ring_place(at, copies):
    at = lax.rem(at + copies, copies)
    return jnp.where(at < copies // 2, 2 * at, 2 * (copies - 1 - at) + 1)


def ring_gather(share):
    copies = lax.axis_size("dp")
    if copies > 8:
        whole = lax.all_gather(share, "dp", axis=0)
        whole = whole.reshape((8, copies // 8 * share.shape[0]) + share.shape[1:])
        return [whole[k] for k in range(8)], jnp.arange(8, dtype=jnp.int32)
    half = copies // 2
    ring = [2 * i for i in range(half)] + [2 * i + 1 for i in reversed(range(half))]
    place = lax.axis_index("dp")
    position = jnp.where(lax.rem(place, 2) == 0, place // 2, copies - 1 - place // 2)

    def hop(value, way):
        return lax.ppermute(
            value, "dp", [(ring[i], ring[(i + way) % copies]) for i in range(copies)]
        )

    pieces, offsets = [share], [0]
    right = left = share
    for step in range(1, half + 1):
        right = hop(right, 1)
        pieces.append(right)
        offsets.append(-step)
        if step < half:
            left = hop(left, -1)
            pieces.append(left)
            offsets.append(step)
    return pieces, ring_place(position + jnp.array(offsets, jnp.int32), copies)


def dot(a, b, left=1, right=0):
    return lax.dot_general(
        a, b, (((left,), (right,)), ((), ())), preferred_element_type=f32
    )


def full(shape):
    return pl.BlockSpec(shape, lambda i: (0,) * len(shape), pipeline_mode=pl.Buffered(1))


SCALARS = pl.BlockSpec(memory_space=pltpu.SMEM)


def kernel_call(body, grid, in_specs, out_specs, out_shape, scratch, flops, operands):
    out_bytes = sum(int(o.size) * o.dtype.itemsize for o in out_shape)
    in_bytes = sum(int(o.size) * o.dtype.itemsize for o in operands)
    return pl.pallas_call(
        body,
        grid=(grid,),
        in_specs=in_specs,
        out_specs=out_specs,
        out_shape=out_shape,
        scratch_shapes=scratch,
        compiler_params=pltpu.CompilerParams(vmem_limit_bytes=56 * 2**20),
        cost_estimate=pl.CostEstimate(
            flops=int(flops), bytes_accessed=out_bytes + in_bytes, transcendentals=0
        ),
    )(*operands)


def shape(dims, dtype):
    return jax.ShapeDtypeStruct(dims, dtype)


def prepare(info, proj, qkv, biases, up, down, rup, rdown, keep, group):
    d_rows, width = proj.shape
    cols = width // group
    f_rows = down.shape[0]
    f_own = f_rows // group
    count = up.shape[1] // f_rows
    wide = 3 * cols
    chunks = rup.shape[1] // 2 // width

    def body(info, proj, qkv, *refs):
        biases, (up, down, rup, rdown, first, third, mine, theirs) = (
            refs[: len(biases_in)],
            refs[len(biases_in) :],
        )
        third[d_rows + f_own :, :] = proj[...]
        lines = [
            jnp.concatenate(
                [b[...].astype(f32).reshape(1, -1), jnp.zeros((1, wide - b.shape[0]), f32)], axis=1
            )
            for b in biases[1:]
        ]
        for p in range(group):

            @pl.when(info[8] == p)
            def _():
                own = slice(p * f_own, (p + 1) * f_own)
                first[:d_rows, :] = jnp.concatenate(
                    [qkv[:, i * width + p * cols : i * width + (p + 1) * cols] for i in range(3)],
                    axis=1,
                )
                line = jnp.concatenate(
                    [
                        biases[0][...].astype(f32).reshape(1, -1)[:, own],
                        jnp.zeros((1, wide - f_own), f32),
                    ],
                    axis=1,
                )
                first[d_rows:, :] = jnp.concatenate(
                    [line] + lines + [jnp.zeros((15 - len(lines), wide), f32)], axis=0
                ).astype(bf16)
                third[:d_rows, :] = jnp.concatenate(
                    [
                        up[:, d * f_rows + p * f_own : d * f_rows + (p + 1) * f_own]
                        for d in range(count)
                    ],
                    axis=1,
                )
                third[d_rows : d_rows + f_own, :] = down[own, :]

        one, two = [], []
        for p in range(count // 2):
            at, to = (d * f_rows for d in pair_places(p))
            one += [(at, at + keep), (to, to + f_rows - keep)]
            two += [(to + f_rows - keep, to + f_rows), (at + keep, at + f_rows)]
        for side in range(2):

            @pl.when(info[9] == side)
            def _():
                own, other = (one, two) if side == 0 else (two, one)
                for ref, parts in ((mine, own), (theirs, other)):
                    line = jnp.concatenate([rup[:, low:high] for low, high in parts], axis=1)
                    for c in range(line.shape[1] // width):
                        ref[c * d_rows : (c + 1) * d_rows, :] = line[:, c * width : (c + 1) * width]
                start = side * (f_rows - keep)
                mine[chunks * d_rows :, :] = rdown[start : start + keep, :]
                start = (1 - side) * keep
                theirs[chunks * d_rows :, :] = rdown[start : start + f_rows - keep, :]

    biases_in = biases
    operands = [proj, qkv, *biases, up, down, rup, rdown]
    outs = [
        shape((d_rows + 16, wide), bf16),
        shape((2 * d_rows + f_own, width), bf16),
        shape((chunks * d_rows + keep, width), bf16),
        shape((chunks * d_rows + f_rows - keep, width), bf16),
    ]
    return kernel_call(
        body,
        1,
        [SCALARS] + [full(o.shape) for o in operands],
        [full(o.shape) for o in outs],
        outs,
        [],
        0,
        [info, *operands],
    )


def middle_back(own, got, middle_rows, attn_out, cotangent, mods):
    rows, width = own.shape

    def body(own, got, mid, out, cot, mod, grad_mid, grad_attn, sums):
        grad = own[...] + got[...].astype(f32)
        normed, inv_std = norm_parts(mid[...])
        value = cot[...].astype(f32) + norm_back(
            grad * (1.0 + mod[0, 4:5, :]), normed, inv_std
        )
        grad_mid[...] = value
        grad_attn[...] = (mod[0, 2:3, :] * value).astype(bf16)
        sums[0:1, :] = jnp.sum(value * out[...], axis=0, keepdims=True)
        sums[1:2, :] = jnp.sum(grad, axis=0, keepdims=True)
        sums[2:3, :] = jnp.sum(grad * normed, axis=0, keepdims=True)
        sums[3:, :] = jnp.zeros((5, width), f32)

    operands = [own, got, middle_rows, attn_out, cotangent]
    outs = [shape((rows, width), f32), shape((rows, width), bf16), shape((8, width), f32)]
    return kernel_call(
        body,
        1,
        [full(o.shape) for o in operands] + [pl.BlockSpec((1, 8, width), lambda i: (0, 0, 0))],
        [full(o.shape) for o in outs],
        outs,
        [],
        0,
        [*operands, mods],
    )


def routed_rows(info, up_own, up_got, down_own, down_got, keep):
    d_rows, half = up_got.shape
    f_rows = down_own.shape[0]
    width = down_own.shape[1]
    pairs = half // f_rows

    def body(info, uo, ug, do, dg, up, down):
        for side in range(2):

            @pl.when(info[9] == side)
            def _():
                first, second = (0, 1) if side == 0 else (1, 0)
                values = (uo[:d_rows, :], ug[...].astype(f32))
                for p in range(pairs):
                    at, to = (d * f_rows for d in pair_places(p))
                    for whose, low, high, frm in (
                        (first, at, at + keep, 0),
                        (first, to, to + f_rows - keep, keep),
                        (second, to + f_rows - keep, to + f_rows, 0),
                        (second, at + keep, at + f_rows, keep),
                    ):
                        base = p * f_rows + frm
                        up[:, low:high] = values[whose][:, base : base + high - low]
                start = side * (f_rows - keep)
                down[start : start + keep, :] = do[:keep, :]
                start = (1 - side) * keep
                down[start : start + f_rows - keep, :] = dg[...].astype(f32)

    operands = [up_own, up_got, down_own, down_got]
    outs = [shape((d_rows, 2 * half), f32), shape((f_rows, width), f32)]
    return kernel_call(
        body,
        1,
        [SCALARS] + [full(o.shape) for o in operands],
        [full(o.shape) for o in outs],
        outs,
        [],
        0,
        [info, *operands],
    )


def group_rows_out(info, shared, last, d_rows, f_rows):
    group = 4
    rows, width = shared[0].shape
    f_own = f_rows // group
    cols = width // group
    count = width // f_own

    def body(info, s0, s2, s13, l0, l2, l13, up, down, qkv, proj, shared, last):
        for all_parts, p0, p2, p13 in ((shared, s0, s2, s13), (last, l0, l2, l13)):
            all_parts[0], all_parts[2] = p0[...].astype(f32), p2[...].astype(f32)
            all_parts[1], all_parts[3] = p13[0].astype(f32), p13[1].astype(f32)
        for a in range(group):
            part = shared[info[8] ^ a]
            for d in range(count):
                at = d * f_rows + a * f_own
                up[:, at : at + f_own] = part[:d_rows, d * f_own : (d + 1) * f_own]
            down[a * f_own : (a + 1) * f_own, :] = part[d_rows:, :]
            part = last[info[8] ^ a]
            for i in range(3):
                at = i * width + a * cols
                qkv[:, at : at + cols] = part[:, i * cols : (i + 1) * cols]
            proj[:, a * cols : (a + 1) * cols] = part[:, 3 * cols :]

    outs = [
        shape((d_rows, count * f_rows), f32),
        shape((f_rows, width), f32),
        shape((d_rows, 3 * width), f32),
        shape((d_rows, width), f32),
    ]
    operands = [*shared, *last]
    return kernel_call(
        body,
        1,
        [SCALARS] + [full(o.shape) for o in operands],
        [full(o.shape) for o in outs],
        outs,
        [pltpu.VMEM((group, rows, width), f32), pltpu.VMEM((group, d_rows, width), f32)],
        0,
        [info, *operands],
    )


def front(info, tokens, mods, bias, pieces, rows_piece, cols_own, cut):
    blocks, rows = tokens.shape[0], tokens.shape[1] - 16
    width = 8 * rows_piece
    wide = 3 * cols_own

    def body(info, tok, more, mod, bias, *refs):
        parts = refs[:8]
        (hid, prj, qkv, table, gates, low_grad, slot, sums, lines, units, three, lists) = refs[8:]
        step = pl.program_id(0)

        @pl.when(step == 0)
        def _():
            for k in range(8):
                at = pl.multiple_of(info[k] * rows_piece, rows_piece)
                qkv[pl.ds(at, rows_piece), :] = parts[k][:rows_piece, :]
                if cut:
                    lists[info[k]] = parts[k][rows_piece:, :].astype(f32)
            three[...] = bias[...]
            if cut:
                three[:, :cols_own] = lists[info[8]][2:3, :cols_own]
                three[:, 2 * cols_own :] = lists[info[8] + 4][2:3, :cols_own]
                lines[...] = jnp.zeros_like(lines)
                for d in range(8):
                    at = slice(d * rows_piece, (d + 1) * rows_piece)
                    for i, row in enumerate((0, 3, 4, 5)):
                        lines[i : i + 1, at] = lists[d, row : row + 1, :rows_piece]
                size = units.shape[2]
                for side in range(2):

                    @pl.when(info[9] == side)
                    def _():
                        for p in range(units.shape[0]):
                            one, two = pair_places(p)
                            if side == 0:
                                units[p, :, :cut] = lists[one, 1:2, :cut]
                                units[p, :, cut:] = lists[two, 1:2, : size - cut]
                            else:
                                units[p, :, :cut] = lists[two, 1:2, size - cut : size]
                                units[p, :, cut:] = lists[one, 1:2, cut:size]

            sums[...] = jnp.zeros_like(sums)

        normed, _ = norm_parts(tok[0, :, :width].astype(f32))
        low = (normed * (1.0 + mod[0, 1:2, :]) + mod[0, 0:1, :]).astype(bf16)
        hid[...] = low
        prj[...] = (dot(low, qkv[...]) + three[...]).astype(bf16)

        me = info[8].astype(f32)
        pairs = more[0].astype(f32)
        one = (pairs[0:1, :] == me).astype(f32)
        two = (pairs[1:2, :] == me).astype(f32)
        hot = one + two
        gate = one * (pairs[2:3, :] + pairs[4:5, :] + pairs[6:7, :]) + two * (
            pairs[3:4, :] + pairs[5:6, :] + pairs[7:8, :]
        )
        across = lax.broadcasted_iota(jnp.int32, (rows, rows), 1)
        down = lax.broadcasted_iota(jnp.int32, (rows, rows), 0)
        earlier = (down < across).astype(f32).astype(bf16)
        rank = dot(jnp.broadcast_to(hot, (8, rows)).astype(bf16), earlier)[0:1, :]
        kept = hot * (rank < CAP).astype(f32)
        places = lax.broadcasted_iota(jnp.int32, (CAP, rows), 0).astype(f32)
        placed = jnp.where(rank == places, kept, 0.0)
        table[0] = placed.astype(bf16)
        gates[0] = jnp.sum(jnp.where(down == across, gate, 0.0), axis=1, keepdims=True)
        cot = tok[0, :, width:]
        grad = (mod[0, 5:6, :] * cot.astype(f32)).astype(bf16)
        low_grad[...] = grad
        gate_slot = jnp.sum(placed * gate, axis=1, keepdims=True)
        slot_grad = (gate_slot * (mod[0, 5:6, :] * dot(table[0], cot))).astype(bf16)
        slot[...] = slot_grad
        sums[0:1, :] += jnp.sum(slot_grad.astype(f32), axis=0, keepdims=True)
        sums[1:2, :] += jnp.sum(grad.astype(f32), axis=0, keepdims=True)
        sums[2:3, :] += jnp.broadcast_to(jnp.sum(kept, axis=1, keepdims=True), (1, width))

    return kernel_call(
        body,
        blocks,
        [
            SCALARS,
            pl.BlockSpec((1, rows, 2 * width), lambda i: (i, 0, 0)),
            pl.BlockSpec((1, 16, rows), lambda i: (i, rows // 16, 0)),
            pl.BlockSpec((1, 8, width), lambda i: (i, 0, 0)),
            full((1, wide)),
        ]
        + [full(p.shape) for p in pieces],
        [
            pl.BlockSpec((rows, width), lambda i: (i, 0)),
            pl.BlockSpec((rows, wide), lambda i: (i, 0)),
            full((width, wide)),
            pl.BlockSpec((1, CAP, rows), lambda i: (i, 0, 0)),
            pl.BlockSpec((1, rows, 1), lambda i: (i, 0, 0)),
            pl.BlockSpec((rows, width), lambda i: (i, 0)),
            pl.BlockSpec((CAP, width), lambda i: (i, 0)),
            full((8, width)),
            full((8, width)),
            full((4, 1, width // 2)),
        ],
        [
            shape((blocks * rows, width), bf16),
            shape((blocks * rows, wide), bf16),
            shape((width, wide), bf16),
            shape((blocks, CAP, rows), bf16),
            shape((blocks, rows, 1), f32),
            shape((blocks * rows, width), bf16),
            shape((blocks * CAP, width), bf16),
            shape((8, width), f32),
            shape((8, width), f32),
            shape((4, 1, width // 2), f32),
        ],
        [pltpu.VMEM((1, wide), f32), pltpu.VMEM((8, 16, wide), f32)],
        2 * blocks * rows * width * wide,
        [info, tokens, tokens, mods, bias, *pieces],
    )


def to_rows(own, got, bias, table, gates, addend, tokens, line):
    blocks, cap, rows = table.shape
    width = own.shape[1]

    def body(own, got, bias, tab, *refs):
        gate, (add, tok, line, send, keep, sums) = refs[:-6], refs[-6:]
        slots = (own[...] + got[...].astype(f32) + bias[...]).astype(bf16)
        value = dot(tab[0], slots, 0, 0)
        value = add[...] + (gate[0][0] * value if gate else value)
        first = (pl.program_id(0) == 0).astype(f32)
        sums[0] = jnp.sum(
            tok[0].astype(f32) * (value + first * line[...]), axis=0, keepdims=True
        )
        for k in range(blocks):

            @pl.when(pl.program_id(0) == k)
            def _():
                if k % 2 == 1:
                    send[k // 2] = value.astype(bf16)
                else:
                    keep[k // 2] = value

    operands = [own, got, bias, table, *gates, addend, tokens, line]
    return kernel_call(
        body,
        blocks,
        [
            pl.BlockSpec((cap, width), lambda i: (i, 0)),
            pl.BlockSpec((cap, width), lambda i: (i, 0)),
            full((1, width)),
            pl.BlockSpec((1, cap, rows), lambda i: (i, 0, 0)),
        ]
        + [pl.BlockSpec((1, rows, 1), lambda i: (i, 0, 0))] * len(gates)
        + [
            pl.BlockSpec((rows, width), lambda i: (i, 0)),
            pl.BlockSpec((1, rows, width), lambda i: (i, 0, 1)),
            full((1, width)),
        ],
        [
            full((2, rows, width)),
            full((2, rows, width)),
            pl.BlockSpec((1, 1, width), lambda i: (i, 0, 0)),
        ],
        [
            shape((2, rows, width), bf16),
            shape((2, rows, width), f32),
            shape((blocks, 1, width), f32),
        ],
        [],
        2 * blocks * rows * width * cap,
        operands,
    )


def score_parts(info, query, key, blocks, rows):
    own = info[10 + pl.program_id(0)]
    lanes = lax.broadcasted_iota(jnp.int32, (1, blocks * rows), 1) // rows
    seen = jnp.zeros((1, blocks * rows), jnp.int32)
    for j in range(blocks):
        seen = jnp.where((lanes == j) & (info[10 + j] == own), 1, seen)
    scores = dot(query * bf16(HEAD_DIM ** (-0.5)), key, 1, 1)
    masked = jnp.where(seen == 1, scores, -1e30)
    exponent = jnp.exp(masked - jnp.max(masked, axis=-1, keepdims=True))
    return exponent * (1.0 / jnp.sum(exponent, axis=-1, keepdims=True))


def attention(info, projected, blocks, cols_own):
    total, wide = projected.shape
    rows = total // blocks

    def body(info, own, every, out):
        for h in range(cols_own // HEAD_DIM):
            q = slice(h * HEAD_DIM, (h + 1) * HEAD_DIM)
            k = slice(cols_own + h * HEAD_DIM, cols_own + (h + 1) * HEAD_DIM)
            v = slice(2 * cols_own + h * HEAD_DIM, 2 * cols_own + (h + 1) * HEAD_DIM)
            probs = score_parts(info, own[:, q], every[:, k], blocks, rows)
            out[:, q] = dot(probs.astype(bf16), every[:, v]).astype(bf16)

    return kernel_call(
        body,
        blocks,
        [SCALARS, pl.BlockSpec((rows, wide), lambda i: (i, 0)), full((total, wide))],
        [pl.BlockSpec((rows, cols_own), lambda i: (i, 0))],
        [shape((total, cols_own), bf16)],
        [],
        4 * total * total * cols_own,
        [info, projected, projected],
    )[0]


def attention_back(info, projected, grad_attn, proj_rel, blocks, cols_own):
    total, wide = projected.shape
    rows = total // blocks
    width = grad_attn.shape[1]
    scale = HEAD_DIM ** (-0.5)

    def body(info, own, every, grad, rel, out, sums_k, sums_v, sums_q):
        step = pl.program_id(0)

        @pl.when(step == 0)
        def _():
            sums_k[...] = jnp.zeros_like(sums_k)
            sums_v[...] = jnp.zeros_like(sums_v)

        back = dot(grad[...], rel[...], 1, 1).astype(bf16)
        for h in range(cols_own // HEAD_DIM):
            q = slice(h * HEAD_DIM, (h + 1) * HEAD_DIM)
            k = slice(cols_own + h * HEAD_DIM, cols_own + (h + 1) * HEAD_DIM)
            v = slice(2 * cols_own + h * HEAD_DIM, 2 * cols_own + (h + 1) * HEAD_DIM)
            probs = score_parts(info, own[:, q], every[:, k], blocks, rows)
            grad_probs = dot(back[:, q], every[:, v], 1, 1)
            inner = jnp.sum(probs * grad_probs, axis=-1, keepdims=True)
            scores = (probs * (grad_probs - inner)).astype(bf16)
            at = pl.multiple_of(step * rows, rows)
            sums_q[pl.ds(at, rows), q] = dot(scores, every[:, k]) * scale
            sums_k[:, q] += dot(scores, own[:, q], 0, 0)
            sums_v[:, q] += dot(probs.astype(bf16), back[:, q], 0, 0)

        @pl.when(step == blocks - 1)
        def _():
            out[:, :cols_own] = sums_q[...].astype(bf16)
            out[:, cols_own : 2 * cols_own] = (sums_k[...] * scale).astype(bf16)
            out[:, 2 * cols_own :] = sums_v[...].astype(bf16)

    return kernel_call(
        body,
        blocks,
        [
            SCALARS,
            pl.BlockSpec((rows, wide), lambda i: (i, 0)),
            full((total, wide)),
            pl.BlockSpec((rows, width), lambda i: (i, 0)),
            full((cols_own, width)),
        ],
        [full((total, wide))],
        [shape((total, wide), bf16)],
        [pltpu.VMEM((total, cols_own), f32)] * 3,
        10 * total * total * cols_own + 2 * total * width * cols_own,
        [info, projected, projected, grad_attn, proj_rel],
    )[0]


def middle(info, tokens, mods, heads, pieces, proj_bias, table, rows_piece):
    blocks, rows = tokens.shape[0], tokens.shape[1] - 16
    width = 8 * rows_piece
    cols = width // blocks
    cap = table.shape[1]

    def body(info, tok, mod, h0, h1, h2, h3, bias, tab, *refs):
        parts, (hid, att, buf, out0, mid0, own, rel) = refs[:8], refs[8:]

        @pl.when(pl.program_id(0) == 0)
        def _():
            for k in range(8):
                place = info[18 + k]
                at = ((place >> 1) ^ info[8]) * cols + (place & 1) * rows_piece
                at = pl.multiple_of(at, rows_piece)
                rel[pl.ds(at, rows_piece), :] = parts[k][2 * rows_piece :, :]
            own[...] = rel[:cols, :]

        attended = jnp.concatenate([h0[...], h1[...], h2[...], h3[...]], axis=1)
        att[...] = attended
        out = dot(attended, rel[...]) + bias[...]
        mid = tok[0].astype(f32) + mod[0, 2:3, :] * out
        normed, _ = norm_parts(mid)
        low = (normed * (1.0 + mod[0, 4:5, :]) + mod[0, 3:4, :]).astype(bf16)
        hid[...] = low
        buf[...] = dot(tab[0], low).astype(bf16)

        @pl.when(pl.program_id(0) == 0)
        def _():
            out0[...] = out
            mid0[...] = mid

    return kernel_call(
        body,
        blocks,
        [
            SCALARS,
            pl.BlockSpec((1, rows, width), lambda i: (i, 0, 0)),
            pl.BlockSpec((1, 8, width), lambda i: (i, 0, 0)),
            pl.BlockSpec((rows, cols), lambda i: (i, 0)),
            pl.BlockSpec((rows, cols), lambda i: (i ^ 1, 0)),
            pl.BlockSpec((rows, cols), lambda i: (i ^ 2, 0)),
            pl.BlockSpec((rows, cols), lambda i: (i ^ 3, 0)),
            full((1, width)),
            pl.BlockSpec((1, cap, rows), lambda i: (i, 0, 0)),
        ]
        + [full(p.shape) for p in pieces],
        [
            pl.BlockSpec((rows, width), lambda i: (i, 0)),
            pl.BlockSpec((rows, width), lambda i: (i, 0)),
            pl.BlockSpec((cap, width), lambda i: (i, 0)),
            full((rows, width)),
            full((rows, width)),
            full((cols, width)),
        ],
        [
            shape((blocks * rows, width), bf16),
            shape((blocks * rows, width), bf16),
            shape((blocks * cap, width), bf16),
            shape((rows, width), f32),
            shape((rows, width), f32),
            shape((cols, width), bf16),
        ],
        [pltpu.VMEM((width, width), bf16)],
        2 * blocks * rows * width * (width + cap),
        [info, tokens, mods, *heads, proj_bias, table, *pieces],
    )


def shared_expert(info, hidden, grad, bias, pieces, rows_piece, blocks, paired):
    total, width = hidden.shape
    rows = total // blocks
    pairs = 4
    sums_mine = (pairs, 2 * rows_piece, width) if paired else (2, width, width)
    sums_theirs = (pairs, 2 * rows_piece, width) if paired else (1, 8, width)

    def body(info, hid, gcl, bias, *refs):
        parts, (out, back, mine, theirs, line, up, down, up_sum, down_sum, wide) = refs[:8], refs[8:]
        step = pl.program_id(0)

        @pl.when(step == 0)
        def _():
            for k in range(8):
                at = pl.multiple_of(info[18 + k] * rows_piece, rows_piece)
                up[pl.ds(at, rows_piece), :] = parts[k][:rows_piece, :]
                down[pl.ds(at, rows_piece), :] = parts[k][rows_piece : 2 * rows_piece, :]
            up_sum[...] = jnp.zeros_like(up_sum)
            down_sum[...] = jnp.zeros_like(down_sum)
            wide[...] = jnp.zeros_like(wide)

        act, slope = gelu_parts(dot(hid[...], up[...]) + bias[...])
        low = act.astype(bf16)
        out[...] = dot(low, down[...])
        down_sum[...] += dot(low, gcl[...], 0, 0)
        grad_pre = dot(gcl[...], down[...], 1, 1) * slope
        grad_low = grad_pre.astype(bf16)
        wide[...] += jnp.sum(grad_low.astype(f32), axis=0, keepdims=True)
        up_sum[...] += dot(hid[...], grad_low, 0, 0)
        back[...] = dot(grad_low, up[...], 1, 1)

        @pl.when(step == blocks - 1)
        def _():
            line[...] = wide[...]
            if not paired:
                mine[0], mine[1] = up_sum[...], down_sum[...]
            for p in range(pairs if paired else 0):
                at = pl.multiple_of(info[18 + 2 * p] * rows_piece, rows_piece)
                far = pl.multiple_of(info[19 + 2 * p] * rows_piece, rows_piece)
                mine[p, :rows_piece, :] = up_sum[pl.ds(at, rows_piece), :]
                mine[p, rows_piece:, :] = down_sum[pl.ds(at, rows_piece), :]
                theirs[p, :rows_piece, :] = up_sum[pl.ds(far, rows_piece), :].astype(bf16)
                theirs[p, rows_piece:, :] = down_sum[pl.ds(far, rows_piece), :].astype(bf16)

    return kernel_call(
        body,
        blocks,
        [
            SCALARS,
            pl.BlockSpec((rows, width), lambda i: (i, 0)),
            pl.BlockSpec((rows, width), lambda i: (i, 0)),
            full((1, width)),
        ]
        + [full(p.shape) for p in pieces],
        [
            pl.BlockSpec((rows, width), lambda i: (i, 0)),
            pl.BlockSpec((rows, width), lambda i: (i, 0)),
            full(sums_mine),
            full(sums_theirs),
            full((1, width)),
        ],
        [
            shape((total, width), f32),
            shape((total, width), f32),
            shape(sums_mine, f32),
            shape(sums_theirs, bf16),
            shape((1, width), f32),
        ],
        [
            pltpu.VMEM((width, width), bf16),
            pltpu.VMEM((width, width), bf16),
            pltpu.VMEM((width, width), f32),
            pltpu.VMEM((width, width), f32),
            pltpu.VMEM((1, width), f32),
        ],
        12 * total * width * width,
        [info, hidden, grad, bias, *pieces],
    )


def routed_rows_grads(info, buffers, slots, own, other, bias):
    pairs, _, units = bias.shape
    count, width = buffers[0].shape
    piece = width // (2 * pairs)
    every = pairs * units
    chunks = every // width
    cut = own[0].shape[0] - chunks * piece

    def body(info, b0, b1, s0, s1, *refs):
        packs, bias = (refs[:4], refs[4:8]), refs[8]
        (g0, g1, e0, e1, line, act_low, grad_low, bs, ss, up, down, gsum, esum) = refs[9:]
        step = pl.program_id(0)

        @pl.when(step == 0)
        def _():
            for r in range(pairs):
                for j in range(2):
                    at = pl.multiple_of(info[18 + 2 * r + j] * piece, piece)
                    for c in range(chunks):
                        up[pl.ds(at, piece), c * width : (c + 1) * width] = packs[j][r][
                            c * piece : (c + 1) * piece, :
                        ]
                    at = info[14 + r] * units + j * cut
                    at = pl.multiple_of(at, 128)
                    size = units - cut if j else cut
                    down[pl.ds(at, size), :] = packs[j][r][chunks * piece :, :]
            bs[:count, :], bs[count:, :] = b0[...], b1[...]
            ss[:count, :], ss[count:, :] = s0[...], s1[...]
            gsum[...] = jnp.zeros_like(gsum)
            esum[...] = jnp.zeros_like(esum)

        at = pl.multiple_of(step * units, 128)
        w_up = up[:, pl.ds(at, units)]
        w_down = down[pl.ds(at, units), :]
        act, slope = gelu_parts(dot(bs[...], w_up) + bias[step])
        low = act.astype(bf16)
        act_low[...] = low
        esum[...] += dot(low, w_down)
        grad = (dot(ss[...], w_down, 1, 1) * slope).astype(bf16)
        grad_low[...] = grad
        line[0] = jnp.sum(grad.astype(f32), axis=0, keepdims=True)
        gsum[...] += dot(grad, w_up, 1, 1)

        @pl.when(step == pairs - 1)
        def _():
            g0[...] = gsum[:count, :]
            g1[...] = gsum[count:, :].astype(bf16)
            e0[...] = esum[:count, :]
            e1[...] = esum[count:, :].astype(bf16)

    outs = [
        shape((count, width), f32),
        shape((count, width), bf16),
        shape((count, width), f32),
        shape((count, width), bf16),
        shape((pairs, 1, units), f32),
        shape((2 * count, every), bf16),
        shape((2 * count, every), bf16),
        shape((2 * count, width), bf16),
        shape((2 * count, width), bf16),
    ]
    operands = [*buffers, *slots, *own, *other, bias]
    by_step = pl.BlockSpec((2 * count, units), lambda i: (0, i))
    return kernel_call(
        body,
        pairs,
        [SCALARS] + [full(o.shape) for o in operands],
        [full(o.shape) for o in outs[:4]]
        + [pl.BlockSpec((1, 1, units), lambda i: (i, 0, 0)), by_step, by_step]
        + [full(o.shape) for o in outs[7:]],
        outs,
        [
            pltpu.VMEM((width, every), bf16),
            pltpu.VMEM((every, width), bf16),
            pltpu.VMEM((2 * count, width), f32),
            pltpu.VMEM((2 * count, width), f32),
        ],
        16 * count * width * every,
        [info, *operands],
    )


def routed_weight_grads(info, act_low, grad_low, rows, slots, pairs):
    total, width = rows.shape
    every = act_low.shape[1]
    units = every // pairs
    piece = width // (2 * pairs)

    def body(info, act, grad, bs, ss, ds, dk, us, uk, values):
        step = pl.program_id(0)
        slot = step ^ info[14]
        at = pl.multiple_of(step * units, 128)
        rdown = dot(act[...], ss[...], 0, 0)
        values[...] = dot(bs[...], grad[...], 0, 0)
        for r in range(pairs):
            for j in range(2):
                row = pl.multiple_of(info[18 + 2 * r + j] * piece, piece)
                value = values[pl.ds(row, piece), :]
                if r % 2 == 1:
                    us[r // 2, j * piece : (j + 1) * piece, pl.ds(at, units)] = value.astype(bf16)
                else:
                    uk[r // 2, j * piece : (j + 1) * piece, pl.ds(at, units)] = value

            @pl.when(slot == r)
            def _():
                if r % 2 == 1:
                    ds[r // 2] = rdown.astype(bf16)
                else:
                    dk[r // 2] = rdown

    outs = [
        shape((2, units, width), bf16),
        shape((2, units, width), f32),
        shape((2, 2 * piece, every), bf16),
        shape((2, 2 * piece, every), f32),
    ]
    operands = [act_low, grad_low, rows, slots]
    return kernel_call(
        body,
        pairs,
        [SCALARS]
        + [pl.BlockSpec((total, units), lambda i: (0, i))] * 2
        + [full(o.shape) for o in operands[2:]],
        [full(o.shape) for o in outs],
        outs,
        [pltpu.VMEM((width, units), f32)],
        4 * total * width * every,
        [info, *operands],
    )


def tail_grads(info, tokens, hidden, grads, attended, grad_attn, qkv):
    total, width = hidden.shape
    wide = grads.shape[1]
    blocks, rows = tokens.shape[0], tokens.shape[1] - 16
    cols = width // blocks
    piece = width // 8

    def body(info, tok, hid, gr, att, ga, qkv, away, stay, send, keep, sums, lines, proj, wq):
        wq[...] = dot(hid[...], gr[...], 0, 0)
        for m in range(blocks):
            these = slice(m * rows, (m + 1) * rows)
            grad = dot(gr[these, :], qkv[...], 1, 1)
            if m % 2 == 1:
                send[m // 2] = grad.astype(bf16)
            else:
                keep[m // 2] = grad
            normed, _ = norm_parts(tok[m].astype(f32))
            sums[m : m + 1, :] = jnp.sum(grad, axis=0, keepdims=True)
            sums[blocks + m : blocks + m + 1, :] = jnp.sum(grad * normed, axis=0, keepdims=True)
        lines[:, :wide] = jnp.sum(gr[...].astype(f32), axis=0, keepdims=True)
        lines[:, wide:] = jnp.sum(ga[...].astype(f32), axis=0, keepdims=True)
        own = ga[:, :cols]
        for k in range(1, blocks):
            own = jnp.where(info[8] == k, ga[:, k * cols : (k + 1) * cols], own)
        proj[...] = dot(att[...], own, 0, 0)
        for k in range(8):
            place = info[18 + k]
            at = pl.multiple_of(place * piece, piece)
            value = wq[pl.ds(at, piece), :]
            at = pl.multiple_of(((place >> 1) ^ info[8]) * cols + (place & 1) * piece, piece)
            other = proj[pl.ds(at, piece), :]
            i = k % 2 + 2 * (k // 4)
            if k // 2 % 2 == 1:
                away[i, :, :wide] = value.astype(bf16)
                away[i, :, wide:] = other.astype(bf16)
            else:
                stay[i, :, :wide] = value
                stay[i, :, wide:] = other

    return kernel_call(
        body,
        1,
        [SCALARS, pl.BlockSpec((blocks, rows, width), lambda i: (0, 0, 0))]
        + [full((total, width)), full((total, wide)), full((total, width))]
        + [full((total, width)), full((width, wide))],
        [
            full((4, piece, width)),
            full((4, piece, width)),
            full((2, rows, width)),
            full((2, rows, width)),
            full((2 * blocks, width)),
            full((1, wide + width)),
        ],
        [
            shape((4, piece, width), bf16),
            shape((4, piece, width), f32),
            shape((2, rows, width), bf16),
            shape((2, rows, width), f32),
            shape((2 * blocks, width), f32),
            shape((1, wide + width), f32),
        ],
        [pltpu.VMEM((width, cols), f32), pltpu.VMEM((width, wide), f32)],
        2 * total * width * (2 * wide + cols),
        [info, tokens, hidden, grads, attended, grad_attn, qkv],
    )


def in_order(relative, position):
    return jnp.stack(
        [
            lax.dynamic_index_in_dim(relative, position ^ a, 0, keepdims=False)
            for a in range(relative.shape[0])
        ]
    )


def body(
    tokens,
    conditioning,
    routes,
    gate_weights,
    image_counts,
    image_lengths,
    cotangent,
    qkv_weight,
    qv_bias,
    proj_weight,
    proj_bias,
    ada_weight,
    ada_bias,
    up_weight,
    up_bias,
    down_weight,
    down_bias,
    routed_up,
    routed_upbias,
    routed_down,
    routed_downbias,
):
    group = lax.axis_size("expert")
    copies = lax.axis_size("dp")
    position = lax.axis_index("expert")
    place = lax.axis_index("dp")
    rows, width = tokens.shape
    group_rows = group * rows
    heads_own = HEADS // group
    cols_own = heads_own * HEAD_DIM
    d_rows = qkv_weight.shape[0]
    f_rows = down_weight.shape[0]
    f_own = f_rows // group
    hidden_units = f_rows * copies
    quarter = hidden_units // group
    side = lax.rem(place // 2, 2)
    first_side = side == 0
    pairs_count = copies // 2
    keep = f_rows * 2 // 3
    send = f_rows - keep
    half_units = hidden_units // 2

    def my_units(value):
        one, two = [], []
        for p in range(pairs_count):
            at, to = (d * f_rows for d in pair_places(p))
            one += [value[..., at : at + keep], value[..., to : to + send]]
            two += [value[..., to + send : to + f_rows], value[..., at + keep : at + f_rows]]
        one, two = jnp.concatenate(one, axis=-1), jnp.concatenate(two, axis=-1)
        return jnp.where(first_side, one, two), jnp.where(first_side, two, one)

    def from_units(mine, theirs):
        one = jnp.where(first_side, mine, theirs)
        two = jnp.where(first_side, theirs, mine)
        out = [None] * copies
        for p in range(pairs_count):
            at = f_rows * p
            first, second = pair_places(p)
            out[first] = [one[..., at : at + keep], two[..., at + keep : at + f_rows]]
            out[second] = [one[..., at + keep : at + f_rows], two[..., at : at + keep]]
        out = sum(out, [])
        return jnp.concatenate(out, axis=-1)

    bias_list = [up_bias, routed_upbias[0], qv_bias, proj_bias, down_bias, routed_downbias[0]]
    if copies == 8:
        first_share, third_share, routed_mine, routed_theirs = prepare(
            jnp.stack([position] * 9 + [side]).astype(jnp.int32),
            proj_weight,
            qkv_weight,
            bias_list,
            up_weight,
            down_weight,
            routed_up[0],
            routed_down[0],
            keep,
            group,
        )
    else:
        qkv_share = lax.dynamic_index_in_dim(
            qkv_weight.reshape(d_rows, 3, group, cols_own), position, 2, keepdims=False
        ).reshape(d_rows, 3 * cols_own)
        first_share = qkv_share
        up_share = lax.dynamic_index_in_dim(
            up_weight.reshape(d_rows, copies, group, f_own), position, 2, keepdims=False
        ).reshape(d_rows, quarter)
        down_share = lax.dynamic_slice_in_dim(down_weight, position * f_own, f_own, axis=0)
        third_share = jnp.concatenate([up_share, down_share, proj_weight], axis=0)
        rup_mine, rup_theirs = my_units(routed_up[0])
        rdown_mine = lax.dynamic_slice_in_dim(routed_down[0], side * send, keep, axis=0)
        rdown_theirs = lax.dynamic_slice_in_dim(routed_down[0], (1 - side) * keep, send, axis=0)
        rup_got = pair_swap(rup_theirs)
        rdown_got = pair_swap(rdown_theirs)
    first, order = ring_gather(first_share)
    bias_three = jnp.zeros((1, 3 * cols_own), f32)
    if copies > 8:
        upb, rupb, qvb, projb, downb, rdownb = (
            lax.all_gather(b, "dp", axis=0, tiled=True).astype(f32) for b in bias_list
        )
        upb_own = lax.dynamic_index_in_dim(
            upb.reshape(copies, group, f_own), position, 1, keepdims=False
        ).reshape(quarter)
        bias_lines = jnp.stack([upb_own, projb, downb, rdownb])
        rupb_own = my_units(rupb)[0].reshape(4, 1, half_units // 4)
        bias_three = jnp.concatenate(
            [
                lax.dynamic_slice_in_dim(qvb, position * cols_own, cols_own),
                jnp.zeros((cols_own,), f32),
                lax.dynamic_slice_in_dim(qvb, width + position * cols_own, cols_own),
            ]
        )[None]

    pair_steps = jnp.arange(4, dtype=jnp.int32)
    if copies == 8:
        third_swap, routed_swap = pair_swap(third_share), pair_swap(routed_theirs)
        third_own = spread(third_share, *first[5:7])
        third_got = spread(third_swap, *first[5:7])
        routed_own = spread(tied(routed_mine, third_got[2]), *first[5:7])
        routed_got = spread(tied(routed_swap, third_got[2]), *first[5:7])
        third = [v for pair in zip(third_own, third_got) for v in pair]
        dues = [(*first[1:3], third_swap), (*first[3:5], third_own[2]), (*first[5:7], routed_swap), (third_got[2],), (third_own[3],), (), (routed_own[2],), (routed_own[3], routed_got[1])]
        pair_now = (place >> 2) * 2 + (place & 1)
        unit_blocks = pair_now ^ pair_steps
        masks = jnp.array([0, 2, 1, 3, 4, 6, 5, 7], jnp.int32)
        row_blocks = place ^ masks
    else:
        groups = side_groups(copies)
        whole = lax.all_gather(third_share, "dp", axis=0)
        third = jnp.concatenate(
            [
                whole[:, :d_rows].reshape(8, -1, width),
                whole[:, d_rows : d_rows + f_own].reshape(8, -1, width),
                whole[:, d_rows + f_own :].reshape(8, -1, width),
            ],
            axis=1,
        ).reshape(4, 2, -1, width)
        sided = jnp.where(
            first_side, jnp.stack([rup_mine, rup_got]), jnp.stack([rup_got, rup_mine])
        )
        ups = lax.all_gather(sided, "dp", axis=0, axis_index_groups=groups)
        ups = ups.reshape(pairs_count // 2, 2, 2, d_rows, half_units).transpose(0, 2, 1, 3, 4)
        ups = ups.reshape(4, 2, width // 8, half_units)
        downs = lax.all_gather(
            jnp.concatenate([rdown_mine, rdown_got]), "dp", axis=0, axis_index_groups=groups
        ).reshape(4, half_units // 4, width)
        third = [third[r, j] for r in range(4) for j in range(2)]
        cut = keep * half_units // (4 * f_rows)

        def packs(j, low, high):
            return [
                jnp.concatenate(
                    [ups[r, j, :, c : c + width] for c in range(0, half_units, width)]
                    + [downs[r, low:high]]
                )
                for r in range(4)
            ]

        routed_own, routed_got = packs(0, 0, cut), packs(1, cut, half_units // 4)
        dues = [()] * 8
        unit_blocks = pair_steps
        row_blocks = jnp.arange(8, dtype=jnp.int32)

    def by_side(whole):
        out = whole.reshape(pairs_count // 2, 2, 2, d_rows, -1).transpose(1, 0, 2, 3, 4)
        return out.reshape(2, 4, width // 8, -1)

    gates_left, gate_parts = gate_weights.T, []
    for _ in range(3):
        part = lax.reduce_precision(gates_left, 8, 7)
        gate_parts.append(part.astype(bf16))
        gates_left = gates_left - part
    under = jnp.concatenate([routes.T.astype(bf16), *gate_parts], axis=0)
    under = jnp.pad(under, ((0, 8), (0, 2 * width - rows)))
    both = gather_group(
        jnp.concatenate([jnp.concatenate([tokens, cotangent], axis=1), under], axis=0)
    )

    lengths = image_lengths[0]
    image_total = image_counts[0]
    slots = lengths.shape[0]
    slot_ids = jnp.arange(slots, dtype=jnp.int32)
    starts = jnp.sum(
        jnp.where(slot_ids[None, :] < slot_ids[:, None], lengths[None, :], 0), axis=1
    )
    live = (slot_ids >= 1) & (slot_ids < image_total)
    block_ids = position ^ jnp.arange(group, dtype=jnp.int32)
    segment = jnp.sum(
        (live[None, :] & (starts[None, :] <= (block_ids * rows)[:, None])).astype(jnp.int32),
        axis=1,
    )
    block_hot = segment[:, None] == slot_ids[None, :]

    info = jnp.concatenate(
        [
            order,
            jnp.stack([position, side]),
            segment,
            unit_blocks,
            row_blocks,
            jnp.zeros((6,), jnp.int32),
        ]
    ).astype(jnp.int32)

    cond_value = conditioning[0].astype(f32)
    cond_act = jax.nn.silu(cond_value).astype(bf16)
    act_parts = lax.all_to_all(
        cond_act.reshape(slots, copies, d_rows).transpose(1, 0, 2),
        "dp",
        split_axis=0,
        concat_axis=0,
        tiled=True,
    ).reshape(copies * slots, d_rows)
    mod_width = ada_weight.shape[1]
    mod_own = mod_width // group
    bias_line = lax.dynamic_update_slice(
        jnp.zeros((mod_width,), f32), ada_bias.astype(f32), (place * ada_bias.shape[0],)
    )
    ada_own = lax.dynamic_slice_in_dim(ada_weight, position * mod_own, mod_own, axis=1)
    bias_own = lax.dynamic_slice_in_dim(bias_line, position * mod_own, mod_own)
    mod_parts = (mm("sd,dm->sm", tied(act_parts, *dues[0]), ada_own) + bias_own[None]).reshape(
        copies, slots, mod_own
    )
    mod_got = lax.all_to_all(mod_parts, "dp", split_axis=0, concat_axis=0, tiled=True)
    mod_sum = jnp.sum(tied(mod_got, *dues[1]), axis=0)
    mod_across = tied(swap(mod_sum, 2), *dues[2])
    mod_beside = swap(jnp.stack([mod_sum, mod_across]), 1)
    mod_group = jnp.stack([mod_sum, mod_beside[0], mod_across, mod_beside[1]])
    modulation = in_order(mod_group, position).transpose(1, 0, 2).reshape(slots, mod_width)
    per_block = jnp.sum(
        jnp.where(block_hot[:, :, None], modulation[None, :, :], 0.0), axis=1
    )
    mods = jnp.pad(per_block.reshape(group, 6, width), ((0, 0), (0, 2), (0, 0)))
    shift_a, scale_a, gate_a, shift_b, scale_b, gate_b = (mods[0, i : i + 1] for i in range(6))

    (
        hidden_a,
        projected,
        qkv_own,
        table,
        gates,
        grad_comb_low,
        slot_own,
        sums_f,
        lines_got,
        units_got,
    ) = front(
        info,
        both,
        tied(mods, *dues[3]),
        bias_three,
        first,
        width // 8,
        cols_own,
        keep if copies == 8 else 0,
    )
    if copies == 8:
        bias_lines, rupb_own = lines_got, units_got
    upb_line, projb_line, downb_line, rdownb_line = (bias_lines[i : i + 1] for i in range(4))
    slot_got = pair_swap(slot_own)
    heads_0 = attention(info, tied(projected, *dues[4]), group, cols_own)
    heads_0 = tied(heads_0, *dues[5])
    heads_2 = swap(heads_0, 2)
    heads_1 = swap(heads_0, 1)
    heads_3 = swap(heads_2, 1)
    hidden_b, attended, buffer_own, attn_out, residual_mid, proj_own = middle(
        info,
        both,
        mods,
        (heads_0, heads_1, heads_2, heads_3),
        third,
        projb_line,
        tied(table, slot_got, *dues[6]),
        width // 8,
    )
    buffer_got = pair_swap(buffer_own)

    shared_parts, shared_back, shared_mine, shared_theirs, upbias_line = shared_expert(
        info, tied(hidden_b, *dues[7]), grad_comb_low, upb_line, third, width // 8, group, copies == 8
    )
    if copies != 8:
        sided = jnp.concatenate([by_side(shared_mine[0]), by_side(shared_mine[1])], axis=2)
        shared_mine, shared_theirs = (
            lax.dynamic_index_in_dim(sided, which, 0, keepdims=False) for which in (side, 1 - side)
        )
        shared_theirs = shared_theirs.astype(bf16)
    shared_back_got = pair_swap(shared_theirs)
    (
        back_own,
        back_theirs,
        out_own,
        out_theirs,
        units_sum,
        act_low,
        grad_low,
        both_rows,
        both_slots,
    ) = routed_rows_grads(
        info,
        (tied(buffer_own, shared_theirs), buffer_got),
        (slot_own, slot_got),
        routed_own,
        routed_got,
        rupb_own,
    )
    shared_sums = shared_mine + shared_back_got.astype(f32)
    shared_send = jnp.stack([shared_sums[1], shared_sums[3]]).astype(bf16)
    down_send, down_keep, up_send, up_keep = routed_weight_grads(
        info, tied(act_low, shared_send), grad_low, both_rows, both_slots, 4
    )
    if copies == 8:
        shared_first = dp_swap(shared_send, 1)
        shared_near = shared_sums[0] + shared_first[0].astype(f32)
        shared_far = dp_swap((shared_sums[2] + shared_first[1].astype(f32)).astype(bf16), 4)
        down_first = dp_swap(down_send, 1)
        due_rows = (down_send, shared_first)
        due_back = (down_first, shared_far)
    else:
        due_rows, due_back = (down_send,), ()
    units_sum = units_sum.reshape(pairs_count, f_rows)
    blank = jnp.zeros((pairs_count, f_rows), f32)
    units_one = jnp.where(first_side, units_sum, blank)
    units_two = jnp.where(first_side, blank, units_sum)
    units_by_place = jnp.stack(
        [
            jnp.concatenate([units_one[:, :keep], units_two[:, keep:]], axis=1),
            jnp.concatenate([units_one[:, keep:], units_two[:, :keep]], axis=1),
        ]
    )
    units_by_place = units_by_place.reshape(2, pairs_count // 2, 2, f_rows).transpose(1, 0, 2, 3)
    expert_line = jnp.concatenate(
        [
            units_by_place.reshape(copies, f_rows),
            upbias_line.reshape(copies, f_own),
            sums_f[0].reshape(copies, d_rows),
            sums_f[1].reshape(copies, d_rows),
        ],
        axis=1,
    )
    zero_line = jnp.zeros((1, width), f32)
    rows_send, rows_keep, _ = to_rows(
        tied(back_own, *due_rows),
        pair_swap(back_theirs),
        zero_line,
        table,
        (),
        shared_back,
        both,
        zero_line,
    )
    back_near, back_got = reduce_group(rows_send, rows_keep)
    grad_mid, grad_attn_own, sums_b = middle_back(
        tied(back_near, *due_back), back_got, residual_mid, attn_out, cotangent, mods
    )
    attn_2 = swap(grad_attn_own, 2)
    grad_attn = jnp.concatenate(
        [grad_attn_own, swap(grad_attn_own, 1), attn_2, swap(attn_2, 1)]
    )

    grad_projected = attention_back(info, projected, grad_attn, proj_own, group, cols_own)
    out_got = pair_swap(out_theirs)
    due_tail = (out_got,)
    if copies == 8:
        down_far = dp_swap((down_keep[1] + down_first[1].astype(f32)).astype(bf16), 4)
        up_first = dp_swap(tied(up_send, down_first), 1)
        due_tail = (down_far, up_first)
    away, stay, back_send, back_keep, sums_a, lines = tail_grads(
        info, both, tied(hidden_a, *due_tail), grad_projected, attended, grad_attn, qkv_own
    )

    if copies == 8:
        up_far = dp_swap((up_keep[1] + up_first[1].astype(f32)).astype(bf16), 4)
        shared_rows = shared_near + shared_far.astype(f32)
        rdown_sums = down_keep[0] + down_first[0].astype(f32) + down_far.astype(f32)
        rup_sums = up_keep[0] + up_first[0].astype(f32) + up_far.astype(f32)
        last_first = stay + dp_swap(away, 1).astype(f32)
        last_second = last_first[:2] + dp_swap(last_first[2:].astype(bf16), 4).astype(f32)
    else:

        def scatter(value, each):
            return lax.psum_scatter(
                value.reshape(pairs_count, each, -1).astype(bf16),
                "dp",
                scatter_dimension=0,
                axis_index_groups=side_groups(copies),
                tiled=False,
            )

        def whole_of(send, keep):
            send = send.astype(f32)
            return jnp.stack([keep[0], send[0], keep[1], send[1]])

        shared_rows = jnp.concatenate(
            [scatter(shared_sums[:, : width // 8], d_rows), scatter(shared_sums[:, width // 8 :], f_own)]
        )
        rdown_sums = scatter(whole_of(down_send, down_keep), f_rows)
        sided = by_side(whole_of(up_send, up_keep))
        rup_sums = jnp.concatenate(
            [
                scatter(lax.dynamic_index_in_dim(sided, which, 0, keepdims=False), d_rows)
                for which in (side, 1 - side)
            ]
        )
        last_parts = jnp.stack(
            [(away if k // 2 % 2 else stay)[k % 2 + 2 * (k // 4)].astype(bf16) for k in range(8)]
        )
        last_sums = jnp.sum(
            lax.all_to_all(
                last_parts.reshape(copies, d_rows, width),
                "dp",
                split_axis=0,
                concat_axis=0,
                tiled=True,
            ).astype(f32),
            axis=0,
        )

    lines = lines[0]
    qv_line = lax.dynamic_update_slice(
        jnp.zeros((2 * width,), f32), lines[:cols_own], (position * cols_own,)
    )
    qv_line = lax.dynamic_update_slice(
        qv_line, lines[2 * cols_own : 3 * cols_own], (width + position * cols_own,)
    ).reshape(copies, -1)
    pb_line = lines[3 * cols_own :].reshape(copies, d_rows)
    count_own = sums_f[2, 0]
    count_high = jnp.floor(count_own / 128.0)
    count_line = jnp.broadcast_to(
        jnp.stack([count_high, count_own - 128.0 * count_high])[None], (copies, 2)
    )
    line = jnp.concatenate([expert_line, qv_line, pb_line, count_line], axis=1)
    line_width = -(-line.shape[1] // (slots * 128)) * 128
    line = jnp.pad(line, ((0, 0), (0, slots * line_width - line.shape[1]))).reshape(
        copies, slots, line_width
    )

    rows_send, rows_keep, sums_out = to_rows(
        tied(out_own, away),
        out_got,
        rdownb_line,
        table,
        (gates,),
        shared_parts,
        both,
        downb_line,
    )
    combined_near, combined_got = reduce_group(rows_send, rows_keep)
    near_a, got_a = reduce_group(back_send, back_keep)

    block_of = block_hot.astype(f32)
    sums_all = jnp.concatenate(
        [
            sums_a[:group],
            sums_a[group:],
            jnp.pad(sums_b[:3].reshape(1, 3 * width), ((0, group - 1), (0, 0))),
            sums_out.reshape(group, width),
        ],
        axis=1,
    )
    slot_sums = jnp.sum(block_of[:, :, None] * sums_all[:, None, :], axis=0)
    slot_sums = slot_sums + swap(slot_sums, 1)
    slot_sums = slot_sums + swap(slot_sums, 2)
    grad_modulation = slot_sums.astype(bf16)
    mod_got = lax.all_to_all(
        jnp.concatenate(
            [
                jnp.broadcast_to(grad_modulation[None], (copies, slots, mod_width)),
                line.astype(bf16),
            ],
            axis=2,
        ),
        "dp",
        split_axis=0,
        concat_axis=0,
        tiled=True,
    )
    if copies == 8:
        mod_got = tied(mod_got, last_second)
    mod_all = mod_got[:, :, :mod_width].reshape(copies * slots, mod_width)
    line_sums = jnp.sum(mod_got[:, :, mod_width:].astype(f32), axis=0).reshape(-1)
    ada_grad = mm("sd,sm->dm", act_parts, mod_all)
    adabias_grad = jnp.sum(
        lax.dynamic_slice_in_dim(
            mod_all, place * ada_bias.shape[0], ada_bias.shape[0], axis=1
        ).astype(f32),
        axis=0,
    )
    cond_parts = mm("sm,dm->sd", mod_all, ada_weight).reshape(copies, slots, d_rows)
    after = cond_parts
    cond_got = lax.all_to_all(cond_parts, "dp", split_axis=0, concat_axis=0, tiled=True)
    cond_got = tied(cond_got, got_a, combined_got)
    combined = combined_near + combined_got.astype(f32) + downb_line
    output = (residual_mid + gate_b * combined).astype(bf16)
    grad_hidden_a = near_a + got_a.astype(f32)
    normed_a, inv_std_a = norm_parts(tokens.astype(f32))
    tokens_grad = grad_mid + norm_back(grad_hidden_a * (1.0 + scale_a), normed_a, inv_std_a)
    if copies == 8:
        last_third = dp_swap(last_second[1].astype(bf16), 2)
        last_sums = last_second[0] + last_third.astype(f32)
        rup_sums = tied(rup_sums, after)
    if copies == 8:
        cond_got = tied(cond_got, last_third)
    grad_cond_act = (
        cond_got
        .transpose(1, 0, 2)
        .reshape(slots, width)
    )
    sigmoid_cond = jax.nn.sigmoid(cond_value)
    conditioning_grad = (grad_cond_act * sigmoid_cond * (1.0 + cond_value * (1.0 - sigmoid_cond)))[
        None
    ]

    rup_got = pair_swap(rup_sums[d_rows:].astype(bf16))
    rdown_got = pair_swap(rdown_sums[keep:].astype(bf16))
    shared_all = exchange_group(shared_rows.astype(bf16))
    last_all = exchange_group(last_sums.astype(bf16))
    if copies == 8:
        rup_rows, rdown_rows = routed_rows(info, rup_sums, rup_got, rdown_sums, rdown_got, keep)
        up_rows, down_rows, qkv_rows, proj_rows = group_rows_out(
            info, shared_all, last_all, d_rows, f_rows
        )
    else:
        rup_rows = from_units(rup_sums[:d_rows].astype(f32), rup_got.astype(f32))
        kept, back = rdown_sums[:keep].astype(f32), rdown_got.astype(f32)
        rdown_rows = jnp.where(
            first_side, jnp.concatenate([kept, back]), jnp.concatenate([back, kept])
        )
        shared_all, last_all = (
            in_order(jnp.stack([v[0], v[2][0], v[1], v[2][1]]), position).astype(f32)
            for v in (shared_all, last_all)
        )
        up_rows = (
            shared_all[:, :d_rows]
            .reshape(group, d_rows, copies, f_own)
            .transpose(1, 2, 0, 3)
            .reshape(d_rows, hidden_units)
        )
        down_rows = shared_all[:, d_rows:].reshape(f_rows, width)
        qkv_rows = (
            last_all[:, :, : 3 * cols_own]
            .reshape(group, d_rows, 3, cols_own)
            .transpose(1, 2, 0, 3)
            .reshape(d_rows, 3 * width)
        )
        proj_rows = last_all[:, :, 3 * cols_own :].transpose(1, 0, 2).reshape(d_rows, width)
    cuts = [f_rows, f_own, d_rows, d_rows, 2 * width // copies, d_rows, 2]
    at = [sum(cuts[:i]) for i in range(len(cuts))]
    rupbias_row, upbias_sum, rdownbias_row, downbias_row, qvbias_sum, projbias_row, counts = (
        line_sums[o : o + n] for o, n in zip(at, cuts)
    )
    small = in_order(
        gather_group(jnp.concatenate([upbias_sum, qvbias_sum, counts])[None]), position
    )[:, 0]
    upbias_rows = small[:, :f_own].reshape(f_rows)
    qvbias_rows = jnp.sum(small[:, f_own:-2], axis=0)
    expert_counts = (128.0 * small[:, -2] + small[:, -1]).astype(jnp.int32)

    return (
        output,
        tokens_grad,
        conditioning_grad,
        qkv_rows,
        qvbias_rows,
        proj_rows,
        projbias_row,
        ada_grad,
        adabias_grad,
        up_rows,
        upbias_rows,
        down_rows,
        downbias_row,
        rup_rows[None],
        rupbias_row[None],
        rdown_rows[None],
        rdownbias_row[None],
        expert_counts,
    )


def solution(mesh):
    in_specs = (
        P(("dp", "expert"), None),
        P("dp", None, None),
        P(("dp", "expert"), None),
        P(("dp", "expert"), None),
        P("dp"),
        P("dp", None),
        P(("dp", "expert"), None),
        P("dp", None),
        P("dp"),
        P("dp", None),
        P("dp"),
        P("dp", None),
        P("dp"),
        P("dp", None),
        P("dp"),
        P("dp", None),
        P("dp"),
        P("expert", "dp", None),
        P("expert", "dp"),
        P("expert", "dp", None),
        P("expert", "dp"),
    )
    out_specs = (
        P(("dp", "expert"), None),
        P(("dp", "expert"), None),
        P("dp", None, None),
        P("dp", None),
        P("dp"),
        P("dp", None),
        P("dp"),
        P("dp", None),
        P("dp"),
        P("dp", None),
        P("dp"),
        P("dp", None),
        P("dp"),
        P("expert", "dp", None),
        P("expert", "dp"),
        P("expert", "dp", None),
        P("expert", "dp"),
        P(),
    )
    return jax.shard_map(body, mesh=mesh, in_specs=in_specs, out_specs=out_specs, check_vma=False)
```

```python
import jax
import jax.numpy as jnp
from jax import lax
from jax.experimental import pallas as pl
from jax.experimental.pallas import tpu as pltpu
from jax.sharding import PartitionSpec as P

HEADS = 12
HEAD_DIM = 64
CAP = 128

epsilon = 1e-06
gelu_root = 0.7978845608028654
gelu_cubic = 0.044715

bf16 = jnp.bfloat16
f32 = jnp.float32


def norm_parts(values):
    centered = values - jnp.mean(values, axis=-1, keepdims=True)
    inv_std = lax.rsqrt(jnp.mean(centered * centered, axis=-1, keepdims=True) + epsilon)
    return (centered * inv_std, inv_std)


def norm_back(grad_normed, normed, inv_std):
    mean_grad = jnp.mean(grad_normed, axis=-1, keepdims=True)
    mean_cross = jnp.mean(grad_normed * normed, axis=-1, keepdims=True)
    return inv_std * (grad_normed - mean_grad - normed * mean_cross)


def gelu_parts(values):
    square = values * values
    half = 0.5 + 0.5 * jnp.tanh(values * (gelu_root + gelu_root * gelu_cubic * square))
    activation = values * half
    slope = half + activation * (1.0 - half) * (
        2.0 * gelu_root + 6.0 * gelu_root * gelu_cubic * square
    )
    return (activation, slope)


def mm(spec, a, b):
    return jnp.einsum(spec, a, b, preferred_element_type=f32)


def swap(value, mask):
    size = lax.axis_size("expert")
    return lax.ppermute(value, "expert", [(i, i ^ mask) for i in range(size)])


def exchange_group(value):
    across = swap(value, 2)
    return value, across, swap(jnp.stack([value, across]), 1)


def gather_group(value):
    value, across, beside = exchange_group(value)
    return jnp.stack([value, beside[0], across, beside[1]])


def reduce_group(send, keep):
    beside = swap(send, 1)
    own = keep[0] + beside[0].astype(f32)
    other = (keep[1] + beside[1].astype(f32)).astype(bf16)
    return own, swap(other, 2)


def dp_swap(value, mask):
    copies = lax.axis_size("dp")
    return lax.ppermute(value, "dp", [(i, i ^ mask) for i in range(copies)])


def pair_swap(value):
    return dp_swap(value, 2)


def side_groups(copies):
    return [[i for i in range(copies) if (i >> 1) % 2 == side] for side in range(2)]


def pair_places(p):
    first = ((p >> 1) << 2) | (p & 1)
    return first, first + 2


def spread(value, *before):
    far = dp_swap(value, 4)
    return [value, dp_swap(tied(value, *before), 1), far, dp_swap(far, 1)]


def collect(send, keep, start, middle, end):
    got = dp_swap(tied(send, *start), 1)
    wide = tied(got, *middle).astype(f32)
    far = dp_swap((keep[1] + wide[1]).astype(bf16), 4)
    return keep[0] + wide[0] + tied(far, *end).astype(f32), got


def tied(value, *others):
    return lax.optimization_barrier((value, *others))[0]


def ring_place(at, copies):
    at = lax.rem(at + copies, copies)
    return jnp.where(at < copies // 2, 2 * at, 2 * (copies - 1 - at) + 1)


def ring_gather(share):
    copies = lax.axis_size("dp")
    if copies > 8:
        whole = lax.all_gather(share, "dp", axis=0)
        whole = whole.reshape((8, copies // 8 * share.shape[0]) + share.shape[1:])
        return [whole[k] for k in range(8)], jnp.arange(8, dtype=jnp.int32)
    half = copies // 2
    ring = [2 * i for i in range(half)] + [2 * i + 1 for i in reversed(range(half))]
    place = lax.axis_index("dp")
    position = jnp.where(lax.rem(place, 2) == 0, place // 2, copies - 1 - place // 2)

    def hop(value, way):
        return lax.ppermute(
            value, "dp", [(ring[i], ring[(i + way) % copies]) for i in range(copies)]
        )

    pieces, offsets = [share], [0]
    right = left = share
    for step in range(1, half + 1):
        right = hop(right, 1)
        pieces.append(right)
        offsets.append(-step)
        if step < half:
            left = hop(left, -1)
            pieces.append(left)
            offsets.append(step)
    return pieces, ring_place(position + jnp.array(offsets, jnp.int32), copies)


def dot(a, b, left=1, right=0):
    return lax.dot_general(
        a, b, (((left,), (right,)), ((), ())), preferred_element_type=f32
    )


def full(shape):
    return pl.BlockSpec(shape, lambda i: (0,) * len(shape), pipeline_mode=pl.Buffered(1))


SCALARS = pl.BlockSpec(memory_space=pltpu.SMEM)


def kernel_call(body, grid, in_specs, out_specs, out_shape, scratch, flops, operands):
    out_bytes = sum(int(o.size) * o.dtype.itemsize for o in out_shape)
    in_bytes = sum(int(o.size) * o.dtype.itemsize for o in operands)
    return pl.pallas_call(
        body,
        grid=(grid,),
        in_specs=in_specs,
        out_specs=out_specs,
        out_shape=out_shape,
        scratch_shapes=scratch,
        compiler_params=pltpu.CompilerParams(vmem_limit_bytes=56 * 2**20),
        cost_estimate=pl.CostEstimate(
            flops=int(flops), bytes_accessed=out_bytes + in_bytes, transcendentals=0
        ),
    )(*operands)


def shape(dims, dtype):
    return jax.ShapeDtypeStruct(dims, dtype)


def prepare(info, proj, qkv, biases, up, down, rup, rdown, keep, group):
    d_rows, width = proj.shape
    cols = width // group
    f_rows = down.shape[0]
    f_own = f_rows // group
    count = up.shape[1] // f_rows
    wide = 3 * cols
    chunks = rup.shape[1] // 2 // width

    def body(info, proj, qkv, *refs):
        biases, (up, down, rup, rdown, first, third, mine, theirs) = (
            refs[: len(biases_in)],
            refs[len(biases_in) :],
        )
        third[d_rows + f_own :, :] = proj[...]
        lines = [
            jnp.concatenate(
                [b[...].astype(f32).reshape(1, -1), jnp.zeros((1, wide - b.shape[0]), f32)], axis=1
            )
            for b in biases[1:]
        ]
        for p in range(group):

            @pl.when(info[8] == p)
            def _():
                own = slice(p * f_own, (p + 1) * f_own)
                first[:d_rows, :] = jnp.concatenate(
                    [qkv[:, i * width + p * cols : i * width + (p + 1) * cols] for i in range(3)],
                    axis=1,
                )
                line = jnp.concatenate(
                    [
                        biases[0][...].astype(f32).reshape(1, -1)[:, own],
                        jnp.zeros((1, wide - f_own), f32),
                    ],
                    axis=1,
                )
                first[d_rows:, :] = jnp.concatenate(
                    [line] + lines + [jnp.zeros((15 - len(lines), wide), f32)], axis=0
                ).astype(bf16)
                third[:d_rows, :] = jnp.concatenate(
                    [
                        up[:, d * f_rows + p * f_own : d * f_rows + (p + 1) * f_own]
                        for d in range(count)
                    ],
                    axis=1,
                )
                third[d_rows : d_rows + f_own, :] = down[own, :]

        one, two = [], []
        for p in range(count // 2):
            at, to = (d * f_rows for d in pair_places(p))
            one += [(at, at + keep), (to, to + f_rows - keep)]
            two += [(to + f_rows - keep, to + f_rows), (at + keep, at + f_rows)]
        for side in range(2):

            @pl.when(info[9] == side)
            def _():
                own, other = (one, two) if side == 0 else (two, one)
                for ref, parts in ((mine, own), (theirs, other)):
                    line = jnp.concatenate([rup[:, low:high] for low, high in parts], axis=1)
                    for c in range(line.shape[1] // width):
                        ref[c * d_rows : (c + 1) * d_rows, :] = line[:, c * width : (c + 1) * width]
                start = side * (f_rows - keep)
                mine[chunks * d_rows :, :] = rdown[start : start + keep, :]
                start = (1 - side) * keep
                theirs[chunks * d_rows :, :] = rdown[start : start + f_rows - keep, :]

    biases_in = biases
    operands = [proj, qkv, *biases, up, down, rup, rdown]
    outs = [
        shape((d_rows + 16, wide), bf16),
        shape((2 * d_rows + f_own, width), bf16),
        shape((chunks * d_rows + keep, width), bf16),
        shape((chunks * d_rows + f_rows - keep, width), bf16),
    ]
    return kernel_call(
        body,
        1,
        [SCALARS] + [full(o.shape) for o in operands],
        [full(o.shape) for o in outs],
        outs,
        [],
        0,
        [info, *operands],
    )


def middle_back(own, got, middle_rows, attn_out, cotangent, mods):
    rows, width = own.shape

    def body(own, got, mid, out, cot, mod, grad_mid, grad_attn, sums):
        grad = own[...] + got[...].astype(f32)
        normed, inv_std = norm_parts(mid[...])
        value = cot[...].astype(f32) + norm_back(
            grad * (1.0 + mod[0, 4:5, :]), normed, inv_std
        )
        grad_mid[...] = value
        grad_attn[...] = (mod[0, 2:3, :] * value).astype(bf16)
        sums[0:1, :] = jnp.sum(value * out[...], axis=0, keepdims=True)
        sums[1:2, :] = jnp.sum(grad, axis=0, keepdims=True)
        sums[2:3, :] = jnp.sum(grad * normed, axis=0, keepdims=True)
        sums[3:, :] = jnp.zeros((5, width), f32)

    operands = [own, got, middle_rows, attn_out, cotangent]
    outs = [shape((rows, width), f32), shape((rows, width), bf16), shape((8, width), f32)]
    return kernel_call(
        body,
        1,
        [full(o.shape) for o in operands] + [pl.BlockSpec((1, 8, width), lambda i: (0, 0, 0))],
        [full(o.shape) for o in outs],
        outs,
        [],
        0,
        [*operands, mods],
    )


def routed_rows(info, up_own, up_got, down_own, down_got, keep):
    d_rows, half = up_got.shape
    f_rows = down_own.shape[0]
    width = down_own.shape[1]
    pairs = half // f_rows

    def body(info, uo, ug, do, dg, up, down):
        for side in range(2):

            @pl.when(info[9] == side)
            def _():
                first, second = (0, 1) if side == 0 else (1, 0)
                values = (uo[:d_rows, :], ug[...].astype(f32))
                for p in range(pairs):
                    at, to = (d * f_rows for d in pair_places(p))
                    for whose, low, high, frm in (
                        (first, at, at + keep, 0),
                        (first, to, to + f_rows - keep, keep),
                        (second, to + f_rows - keep, to + f_rows, 0),
                        (second, at + keep, at + f_rows, keep),
                    ):
                        base = p * f_rows + frm
                        up[:, low:high] = values[whose][:, base : base + high - low]
                start = side * (f_rows - keep)
                down[start : start + keep, :] = do[:keep, :]
                start = (1 - side) * keep
                down[start : start + f_rows - keep, :] = dg[...].astype(f32)

    operands = [up_own, up_got, down_own, down_got]
    outs = [shape((d_rows, 2 * half), f32), shape((f_rows, width), f32)]
    return kernel_call(
        body,
        1,
        [SCALARS] + [full(o.shape) for o in operands],
        [full(o.shape) for o in outs],
        outs,
        [],
        0,
        [info, *operands],
    )


def group_rows_out(info, shared, last, d_rows, f_rows):
    group = 4
    rows, width = shared[0].shape
    f_own = f_rows // group
    cols = width // group
    count = width // f_own

    def body(info, s0, s2, s13, l0, l2, l13, up, down, qkv, proj, shared, last):
        for all_parts, p0, p2, p13 in ((shared, s0, s2, s13), (last, l0, l2, l13)):
            all_parts[0], all_parts[2] = p0[...].astype(f32), p2[...].astype(f32)
            all_parts[1], all_parts[3] = p13[0].astype(f32), p13[1].astype(f32)
        for a in range(group):
            part = shared[info[8] ^ a]
            for d in range(count):
                at = d * f_rows + a * f_own
                up[:, at : at + f_own] = part[:d_rows, d * f_own : (d + 1) * f_own]
            down[a * f_own : (a + 1) * f_own, :] = part[d_rows:, :]
            part = last[info[8] ^ a]
            for i in range(3):
                at = i * width + a * cols
                qkv[:, at : at + cols] = part[:, i * cols : (i + 1) * cols]
            proj[:, a * cols : (a + 1) * cols] = part[:, 3 * cols :]

    outs = [
        shape((d_rows, count * f_rows), f32),
        shape((f_rows, width), f32),
        shape((d_rows, 3 * width), f32),
        shape((d_rows, width), f32),
    ]
    operands = [*shared, *last]
    return kernel_call(
        body,
        1,
        [SCALARS] + [full(o.shape) for o in operands],
        [full(o.shape) for o in outs],
        outs,
        [pltpu.VMEM((group, rows, width), f32), pltpu.VMEM((group, d_rows, width), f32)],
        0,
        [info, *operands],
    )


def front(info, tokens, mods, bias, pieces, rows_piece, cols_own, cut):
    blocks, rows = tokens.shape[0], tokens.shape[1] - 16
    width = 8 * rows_piece
    wide = 3 * cols_own

    def body(info, tok, more, mod, bias, *refs):
        parts = refs[:8]
        (hid, prj, qkv, table, gates, low_grad, slot, sums, lines, units, three, lists) = refs[8:]
        step = pl.program_id(0)

        @pl.when(step == 0)
        def _():
            for k in range(8):
                at = pl.multiple_of(info[k] * rows_piece, rows_piece)
                qkv[pl.ds(at, rows_piece), :] = parts[k][:rows_piece, :]
                if cut:
                    lists[info[k]] = parts[k][rows_piece:, :].astype(f32)
            three[...] = bias[...]
            if cut:
                three[:, :cols_own] = lists[info[8]][2:3, :cols_own]
                three[:, 2 * cols_own :] = lists[info[8] + 4][2:3, :cols_own]
                lines[...] = jnp.zeros_like(lines)
                for d in range(8):
                    at = slice(d * rows_piece, (d + 1) * rows_piece)
                    for i, row in enumerate((0, 3, 4, 5)):
                        lines[i : i + 1, at] = lists[d, row : row + 1, :rows_piece]
                size = units.shape[2]
                for side in range(2):

                    @pl.when(info[9] == side)
                    def _():
                        for p in range(units.shape[0]):
                            one, two = pair_places(p)
                            if side == 0:
                                units[p, :, :cut] = lists[one, 1:2, :cut]
                                units[p, :, cut:] = lists[two, 1:2, : size - cut]
                            else:
                                units[p, :, :cut] = lists[two, 1:2, size - cut : size]
                                units[p, :, cut:] = lists[one, 1:2, cut:size]

            sums[...] = jnp.zeros_like(sums)

        normed, _ = norm_parts(tok[0, :, :width].astype(f32))
        low = (normed * (1.0 + mod[0, 1:2, :]) + mod[0, 0:1, :]).astype(bf16)
        hid[...] = low
        prj[...] = (dot(low, qkv[...]) + three[...]).astype(bf16)

        me = info[8].astype(f32)
        pairs = more[0].astype(f32)
        one = (pairs[0:1, :] == me).astype(f32)
        two = (pairs[1:2, :] == me).astype(f32)
        hot = one + two
        gate = one * (pairs[2:3, :] + pairs[4:5, :] + pairs[6:7, :]) + two * (
            pairs[3:4, :] + pairs[5:6, :] + pairs[7:8, :]
        )
        across = lax.broadcasted_iota(jnp.int32, (rows, rows), 1)
        down = lax.broadcasted_iota(jnp.int32, (rows, rows), 0)
        earlier = (down < across).astype(f32).astype(bf16)
        rank = dot(jnp.broadcast_to(hot, (8, rows)).astype(bf16), earlier)[0:1, :]
        kept = hot * (rank < CAP).astype(f32)
        places = lax.broadcasted_iota(jnp.int32, (CAP, rows), 0).astype(f32)
        placed = jnp.where(rank == places, kept, 0.0)
        table[0] = placed.astype(bf16)
        gates[0] = jnp.sum(jnp.where(down == across, gate, 0.0), axis=1, keepdims=True)
        cot = tok[0, :, width:]
        grad = (mod[0, 5:6, :] * cot.astype(f32)).astype(bf16)
        low_grad[...] = grad
        gate_slot = jnp.sum(placed * gate, axis=1, keepdims=True)
        slot_grad = (gate_slot * (mod[0, 5:6, :] * dot(table[0], cot))).astype(bf16)
        slot[...] = slot_grad
        sums[0:1, :] += jnp.sum(slot_grad.astype(f32), axis=0, keepdims=True)
        sums[1:2, :] += jnp.sum(grad.astype(f32), axis=0, keepdims=True)
        sums[2:3, :] += jnp.broadcast_to(jnp.sum(kept, axis=1, keepdims=True), (1, width))

    return kernel_call(
        body,
        blocks,
        [
            SCALARS,
            pl.BlockSpec((1, rows, 2 * width), lambda i: (i, 0, 0)),
            pl.BlockSpec((1, 16, rows), lambda i: (i, rows // 16, 0)),
            pl.BlockSpec((1, 8, width), lambda i: (i, 0, 0)),
            full((1, wide)),
        ]
        + [full(p.shape) for p in pieces],
        [
            pl.BlockSpec((rows, width), lambda i: (i, 0)),
            pl.BlockSpec((rows, wide), lambda i: (i, 0)),
            full((width, wide)),
            pl.BlockSpec((1, CAP, rows), lambda i: (i, 0, 0)),
            pl.BlockSpec((1, rows, 1), lambda i: (i, 0, 0)),
            pl.BlockSpec((rows, width), lambda i: (i, 0)),
            pl.BlockSpec((CAP, width), lambda i: (i, 0)),
            full((8, width)),
            full((8, width)),
            full((4, 1, width // 2)),
        ],
        [
            shape((blocks * rows, width), bf16),
            shape((blocks * rows, wide), bf16),
            shape((width, wide), bf16),
            shape((blocks, CAP, rows), bf16),
            shape((blocks, rows, 1), f32),
            shape((blocks * rows, width), bf16),
            shape((blocks * CAP, width), bf16),
            shape((8, width), f32),
            shape((8, width), f32),
            shape((4, 1, width // 2), f32),
        ],
        [pltpu.VMEM((1, wide), f32), pltpu.VMEM((8, 16, wide), f32)],
        2 * blocks * rows * width * wide,
        [info, tokens, tokens, mods, bias, *pieces],
    )


def to_rows(own, got, bias, table, gates, addend, tokens, line):
    blocks, cap, rows = table.shape
    width = own.shape[1]

    def body(own, got, bias, tab, *refs):
        gate, (add, tok, line, send, keep, sums) = refs[:-6], refs[-6:]
        slots = (own[...] + got[...].astype(f32) + bias[...]).astype(bf16)
        value = dot(tab[0], slots, 0, 0)
        value = add[...] + (gate[0][0] * value if gate else value)
        first = (pl.program_id(0) == 0).astype(f32)
        sums[0] = jnp.sum(
            tok[0].astype(f32) * (value + first * line[...]), axis=0, keepdims=True
        )
        for k in range(blocks):

            @pl.when(pl.program_id(0) == k)
            def _():
                if k % 2 == 1:
                    send[k // 2] = value.astype(bf16)
                else:
                    keep[k // 2] = value

    operands = [own, got, bias, table, *gates, addend, tokens, line]
    return kernel_call(
        body,
        blocks,
        [
            pl.BlockSpec((cap, width), lambda i: (i, 0)),
            pl.BlockSpec((cap, width), lambda i: (i, 0)),
            full((1, width)),
            pl.BlockSpec((1, cap, rows), lambda i: (i, 0, 0)),
        ]
        + [pl.BlockSpec((1, rows, 1), lambda i: (i, 0, 0))] * len(gates)
        + [
            pl.BlockSpec((rows, width), lambda i: (i, 0)),
            pl.BlockSpec((1, rows, width), lambda i: (i, 0, 1)),
            full((1, width)),
        ],
        [
            full((2, rows, width)),
            full((2, rows, width)),
            pl.BlockSpec((1, 1, width), lambda i: (i, 0, 0)),
        ],
        [
            shape((2, rows, width), bf16),
            shape((2, rows, width), f32),
            shape((blocks, 1, width), f32),
        ],
        [],
        2 * blocks * rows * width * cap,
        operands,
    )


def score_parts(info, query, key, blocks, rows):
    own = info[10 + pl.program_id(0)]
    lanes = lax.broadcasted_iota(jnp.int32, (1, blocks * rows), 1) // rows
    seen = jnp.zeros((1, blocks * rows), jnp.int32)
    for j in range(blocks):
        seen = jnp.where((lanes == j) & (info[10 + j] == own), 1, seen)
    scores = dot(query * bf16(HEAD_DIM ** (-0.5)), key, 1, 1)
    masked = jnp.where(seen == 1, scores, -1e30)
    exponent = jnp.exp(masked - jnp.max(masked, axis=-1, keepdims=True))
    return exponent * (1.0 / jnp.sum(exponent, axis=-1, keepdims=True))


def attention(info, projected, blocks, cols_own):
    total, wide = projected.shape
    rows = total // blocks

    def body(info, own, every, out):
        for h in range(cols_own // HEAD_DIM):
            q = slice(h * HEAD_DIM, (h + 1) * HEAD_DIM)
            k = slice(cols_own + h * HEAD_DIM, cols_own + (h + 1) * HEAD_DIM)
            v = slice(2 * cols_own + h * HEAD_DIM, 2 * cols_own + (h + 1) * HEAD_DIM)
            probs = score_parts(info, own[:, q], every[:, k], blocks, rows)
            out[:, q] = dot(probs.astype(bf16), every[:, v]).astype(bf16)

    return kernel_call(
        body,
        blocks,
        [SCALARS, pl.BlockSpec((rows, wide), lambda i: (i, 0)), full((total, wide))],
        [pl.BlockSpec((rows, cols_own), lambda i: (i, 0))],
        [shape((total, cols_own), bf16)],
        [],
        4 * total * total * cols_own,
        [info, projected, projected],
    )[0]


def attention_back(info, projected, grad_attn, proj_rel, blocks, cols_own):
    total, wide = projected.shape
    rows = total // blocks
    width = grad_attn.shape[1]
    scale = HEAD_DIM ** (-0.5)

    def body(info, own, every, grad, rel, out, sums_k, sums_v, sums_q):
        step = pl.program_id(0)

        @pl.when(step == 0)
        def _():
            sums_k[...] = jnp.zeros_like(sums_k)
            sums_v[...] = jnp.zeros_like(sums_v)

        back = dot(grad[...], rel[...], 1, 1).astype(bf16)
        for h in range(cols_own // HEAD_DIM):
            q = slice(h * HEAD_DIM, (h + 1) * HEAD_DIM)
            k = slice(cols_own + h * HEAD_DIM, cols_own + (h + 1) * HEAD_DIM)
            v = slice(2 * cols_own + h * HEAD_DIM, 2 * cols_own + (h + 1) * HEAD_DIM)
            probs = score_parts(info, own[:, q], every[:, k], blocks, rows)
            grad_probs = dot(back[:, q], every[:, v], 1, 1)
            inner = jnp.sum(probs * grad_probs, axis=-1, keepdims=True)
            scores = (probs * (grad_probs - inner)).astype(bf16)
            at = pl.multiple_of(step * rows, rows)
            sums_q[pl.ds(at, rows), q] = dot(scores, every[:, k]) * scale
            sums_k[:, q] += dot(scores, own[:, q], 0, 0)
            sums_v[:, q] += dot(probs.astype(bf16), back[:, q], 0, 0)

        @pl.when(step == blocks - 1)
        def _():
            out[:, :cols_own] = sums_q[...].astype(bf16)
            out[:, cols_own : 2 * cols_own] = (sums_k[...] * scale).astype(bf16)
            out[:, 2 * cols_own :] = sums_v[...].astype(bf16)

    return kernel_call(
        body,
        blocks,
        [
            SCALARS,
            pl.BlockSpec((rows, wide), lambda i: (i, 0)),
            full((total, wide)),
            pl.BlockSpec((rows, width), lambda i: (i, 0)),
            full((cols_own, width)),
        ],
        [full((total, wide))],
        [shape((total, wide), bf16)],
        [pltpu.VMEM((total, cols_own), f32)] * 3,
        10 * total * total * cols_own + 2 * total * width * cols_own,
        [info, projected, projected, grad_attn, proj_rel],
    )[0]


def middle(info, tokens, mods, heads, pieces, proj_bias, table, rows_piece):
    blocks, rows = tokens.shape[0], tokens.shape[1] - 16
    width = 8 * rows_piece
    cols = width // blocks
    cap = table.shape[1]

    def body(info, tok, mod, h0, h1, h2, h3, bias, tab, *refs):
        parts, (hid, att, buf, out0, mid0, own, rel) = refs[:8], refs[8:]

        @pl.when(pl.program_id(0) == 0)
        def _():
            for k in range(8):
                place = info[18 + k]
                at = ((place >> 1) ^ info[8]) * cols + (place & 1) * rows_piece
                at = pl.multiple_of(at, rows_piece)
                rel[pl.ds(at, rows_piece), :] = parts[k][2 * rows_piece :, :]
            own[...] = rel[:cols, :]

        attended = jnp.concatenate([h0[...], h1[...], h2[...], h3[...]], axis=1)
        att[...] = attended
        out = dot(attended, rel[...]) + bias[...]
        mid = tok[0].astype(f32) + mod[0, 2:3, :] * out
        normed, _ = norm_parts(mid)
        low = (normed * (1.0 + mod[0, 4:5, :]) + mod[0, 3:4, :]).astype(bf16)
        hid[...] = low
        buf[...] = dot(tab[0], low).astype(bf16)

        @pl.when(pl.program_id(0) == 0)
        def _():
            out0[...] = out
            mid0[...] = mid

    return kernel_call(
        body,
        blocks,
        [
            SCALARS,
            pl.BlockSpec((1, rows, width), lambda i: (i, 0, 0)),
            pl.BlockSpec((1, 8, width), lambda i: (i, 0, 0)),
            pl.BlockSpec((rows, cols), lambda i: (i, 0)),
            pl.BlockSpec((rows, cols), lambda i: (i ^ 1, 0)),
            pl.BlockSpec((rows, cols), lambda i: (i ^ 2, 0)),
            pl.BlockSpec((rows, cols), lambda i: (i ^ 3, 0)),
            full((1, width)),
            pl.BlockSpec((1, cap, rows), lambda i: (i, 0, 0)),
        ]
        + [full(p.shape) for p in pieces],
        [
            pl.BlockSpec((rows, width), lambda i: (i, 0)),
            pl.BlockSpec((rows, width), lambda i: (i, 0)),
            pl.BlockSpec((cap, width), lambda i: (i, 0)),
            full((rows, width)),
            full((rows, width)),
            full((cols, width)),
        ],
        [
            shape((blocks * rows, width), bf16),
            shape((blocks * rows, width), bf16),
            shape((blocks * cap, width), bf16),
            shape((rows, width), f32),
            shape((rows, width), f32),
            shape((cols, width), bf16),
        ],
        [pltpu.VMEM((width, width), bf16)],
        2 * blocks * rows * width * (width + cap),
        [info, tokens, mods, *heads, proj_bias, table, *pieces],
    )


def shared_expert(info, hidden, grad, bias, pieces, rows_piece, blocks, paired):
    total, width = hidden.shape
    rows = total // blocks
    pairs = 4
    sums_mine = (pairs, 2 * rows_piece, width) if paired else (2, width, width)
    sums_theirs = (pairs, 2 * rows_piece, width) if paired else (1, 8, width)

    def body(info, hid, gcl, bias, *refs):
        parts, (out, back, mine, theirs, line, up, down, up_sum, down_sum, wide) = refs[:8], refs[8:]
        step = pl.program_id(0)

        @pl.when(step == 0)
        def _():
            for k in range(8):
                at = pl.multiple_of(info[18 + k] * rows_piece, rows_piece)
                up[pl.ds(at, rows_piece), :] = parts[k][:rows_piece, :]
                down[pl.ds(at, rows_piece), :] = parts[k][rows_piece : 2 * rows_piece, :]
            up_sum[...] = jnp.zeros_like(up_sum)
            down_sum[...] = jnp.zeros_like(down_sum)
            wide[...] = jnp.zeros_like(wide)

        act, slope = gelu_parts(dot(hid[...], up[...]) + bias[...])
        low = act.astype(bf16)
        out[...] = dot(low, down[...])
        down_sum[...] += dot(low, gcl[...], 0, 0)
        grad_pre = dot(gcl[...], down[...], 1, 1) * slope
        grad_low = grad_pre.astype(bf16)
        wide[...] += jnp.sum(grad_low.astype(f32), axis=0, keepdims=True)
        up_sum[...] += dot(hid[...], grad_low, 0, 0)
        back[...] = dot(grad_low, up[...], 1, 1)

        @pl.when(step == blocks - 1)
        def _():
            line[...] = wide[...]
            if not paired:
                mine[0], mine[1] = up_sum[...], down_sum[...]
            for p in range(pairs if paired else 0):
                at = pl.multiple_of(info[18 + 2 * p] * rows_piece, rows_piece)
                far = pl.multiple_of(info[19 + 2 * p] * rows_piece, rows_piece)
                mine[p, :rows_piece, :] = up_sum[pl.ds(at, rows_piece), :]
                mine[p, rows_piece:, :] = down_sum[pl.ds(at, rows_piece), :]
                theirs[p, :rows_piece, :] = up_sum[pl.ds(far, rows_piece), :].astype(bf16)
                theirs[p, rows_piece:, :] = down_sum[pl.ds(far, rows_piece), :].astype(bf16)

    return kernel_call(
        body,
        blocks,
        [
            SCALARS,
            pl.BlockSpec((rows, width), lambda i: (i, 0)),
            pl.BlockSpec((rows, width), lambda i: (i, 0)),
            full((1, width)),
        ]
        + [full(p.shape) for p in pieces],
        [
            pl.BlockSpec((rows, width), lambda i: (i, 0)),
            pl.BlockSpec((rows, width), lambda i: (i, 0)),
            full(sums_mine),
            full(sums_theirs),
            full((1, width)),
        ],
        [
            shape((total, width), f32),
            shape((total, width), f32),
            shape(sums_mine, f32),
            shape(sums_theirs, bf16),
            shape((1, width), f32),
        ],
        [
            pltpu.VMEM((width, width), bf16),
            pltpu.VMEM((width, width), bf16),
            pltpu.VMEM((width, width), f32),
            pltpu.VMEM((width, width), f32),
            pltpu.VMEM((1, width), f32),
        ],
        12 * total * width * width,
        [info, hidden, grad, bias, *pieces],
    )


def routed_rows_grads(info, buffers, slots, own, other, bias):
    pairs, _, units = bias.shape
    count, width = buffers[0].shape
    piece = width // (2 * pairs)
    every = pairs * units
    chunks = every // width
    cut = own[0].shape[0] - chunks * piece

    def body(info, b0, b1, s0, s1, *refs):
        packs, bias = (refs[:4], refs[4:8]), refs[8]
        (g0, g1, e0, e1, line, act_low, grad_low, bs, ss, up, down, gsum, esum) = refs[9:]
        step = pl.program_id(0)

        @pl.when(step == 0)
        def _():
            for r in range(pairs):
                for j in range(2):
                    at = pl.multiple_of(info[18 + 2 * r + j] * piece, piece)
                    for c in range(chunks):
                        up[pl.ds(at, piece), c * width : (c + 1) * width] = packs[j][r][
                            c * piece : (c + 1) * piece, :
                        ]
                    at = info[14 + r] * units + j * cut
                    at = pl.multiple_of(at, 128)
                    size = units - cut if j else cut
                    down[pl.ds(at, size), :] = packs[j][r][chunks * piece :, :]
            bs[:count, :], bs[count:, :] = b0[...], b1[...]
            ss[:count, :], ss[count:, :] = s0[...], s1[...]
            gsum[...] = jnp.zeros_like(gsum)
            esum[...] = jnp.zeros_like(esum)

        at = pl.multiple_of(step * units, 128)
        w_up = up[:, pl.ds(at, units)]
        w_down = down[pl.ds(at, units), :]
        act, slope = gelu_parts(dot(bs[...], w_up) + bias[step])
        low = act.astype(bf16)
        act_low[...] = low
        esum[...] += dot(low, w_down)
        grad = (dot(ss[...], w_down, 1, 1) * slope).astype(bf16)
        grad_low[...] = grad
        line[0] = jnp.sum(grad.astype(f32), axis=0, keepdims=True)
        gsum[...] += dot(grad, w_up, 1, 1)

        @pl.when(step == pairs - 1)
        def _():
            g0[...] = gsum[:count, :]
            g1[...] = gsum[count:, :].astype(bf16)
            e0[...] = esum[:count, :]
            e1[...] = esum[count:, :].astype(bf16)

    outs = [
        shape((count, width), f32),
        shape((count, width), bf16),
        shape((count, width), f32),
        shape((count, width), bf16),
        shape((pairs, 1, units), f32),
        shape((2 * count, every), bf16),
        shape((2 * count, every), bf16),
        shape((2 * count, width), bf16),
        shape((2 * count, width), bf16),
    ]
    operands = [*buffers, *slots, *own, *other, bias]
    by_step = pl.BlockSpec((2 * count, units), lambda i: (0, i))
    return kernel_call(
        body,
        pairs,
        [SCALARS] + [full(o.shape) for o in operands],
        [full(o.shape) for o in outs[:4]]
        + [pl.BlockSpec((1, 1, units), lambda i: (i, 0, 0)), by_step, by_step]
        + [full(o.shape) for o in outs[7:]],
        outs,
        [
            pltpu.VMEM((width, every), bf16),
            pltpu.VMEM((every, width), bf16),
            pltpu.VMEM((2 * count, width), f32),
            pltpu.VMEM((2 * count, width), f32),
        ],
        16 * count * width * every,
        [info, *operands],
    )


def routed_weight_grads(info, act_low, grad_low, rows, slots, pairs):
    total, width = rows.shape
    every = act_low.shape[1]
    units = every // pairs
    piece = width // (2 * pairs)

    def body(info, act, grad, bs, ss, ds, dk, us, uk, values):
        step = pl.program_id(0)
        slot = step ^ info[14]
        at = pl.multiple_of(step * units, 128)
        rdown = dot(act[...], ss[...], 0, 0)
        values[...] = dot(bs[...], grad[...], 0, 0)
        for r in range(pairs):
            for j in range(2):
                row = pl.multiple_of(info[18 + 2 * r + j] * piece, piece)
                value = values[pl.ds(row, piece), :]
                if r % 2 == 1:
                    us[r // 2, j * piece : (j + 1) * piece, pl.ds(at, units)] = value.astype(bf16)
                else:
                    uk[r // 2, j * piece : (j + 1) * piece, pl.ds(at, units)] = value

            @pl.when(slot == r)
            def _():
                if r % 2 == 1:
                    ds[r // 2] = rdown.astype(bf16)
                else:
                    dk[r // 2] = rdown

    outs = [
        shape((2, units, width), bf16),
        shape((2, units, width), f32),
        shape((2, 2 * piece, every), bf16),
        shape((2, 2 * piece, every), f32),
    ]
    operands = [act_low, grad_low, rows, slots]
    return kernel_call(
        body,
        pairs,
        [SCALARS]
        + [pl.BlockSpec((total, units), lambda i: (0, i))] * 2
        + [full(o.shape) for o in operands[2:]],
        [full(o.shape) for o in outs],
        outs,
        [pltpu.VMEM((width, units), f32)],
        4 * total * width * every,
        [info, *operands],
    )


def tail_grads(info, tokens, hidden, grads, attended, grad_attn, qkv):
    total, width = hidden.shape
    wide = grads.shape[1]
    blocks, rows = tokens.shape[0], tokens.shape[1] - 16
    cols = width // blocks
    piece = width // 8

    def body(info, tok, hid, gr, att, ga, qkv, away, stay, send, keep, sums, lines, proj, wq):
        wq[...] = dot(hid[...], gr[...], 0, 0)
        for m in range(blocks):
            these = slice(m * rows, (m + 1) * rows)
            grad = dot(gr[these, :], qkv[...], 1, 1)
            if m % 2 == 1:
                send[m // 2] = grad.astype(bf16)
            else:
                keep[m // 2] = grad
            normed, _ = norm_parts(tok[m].astype(f32))
            sums[m : m + 1, :] = jnp.sum(grad, axis=0, keepdims=True)
            sums[blocks + m : blocks + m + 1, :] = jnp.sum(grad * normed, axis=0, keepdims=True)
        lines[:, :wide] = jnp.sum(gr[...].astype(f32), axis=0, keepdims=True)
        lines[:, wide:] = jnp.sum(ga[...].astype(f32), axis=0, keepdims=True)
        own = ga[:, :cols]
        for k in range(1, blocks):
            own = jnp.where(info[8] == k, ga[:, k * cols : (k + 1) * cols], own)
        proj[...] = dot(att[...], own, 0, 0)
        for k in range(8):
            place = info[18 + k]
            at = pl.multiple_of(place * piece, piece)
            value = wq[pl.ds(at, piece), :]
            at = pl.multiple_of(((place >> 1) ^ info[8]) * cols + (place & 1) * piece, piece)
            other = proj[pl.ds(at, piece), :]
            i = k % 2 + 2 * (k // 4)
            if k // 2 % 2 == 1:
                away[i, :, :wide] = value.astype(bf16)
                away[i, :, wide:] = other.astype(bf16)
            else:
                stay[i, :, :wide] = value
                stay[i, :, wide:] = other

    return kernel_call(
        body,
        1,
        [SCALARS, pl.BlockSpec((blocks, rows, width), lambda i: (0, 0, 0))]
        + [full((total, width)), full((total, wide)), full((total, width))]
        + [full((total, width)), full((width, wide))],
        [
            full((4, piece, width)),
            full((4, piece, width)),
            full((2, rows, width)),
            full((2, rows, width)),
            full((2 * blocks, width)),
            full((1, wide + width)),
        ],
        [
            shape((4, piece, width), bf16),
            shape((4, piece, width), f32),
            shape((2, rows, width), bf16),
            shape((2, rows, width), f32),
            shape((2 * blocks, width), f32),
            shape((1, wide + width), f32),
        ],
        [pltpu.VMEM((width, cols), f32), pltpu.VMEM((width, wide), f32)],
        2 * total * width * (2 * wide + cols),
        [info, tokens, hidden, grads, attended, grad_attn, qkv],
    )


def in_order(relative, position):
    return jnp.stack(
        [
            lax.dynamic_index_in_dim(relative, position ^ a, 0, keepdims=False)
            for a in range(relative.shape[0])
        ]
    )


def body(
    tokens,
    conditioning,
    routes,
    gate_weights,
    image_counts,
    image_lengths,
    cotangent,
    qkv_weight,
    qv_bias,
    proj_weight,
    proj_bias,
    ada_weight,
    ada_bias,
    up_weight,
    up_bias,
    down_weight,
    down_bias,
    routed_up,
    routed_upbias,
    routed_down,
    routed_downbias,
):
    group = lax.axis_size("expert")
    copies = lax.axis_size("dp")
    position = lax.axis_index("expert")
    place = lax.axis_index("dp")
    rows, width = tokens.shape
    group_rows = group * rows
    heads_own = HEADS // group
    cols_own = heads_own * HEAD_DIM
    d_rows = qkv_weight.shape[0]
    f_rows = down_weight.shape[0]
    f_own = f_rows // group
    hidden_units = f_rows * copies
    quarter = hidden_units // group
    side = lax.rem(place // 2, 2)
    first_side = side == 0
    pairs_count = copies // 2
    keep = f_rows * 2 // 3
    send = f_rows - keep
    half_units = hidden_units // 2

    def my_units(value):
        one, two = [], []
        for p in range(pairs_count):
            at, to = (d * f_rows for d in pair_places(p))
            one += [value[..., at : at + keep], value[..., to : to + send]]
            two += [value[..., to + send : to + f_rows], value[..., at + keep : at + f_rows]]
        one, two = jnp.concatenate(one, axis=-1), jnp.concatenate(two, axis=-1)
        return jnp.where(first_side, one, two), jnp.where(first_side, two, one)

    def from_units(mine, theirs):
        one = jnp.where(first_side, mine, theirs)
        two = jnp.where(first_side, theirs, mine)
        out = [None] * copies
        for p in range(pairs_count):
            at = f_rows * p
            first, second = pair_places(p)
            out[first] = [one[..., at : at + keep], two[..., at + keep : at + f_rows]]
            out[second] = [one[..., at + keep : at + f_rows], two[..., at : at + keep]]
        out = sum(out, [])
        return jnp.concatenate(out, axis=-1)

    bias_list = [up_bias, routed_upbias[0], qv_bias, proj_bias, down_bias, routed_downbias[0]]
    if copies == 8:
        first_share, third_share, routed_mine, routed_theirs = prepare(
            jnp.stack([position] * 9 + [side]).astype(jnp.int32),
            proj_weight,
            qkv_weight,
            bias_list,
            up_weight,
            down_weight,
            routed_up[0],
            routed_down[0],
            keep,
            group,
        )
    else:
        qkv_share = lax.dynamic_index_in_dim(
            qkv_weight.reshape(d_rows, 3, group, cols_own), position, 2, keepdims=False
        ).reshape(d_rows, 3 * cols_own)
        first_share = qkv_share
        up_share = lax.dynamic_index_in_dim(
            up_weight.reshape(d_rows, copies, group, f_own), position, 2, keepdims=False
        ).reshape(d_rows, quarter)
        down_share = lax.dynamic_slice_in_dim(down_weight, position * f_own, f_own, axis=0)
        third_share = jnp.concatenate([up_share, down_share, proj_weight], axis=0)
        rup_mine, rup_theirs = my_units(routed_up[0])
        rdown_mine = lax.dynamic_slice_in_dim(routed_down[0], side * send, keep, axis=0)
        rdown_theirs = lax.dynamic_slice_in_dim(routed_down[0], (1 - side) * keep, send, axis=0)
        rup_got = pair_swap(rup_theirs)
        rdown_got = pair_swap(rdown_theirs)
    first, order = ring_gather(first_share)
    bias_three = jnp.zeros((1, 3 * cols_own), f32)
    if copies > 8:
        upb, rupb, qvb, projb, downb, rdownb = (
            lax.all_gather(b, "dp", axis=0, tiled=True).astype(f32) for b in bias_list
        )
        upb_own = lax.dynamic_index_in_dim(
            upb.reshape(copies, group, f_own), position, 1, keepdims=False
        ).reshape(quarter)
        bias_lines = jnp.stack([upb_own, projb, downb, rdownb])
        rupb_own = my_units(rupb)[0].reshape(4, 1, half_units // 4)
        bias_three = jnp.concatenate(
            [
                lax.dynamic_slice_in_dim(qvb, position * cols_own, cols_own),
                jnp.zeros((cols_own,), f32),
                lax.dynamic_slice_in_dim(qvb, width + position * cols_own, cols_own),
            ]
        )[None]

    pair_steps = jnp.arange(4, dtype=jnp.int32)
    if copies == 8:
        third_swap, routed_swap = pair_swap(third_share), pair_swap(routed_theirs)
        third_own = spread(third_share, *first[5:7])
        third_got = spread(third_swap, *first[5:7])
        routed_own = spread(tied(routed_mine, third_got[2]), *first[5:7])
        routed_got = spread(tied(routed_swap, third_got[2]), *first[5:7])
        third = [v for pair in zip(third_own, third_got) for v in pair]
        dues = [(*first[1:3], third_swap), (*first[3:5], third_own[2]), (*first[5:7], routed_swap), (third_got[2],), (third_own[3],), (), (routed_own[2],), (routed_own[3], routed_got[1])]
        pair_now = (place >> 2) * 2 + (place & 1)
        unit_blocks = pair_now ^ pair_steps
        masks = jnp.array([0, 2, 1, 3, 4, 6, 5, 7], jnp.int32)
        row_blocks = place ^ masks
    else:
        groups = side_groups(copies)
        whole = lax.all_gather(third_share, "dp", axis=0)
        third = jnp.concatenate(
            [
                whole[:, :d_rows].reshape(8, -1, width),
                whole[:, d_rows : d_rows + f_own].reshape(8, -1, width),
                whole[:, d_rows + f_own :].reshape(8, -1, width),
            ],
            axis=1,
        ).reshape(4, 2, -1, width)
        sided = jnp.where(
            first_side, jnp.stack([rup_mine, rup_got]), jnp.stack([rup_got, rup_mine])
        )
        ups = lax.all_gather(sided, "dp", axis=0, axis_index_groups=groups)
        ups = ups.reshape(pairs_count // 2, 2, 2, d_rows, half_units).transpose(0, 2, 1, 3, 4)
        ups = ups.reshape(4, 2, width // 8, half_units)
        downs = lax.all_gather(
            jnp.concatenate([rdown_mine, rdown_got]), "dp", axis=0, axis_index_groups=groups
        ).reshape(4, half_units // 4, width)
        third = [third[r, j] for r in range(4) for j in range(2)]
        cut = keep * half_units // (4 * f_rows)

        def packs(j, low, high):
            return [
                jnp.concatenate(
                    [ups[r, j, :, c : c + width] for c in range(0, half_units, width)]
                    + [downs[r, low:high]]
                )
                for r in range(4)
            ]

        routed_own, routed_got = packs(0, 0, cut), packs(1, cut, half_units // 4)
        dues = [()] * 8
        unit_blocks = pair_steps
        row_blocks = jnp.arange(8, dtype=jnp.int32)

    def by_side(whole):
        out = whole.reshape(pairs_count // 2, 2, 2, d_rows, -1).transpose(1, 0, 2, 3, 4)
        return out.reshape(2, 4, width // 8, -1)

    gates_left, gate_parts = gate_weights.T, []
    for _ in range(3):
        part = lax.reduce_precision(gates_left, 8, 7)
        gate_parts.append(part.astype(bf16))
        gates_left = gates_left - part
    under = jnp.concatenate([routes.T.astype(bf16), *gate_parts], axis=0)
    under = jnp.pad(under, ((0, 8), (0, 2 * width - rows)))
    both = gather_group(
        jnp.concatenate([jnp.concatenate([tokens, cotangent], axis=1), under], axis=0)
    )

    lengths = image_lengths[0]
    image_total = image_counts[0]
    slots = lengths.shape[0]
    slot_ids = jnp.arange(slots, dtype=jnp.int32)
    starts = jnp.sum(
        jnp.where(slot_ids[None, :] < slot_ids[:, None], lengths[None, :], 0), axis=1
    )
    live = (slot_ids >= 1) & (slot_ids < image_total)
    block_ids = position ^ jnp.arange(group, dtype=jnp.int32)
    segment = jnp.sum(
        (live[None, :] & (starts[None, :] <= (block_ids * rows)[:, None])).astype(jnp.int32),
        axis=1,
    )
    block_hot = segment[:, None] == slot_ids[None, :]

    info = jnp.concatenate(
        [
            order,
            jnp.stack([position, side]),
            segment,
            unit_blocks,
            row_blocks,
            jnp.zeros((6,), jnp.int32),
        ]
    ).astype(jnp.int32)

    cond_value = conditioning[0].astype(f32)
    cond_act = jax.nn.silu(cond_value).astype(bf16)
    act_parts = lax.all_to_all(
        cond_act.reshape(slots, copies, d_rows).transpose(1, 0, 2),
        "dp",
        split_axis=0,
        concat_axis=0,
        tiled=True,
    ).reshape(copies * slots, d_rows)
    mod_width = ada_weight.shape[1]
    mod_own = mod_width // group
    bias_line = lax.dynamic_update_slice(
        jnp.zeros((mod_width,), f32), ada_bias.astype(f32), (place * ada_bias.shape[0],)
    )
    ada_own = lax.dynamic_slice_in_dim(ada_weight, position * mod_own, mod_own, axis=1)
    bias_own = lax.dynamic_slice_in_dim(bias_line, position * mod_own, mod_own)
    mod_parts = (mm("sd,dm->sm", tied(act_parts, *dues[0]), ada_own) + bias_own[None]).reshape(
        copies, slots, mod_own
    )
    mod_got = lax.all_to_all(mod_parts, "dp", split_axis=0, concat_axis=0, tiled=True)
    mod_sum = jnp.sum(tied(mod_got, *dues[1]), axis=0)
    mod_across = tied(swap(mod_sum, 2), *dues[2])
    mod_beside = swap(jnp.stack([mod_sum, mod_across]), 1)
    mod_group = jnp.stack([mod_sum, mod_beside[0], mod_across, mod_beside[1]])
    modulation = in_order(mod_group, position).transpose(1, 0, 2).reshape(slots, mod_width)
    per_block = jnp.sum(
        jnp.where(block_hot[:, :, None], modulation[None, :, :], 0.0), axis=1
    )
    mods = jnp.pad(per_block.reshape(group, 6, width), ((0, 0), (0, 2), (0, 0)))
    shift_a, scale_a, gate_a, shift_b, scale_b, gate_b = (mods[0, i : i + 1] for i in range(6))

    (
        hidden_a,
        projected,
        qkv_own,
        table,
        gates,
        grad_comb_low,
        slot_own,
        sums_f,
        lines_got,
        units_got,
    ) = front(
        info,
        both,
        tied(mods, *dues[3]),
        bias_three,
        first,
        width // 8,
        cols_own,
        keep if copies == 8 else 0,
    )
    if copies == 8:
        bias_lines, rupb_own = lines_got, units_got
    upb_line, projb_line, downb_line, rdownb_line = (bias_lines[i : i + 1] for i in range(4))
    slot_got = pair_swap(slot_own)
    heads_0 = attention(info, tied(projected, *dues[4]), group, cols_own)
    heads_0 = tied(heads_0, *dues[5])
    heads_2 = swap(heads_0, 2)
    heads_1 = swap(heads_0, 1)
    heads_3 = swap(heads_2, 1)
    hidden_b, attended, buffer_own, attn_out, residual_mid, proj_own = middle(
        info,
        both,
        mods,
        (heads_0, heads_1, heads_2, heads_3),
        third,
        projb_line,
        tied(table, slot_got, *dues[6]),
        width // 8,
    )
    buffer_got = pair_swap(buffer_own)

    shared_parts, shared_back, shared_mine, shared_theirs, upbias_line = shared_expert(
        info, tied(hidden_b, *dues[7]), grad_comb_low, upb_line, third, width // 8, group, copies == 8
    )
    if copies != 8:
        sided = jnp.concatenate([by_side(shared_mine[0]), by_side(shared_mine[1])], axis=2)
        shared_mine, shared_theirs = (
            lax.dynamic_index_in_dim(sided, which, 0, keepdims=False) for which in (side, 1 - side)
        )
        shared_theirs = shared_theirs.astype(bf16)
    shared_back_got = pair_swap(shared_theirs)
    (
        back_own,
        back_theirs,
        out_own,
        out_theirs,
        units_sum,
        act_low,
        grad_low,
        both_rows,
        both_slots,
    ) = routed_rows_grads(
        info,
        (tied(buffer_own, shared_theirs), buffer_got),
        (slot_own, slot_got),
        routed_own,
        routed_got,
        rupb_own,
    )
    shared_sums = shared_mine + shared_back_got.astype(f32)
    shared_send = jnp.stack([shared_sums[1], shared_sums[3]]).astype(bf16)
    down_send, down_keep, up_send, up_keep = routed_weight_grads(
        info, tied(act_low, shared_send), grad_low, both_rows, both_slots, 4
    )
    if copies == 8:
        shared_first = dp_swap(shared_send, 1)
        shared_near = shared_sums[0] + shared_first[0].astype(f32)
        shared_far = dp_swap((shared_sums[2] + shared_first[1].astype(f32)).astype(bf16), 4)
        down_first = dp_swap(down_send, 1)
        due_rows = (down_send, shared_first)
        due_back = (down_first, shared_far)
    else:
        due_rows, due_back = (down_send,), ()
    units_sum = units_sum.reshape(pairs_count, f_rows)
    blank = jnp.zeros((pairs_count, f_rows), f32)
    units_one = jnp.where(first_side, units_sum, blank)
    units_two = jnp.where(first_side, blank, units_sum)
    units_by_place = jnp.stack(
        [
            jnp.concatenate([units_one[:, :keep], units_two[:, keep:]], axis=1),
            jnp.concatenate([units_one[:, keep:], units_two[:, :keep]], axis=1),
        ]
    )
    units_by_place = units_by_place.reshape(2, pairs_count // 2, 2, f_rows).transpose(1, 0, 2, 3)
    expert_line = jnp.concatenate(
        [
            units_by_place.reshape(copies, f_rows),
            upbias_line.reshape(copies, f_own),
            sums_f[0].reshape(copies, d_rows),
            sums_f[1].reshape(copies, d_rows),
        ],
        axis=1,
    )
    zero_line = jnp.zeros((1, width), f32)
    rows_send, rows_keep, _ = to_rows(
        tied(back_own, *due_rows),
        pair_swap(back_theirs),
        zero_line,
        table,
        (),
        shared_back,
        both,
        zero_line,
    )
    back_near, back_got = reduce_group(rows_send, rows_keep)
    grad_mid, grad_attn_own, sums_b = middle_back(
        tied(back_near, *due_back), back_got, residual_mid, attn_out, cotangent, mods
    )
    attn_2 = swap(grad_attn_own, 2)
    grad_attn = jnp.concatenate(
        [grad_attn_own, swap(grad_attn_own, 1), attn_2, swap(attn_2, 1)]
    )

    grad_projected = attention_back(info, projected, grad_attn, proj_own, group, cols_own)
    out_got = pair_swap(out_theirs)
    due_tail = (out_got,)
    if copies == 8:
        down_far = dp_swap((down_keep[1] + down_first[1].astype(f32)).astype(bf16), 4)
        up_first = dp_swap(tied(up_send, down_first), 1)
        due_tail = (down_far, up_first)
    away, stay, back_send, back_keep, sums_a, lines = tail_grads(
        info, both, tied(hidden_a, *due_tail), grad_projected, attended, grad_attn, qkv_own
    )

    if copies == 8:
        up_far = dp_swap((up_keep[1] + up_first[1].astype(f32)).astype(bf16), 4)
        shared_rows = shared_near + shared_far.astype(f32)
        rdown_sums = down_keep[0] + down_first[0].astype(f32) + down_far.astype(f32)
        rup_sums = up_keep[0] + up_first[0].astype(f32) + up_far.astype(f32)
        last_first = stay + dp_swap(away, 1).astype(f32)
        last_got = dp_swap(jnp.stack([last_first[1], last_first[3]]).astype(bf16), 2)
        last_second = jnp.stack([last_first[0], last_first[2]]) + last_got.astype(f32)
    else:

        def scatter(value, each):
            return lax.psum_scatter(
                value.reshape(pairs_count, each, -1).astype(bf16),
                "dp",
                scatter_dimension=0,
                axis_index_groups=side_groups(copies),
                tiled=False,
            )

        def whole_of(send, keep):
            send = send.astype(f32)
            return jnp.stack([keep[0], send[0], keep[1], send[1]])

        shared_rows = jnp.concatenate(
            [scatter(shared_sums[:, : width // 8], d_rows), scatter(shared_sums[:, width // 8 :], f_own)]
        )
        rdown_sums = scatter(whole_of(down_send, down_keep), f_rows)
        sided = by_side(whole_of(up_send, up_keep))
        rup_sums = jnp.concatenate(
            [
                scatter(lax.dynamic_index_in_dim(sided, which, 0, keepdims=False), d_rows)
                for which in (side, 1 - side)
            ]
        )
        last_parts = jnp.stack(
            [(away if k // 2 % 2 else stay)[k % 2 + 2 * (k // 4)].astype(bf16) for k in range(8)]
        )
        last_sums = jnp.sum(
            lax.all_to_all(
                last_parts.reshape(copies, d_rows, width),
                "dp",
                split_axis=0,
                concat_axis=0,
                tiled=True,
            ).astype(f32),
            axis=0,
        )

    lines = lines[0]
    qv_line = lax.dynamic_update_slice(
        jnp.zeros((2 * width,), f32), lines[:cols_own], (position * cols_own,)
    )
    qv_line = lax.dynamic_update_slice(
        qv_line, lines[2 * cols_own : 3 * cols_own], (width + position * cols_own,)
    ).reshape(copies, -1)
    pb_line = lines[3 * cols_own :].reshape(copies, d_rows)
    count_own = sums_f[2, 0]
    count_high = jnp.floor(count_own / 128.0)
    count_line = jnp.broadcast_to(
        jnp.stack([count_high, count_own - 128.0 * count_high])[None], (copies, 2)
    )
    line = jnp.concatenate([expert_line, qv_line, pb_line, count_line], axis=1)
    line_width = -(-line.shape[1] // (slots * 128)) * 128
    line = jnp.pad(line, ((0, 0), (0, slots * line_width - line.shape[1]))).reshape(
        copies, slots, line_width
    )

    rows_send, rows_keep, sums_out = to_rows(
        tied(out_own, away),
        out_got,
        rdownb_line,
        table,
        (gates,),
        shared_parts,
        both,
        downb_line,
    )
    combined_near, combined_got = reduce_group(rows_send, rows_keep)
    near_a, got_a = reduce_group(back_send, back_keep)

    block_of = block_hot.astype(f32)
    sums_all = jnp.concatenate(
        [
            sums_a[:group],
            sums_a[group:],
            jnp.pad(sums_b[:3].reshape(1, 3 * width), ((0, group - 1), (0, 0))),
            sums_out.reshape(group, width),
        ],
        axis=1,
    )
    slot_sums = jnp.sum(block_of[:, :, None] * sums_all[:, None, :], axis=0)
    slot_sums = slot_sums + swap(slot_sums, 1)
    slot_sums = slot_sums + swap(slot_sums, 2)
    grad_modulation = slot_sums.astype(bf16)
    mod_got = lax.all_to_all(
        jnp.concatenate(
            [
                jnp.broadcast_to(grad_modulation[None], (copies, slots, mod_width)),
                line.astype(bf16),
            ],
            axis=2,
        ),
        "dp",
        split_axis=0,
        concat_axis=0,
        tiled=True,
    )
    if copies == 8:
        mod_got = tied(mod_got, last_second)
    mod_all = mod_got[:, :, :mod_width].reshape(copies * slots, mod_width)
    line_sums = jnp.sum(mod_got[:, :, mod_width:].astype(f32), axis=0).reshape(-1)
    ada_grad = mm("sd,sm->dm", act_parts, mod_all)
    adabias_grad = jnp.sum(
        lax.dynamic_slice_in_dim(
            mod_all, place * ada_bias.shape[0], ada_bias.shape[0], axis=1
        ).astype(f32),
        axis=0,
    )
    cond_parts = mm("sm,dm->sd", mod_all, ada_weight).reshape(copies, slots, d_rows)
    after = cond_parts
    cond_got = lax.all_to_all(cond_parts, "dp", split_axis=0, concat_axis=0, tiled=True)
    cond_got = tied(cond_got, got_a, combined_got)
    combined = combined_near + combined_got.astype(f32) + downb_line
    output = (residual_mid + gate_b * combined).astype(bf16)
    grad_hidden_a = near_a + got_a.astype(f32)
    normed_a, inv_std_a = norm_parts(tokens.astype(f32))
    tokens_grad = grad_mid + norm_back(grad_hidden_a * (1.0 + scale_a), normed_a, inv_std_a)
    if copies == 8:
        last_third = dp_swap(last_second[1].astype(bf16), 4)
        last_sums = last_second[0] + last_third.astype(f32)
        rup_sums = tied(rup_sums, after)
    if copies == 8:
        cond_got = tied(cond_got, last_third)
    grad_cond_act = (
        cond_got
        .transpose(1, 0, 2)
        .reshape(slots, width)
    )
    sigmoid_cond = jax.nn.sigmoid(cond_value)
    conditioning_grad = (grad_cond_act * sigmoid_cond * (1.0 + cond_value * (1.0 - sigmoid_cond)))[
        None
    ]

    rup_got = pair_swap(rup_sums[d_rows:].astype(bf16))
    rdown_got = pair_swap(rdown_sums[keep:].astype(bf16))
    shared_all = exchange_group(shared_rows.astype(bf16))
    last_all = exchange_group(last_sums.astype(bf16))
    if copies == 8:
        rup_rows, rdown_rows = routed_rows(info, rup_sums, rup_got, rdown_sums, rdown_got, keep)
        up_rows, down_rows, qkv_rows, proj_rows = group_rows_out(
            info, shared_all, last_all, d_rows, f_rows
        )
    else:
        rup_rows = from_units(rup_sums[:d_rows].astype(f32), rup_got.astype(f32))
        kept, back = rdown_sums[:keep].astype(f32), rdown_got.astype(f32)
        rdown_rows = jnp.where(
            first_side, jnp.concatenate([kept, back]), jnp.concatenate([back, kept])
        )
        shared_all, last_all = (
            in_order(jnp.stack([v[0], v[2][0], v[1], v[2][1]]), position).astype(f32)
            for v in (shared_all, last_all)
        )
        up_rows = (
            shared_all[:, :d_rows]
            .reshape(group, d_rows, copies, f_own)
            .transpose(1, 2, 0, 3)
            .reshape(d_rows, hidden_units)
        )
        down_rows = shared_all[:, d_rows:].reshape(f_rows, width)
        qkv_rows = (
            last_all[:, :, : 3 * cols_own]
            .reshape(group, d_rows, 3, cols_own)
            .transpose(1, 2, 0, 3)
            .reshape(d_rows, 3 * width)
        )
        proj_rows = last_all[:, :, 3 * cols_own :].transpose(1, 0, 2).reshape(d_rows, width)
    cuts = [f_rows, f_own, d_rows, d_rows, 2 * width // copies, d_rows, 2]
    at = [sum(cuts[:i]) for i in range(len(cuts))]
    rupbias_row, upbias_sum, rdownbias_row, downbias_row, qvbias_sum, projbias_row, counts = (
        line_sums[o : o + n] for o, n in zip(at, cuts)
    )
    small = in_order(
        gather_group(jnp.concatenate([upbias_sum, qvbias_sum, counts])[None]), position
    )[:, 0]
    upbias_rows = small[:, :f_own].reshape(f_rows)
    qvbias_rows = jnp.sum(small[:, f_own:-2], axis=0)
    expert_counts = (128.0 * small[:, -2] + small[:, -1]).astype(jnp.int32)

    return (
        output,
        tokens_grad,
        conditioning_grad,
        qkv_rows,
        qvbias_rows,
        proj_rows,
        projbias_row,
        ada_grad,
        adabias_grad,
        up_rows,
        upbias_rows,
        down_rows,
        downbias_row,
        rup_rows[None],
        rupbias_row[None],
        rdown_rows[None],
        rdownbias_row[None],
        expert_counts,
    )


def solution(mesh):
    in_specs = (
        P(("dp", "expert"), None),
        P("dp", None, None),
        P(("dp", "expert"), None),
        P(("dp", "expert"), None),
        P("dp"),
        P("dp", None),
        P(("dp", "expert"), None),
        P("dp", None),
        P("dp"),
        P("dp", None),
        P("dp"),
        P("dp", None),
        P("dp"),
        P("dp", None),
        P("dp"),
        P("dp", None),
        P("dp"),
        P("expert", "dp", None),
        P("expert", "dp"),
        P("expert", "dp", None),
        P("expert", "dp"),
    )
    out_specs = (
        P(("dp", "expert"), None),
        P(("dp", "expert"), None),
        P("dp", None, None),
        P("dp", None),
        P("dp"),
        P("dp", None),
        P("dp"),
        P("dp", None),
        P("dp"),
        P("dp", None),
        P("dp"),
        P("dp", None),
        P("dp"),
        P("expert", "dp", None),
        P("expert", "dp"),
        P("expert", "dp", None),
        P("expert", "dp"),
        P(),
    )
    return jax.shard_map(body, mesh=mesh, in_specs=in_specs, out_specs=out_specs, check_vma=False)
```
